32 devices in a mesh: group: 2 (over y), tile: 16 (over z, x, core).
Axes of the slice: x: 2, y: 2, z: 4, core: 2. Of those that a mesh axis runs over, the one named last changes fastest.
Arguments:
- site_tensors: bfloat16 [16, 6, 2, 65536], P('tile', 'group'), may hold values from -6 to 6
- msg_in: float32 [16, 6, 4, 256], P('tile', 'group'), may hold values from -6 to 6
Outputs:
- new_tensors: bfloat16 [16, 6, 2, 65536], P('tile', 'group')
- messages: float32 [16, 6, 4, 256], P('tile', 'group')
The draws below stay inside these ranges and needn't reach their ends.
All inputs are finite; a program needn't handle non-finite values.
Results may differ from the reference program's by a relative error of at most 0.029.
The reference program's roundings to bfloat16 on the way count: a program that leaves them out, or rounds other values in their place, can miss the bound.
Values may be sent and summed in bfloat16 or wider, within the bound.
A program may use at most 256 MiB of HBM per device.

```python
import math
import jax
import jax.numpy as jnp
from jax import lax

D = 16
ITERS = 2
NS_STEPS = 6
COLS = 6
ROWS = 16


def steps_of(own_key, extent, split, low, largest):
    def one(position, parts):
        draws = jax.random.uniform(jax.random.fold_in(jax.random.fold_in(own_key, 6), position), (parts,), jnp.float32, low / len(split), largest / len(split))
        return jnp.repeat(jnp.exp(draws), extent[position] // parts).reshape((-1,) + (1,) * (len(extent) - position - 1))

    factor_of = one(*split[0])
    for cut in split[1:]:
        factor_of = factor_of * one(*cut)
    return factor_of


def centred(key, extent, deviation, bound, cuts=(), kind=jnp.bfloat16):
    array = jax.random.normal(key, extent, jnp.float32) * deviation
    if len(cuts) > 0:
        array = steps_of(key, extent, cuts, -0.22, 0.18) * array
    return jnp.clip(array, min=-bound, max=bound).astype(kind)


def setup_inputs(seed: int = 0) -> dict:
    keys = jax.random.split(jax.random.key(seed), 3)
    site_tensors = centred(keys[0], (ROWS, COLS, 2, D**4), 1.0, 6.0, ((0, 16), (1, 2)))
    msg_in = centred(keys[1], (ROWS, COLS, 4, D*D), 1.0, 6.0, ((0, 16), (1, 2)), jnp.float32)
    return dict(site_tensors=site_tensors, msg_in=msg_in)


epsilon = 1e-06
coupling_step = 0.5
field_step = 0.3
precise = lax.Precision.HIGHEST
apply_forms = ('nsuldr,nua->nsaldr', 'nsuldr,nla->nsuadr', 'nsuldr,nda->nsular', 'nsuldr,nra->nsulda')
gate_forms = ('nsuldr,nsua->nsaldr', 'nsuldr,nsla->nsuadr', 'nsuldr,nsda->nsular', 'nsuldr,nsra->nsulda')
pair_forms = ('nsuldr,nsvldr->nsuv', 'nsuldr,nsuvdr->nslv', 'nsuldr,nsulvr->nsdv', 'nsuldr,nsuldv->nsrv')

def contract(form, left_op, right_op):
    return jnp.einsum(form, left_op.astype(jnp.float32), right_op.astype(jnp.float32), precision=precise)

def outgoing(tensors, incoming):
    site_count = tensors.shape[0]
    site_block = tensors.reshape(site_count, 2, D, D, D, D)
    msg_bf = incoming.reshape(site_count, 4, D, D).astype(jnp.bfloat16)

    def apply_leg(tensor, leg_idx):
        return contract(apply_forms[leg_idx], tensor, msg_bf[:, leg_idx]).astype(jnp.bfloat16)
    upper_left = apply_leg(apply_leg(site_block, 0), 1)
    lower_right = apply_leg(apply_leg(site_block, 2), 3)
    kept = (apply_leg(lower_right, 1), apply_leg(lower_right, 0), apply_leg(upper_left, 3), apply_leg(upper_left, 2))
    pairs = jnp.stack([contract(pair_forms[leg_idx], kept[leg_idx], site_block) for leg_idx in range(4)], axis=1)
    summed = pairs[:, :, 0] + pairs[:, :, 1]
    scale = jnp.sqrt(lax.optimization_barrier(jnp.mean(summed * summed, axis=(2, 3), keepdims=True)) + epsilon)
    twisted = (pairs[:, :, 0] - pairs[:, :, 1]) / scale
    return ((summed / scale).reshape(site_count, 4, D * D), twisted.reshape(site_count, 4, D * D))

def route(values, edge_msgs):
    in_up = jnp.concatenate([edge_msgs[:1, :, 0], values[:-1, :, 2]], axis=0)
    in_down = jnp.concatenate([values[1:, :, 0], edge_msgs[-1:, :, 2]], axis=0)
    in_left = jnp.concatenate([edge_msgs[:, :1, 1], values[:, :-1, 3]], axis=1)
    in_right = jnp.concatenate([values[:, 1:, 1], edge_msgs[:, -1:, 3]], axis=1)
    return jnp.stack([in_up, in_left, in_down, in_right], axis=2)

def leg_weights(msg_sum, twist_sum):
    weight_zero = math.cosh(coupling_step)
    weight_one = math.sinh(coupling_step)
    cross_weight = math.sqrt(weight_zero * weight_one)
    y_top = ((weight_zero * msg_sum + cross_weight * twist_sum) / math.sqrt(2.0)).astype(jnp.bfloat16).astype(jnp.float32)
    bottom = ((cross_weight * twist_sum + weight_one * msg_sum) / math.sqrt(2.0)).astype(jnp.bfloat16).astype(jnp.float32)
    gram_mat = jnp.einsum('...ab,...ac->...bc', y_top, y_top, precision=precise) + jnp.einsum('...ab,...ac->...bc', bottom, bottom, precision=precise)
    identity = jnp.eye(D, dtype=jnp.float32)
    trace_sum = lax.optimization_barrier(jnp.sum(gram_mat * identity, axis=(-2, -1), keepdims=True)) + epsilon
    current = gram_mat / trace_sum
    inverse = jnp.broadcast_to(identity, gram_mat.shape)
    for sweep in range(NS_STEPS):
        factor = 1.5 * identity - 0.5 * jnp.matmul(inverse, current, precision=precise)
        current, inverse = (jnp.matmul(current, factor, precision=precise), jnp.matmul(factor, inverse, precision=precise))
    inverse = inverse.astype(jnp.bfloat16).astype(jnp.float32)
    root_trace = jnp.sqrt(trace_sum)
    q_top = jnp.matmul(y_top, inverse, precision=precise) / root_trace
    q_bottom = jnp.matmul(bottom, inverse, precision=precise) / root_trace
    first = math.sqrt(weight_zero) * q_top
    second = math.sqrt(weight_one) * q_bottom
    return jnp.stack([first + second, first - second], axis=-3)

def update_row(tensors, weights):
    site_count = tensors.shape[0]
    site_block = tensors.reshape(site_count, 2, D, D, D, D).astype(jnp.float32)
    gated = (math.cosh(field_step) * site_block + math.sinh(field_step) * site_block[:, ::-1]).astype(jnp.bfloat16)
    for leg_idx in range(4):
        gated = contract(gate_forms[leg_idx], gated, weights[:, leg_idx]).astype(jnp.bfloat16)
    return gated.reshape(site_count, 2, D ** 4)

def reference(site_tensors, msg_in):
    incoming = msg_in
    for sweep in range(ITERS):
        summed, twisted = lax.map(lambda row_data: outgoing(row_data[0], row_data[1]), (site_tensors, incoming))
        incoming = route(summed, msg_in)
    twisted_in = route(twisted, jnp.zeros_like(msg_in))
    shape_env = (ROWS, COLS, 4, D, D)
    weights = leg_weights((summed + incoming).reshape(shape_env), (twisted + twisted_in).reshape(shape_env))
    row_ids = jnp.arange(ROWS)[:, None, None]
    col_ids = jnp.arange(COLS)[None, :, None]
    leg_ids = jnp.arange(4)[None, None, :]
    at_edge = (leg_ids == 0) & (row_ids == 0) | (leg_ids == 2) & (row_ids == ROWS - 1) | (leg_ids == 1) & (col_ids == 0) | (leg_ids == 3) & (col_ids == COLS - 1)
    identity = jnp.eye(D, dtype=jnp.float32)
    weights = jnp.where(at_edge[:, :, :, None, None, None], identity, weights).astype(jnp.bfloat16)
    new_tensors = lax.map(lambda row_data: update_row(row_data[0], row_data[1]), (site_tensors, weights))
    return (new_tensors, incoming)
```

```python
import functools
import math

import jax
import jax.numpy as jnp
from jax import lax
from jax.experimental import pallas as pl
from jax.experimental.pallas import tpu as pltpu
from jax.sharding import PartitionSpec as P

ITERS = 2
NS_STEPS = 6
LANES = 128
EPSILON = 1e-06
COUPLING = 0.5
FIELD = 0.3
F32 = jnp.float32
BF16 = jnp.bfloat16
MESH = pl.DeviceIdType.MESH


def iota(shape, axis):
    return lax.broadcasted_iota(jnp.int32, shape, axis)


def dot(a, b):
    return jnp.dot(a, b, preferred_element_type=F32)


def dot_nt(a, b):
    return lax.dot_general(a, b, (((1,), (1,)), ((), ())), preferred_element_type=F32)


def dot_tn(a, b):
    return lax.dot_general(a, b, (((0,), (0,)), ((), ())), preferred_element_type=F32)


def parts(value, count):
    out = []
    for _ in range(count):
        piece = value.astype(BF16)
        out.append(piece)
        value = value - piece.astype(F32)
    return out


def select_dot(value, selector, count):
    total = None
    for piece in parts(value, count):
        term = dot(piece, selector)
        total = term if total is None else total + term
    return total


def one_hot(mask):
    return jnp.where(mask, 1.0, 0.0).astype(BF16)


def build_kron(kron_ref, slot, first, second):
    D = first.shape[0]
    for d in range(D):
        kron_ref[slot, d * D : (d + 1) * D, :] = (first[d : d + 1, :] * second).astype(BF16)


def permutation(DD, rows, mixed, out_axis):
    p, k = iota((DD, DD), out_axis), iota((DD, DD), 1 - out_axis)
    row_bits = rows.bit_length() - 1
    return one_hot(k == (p & (rows - 1)) * mixed + (p >> row_bits))


def messages_kernel(tiles, groups, cols, D, a_hbm, msg_hbm, ax_ref, env_ref, mout_ref,
           a_ref, msg_ref, x_ref, xt_ref, kron_ref, gram_ref,
           send_up, send_down, send_side, recv_up, recv_down, recv_side,
           send_sem, recv_sem, load_sem):
    loads = [pltpu.make_async_copy(msg_hbm, msg_ref, load_sem.at[cols])]
    loads += [
        pltpu.make_async_copy(a_hbm.at[i], a_ref.at[i], load_sem.at[i]) for i in range(cols)
    ]
    for load in loads:
        load.start()
    tile = lax.axis_index("tile")
    group = lax.axis_index("group")
    DD = D * D
    shift = D.bit_length() - 1
    halves = DD // LANES
    mixed = 2 * halves
    rows = DD // mixed
    legs = 4 * cols
    wide = legs * D
    has_up = tile > 0
    has_down = tile < tiles - 1

    barrier = pltpu.get_barrier_semaphore()

    @pl.when(has_up)
    def _():
        pl.semaphore_signal(barrier, inc=1, device_id={"tile": tile - 1}, device_id_type=MESH)

    @pl.when(has_down)
    def _():
        pl.semaphore_signal(barrier, inc=1, device_id={"tile": tile + 1}, device_id_type=MESH)

    pl.semaphore_signal(barrier, inc=1, device_id={"group": 1 - group}, device_id_type=MESH)

    lane = iota((D, DD), 1)
    row = iota((D, DD), 0)
    major = one_hot((lane >> shift) == row)
    minor = one_hot((lane & (D - 1)) == row)
    both = jnp.concatenate([major, minor], axis=1)
    major_t = one_hot((iota((DD, D), 0) >> shift) == iota((DD, D), 1))
    minor_t = one_hot((iota((DD, D), 0) & (D - 1)) == iota((DD, D), 1))

    unfold_mask = (lane >> shift) == row
    loads[0].wait()
    flat = msg_ref[...].reshape(legs, DD)
    spread = jnp.concatenate(
        [jnp.where(unfold_mask, flat[m : m + 1, :], 0.0) for m in range(legs)], axis=0
    )
    edge_all = select_dot(spread, minor_t, 3)
    edge = [edge_all[m * D : (m + 1) * D] for m in range(legs)]

    gather = permutation(DD, rows, mixed, 0)

    def unmix(i):
        for b in range(0, mixed, 2):
            pair = jnp.concatenate(
                [a_ref[i, b * DD : (b + 1) * DD, :], a_ref[i, (b + 1) * DD : (b + 2) * DD, :]],
                axis=1,
            )
            block = dot(gather, pair).astype(BF16)
            for c in range(2):
                for g in range(mixed):
                    x_ref[
                        i,
                        g % 2,
                        (b + c) * rows : (b + c + 1) * rows,
                        (g // 2) * LANES : (g // 2 + 1) * LANES,
                    ] = block[g * rows : (g + 1) * rows, c * LANES : (c + 1) * LANES]
        for s in range(2):
            xt_ref[i, s] = x_ref[i, s].T

    def reduce_major(gram, weight):
        total = gram[:D] * weight[0:1, :]
        for d in range(1, D):
            total = total + gram[d * D : (d + 1) * D] * weight[d : d + 1, :]
        return total

    def reduce_minor(gram, weight):
        return jnp.concatenate(
            [
                jnp.sum(gram[d * D : (d + 1) * D] * weight, axis=0, keepdims=True)
                for d in range(D)
            ],
            axis=0,
        )

    def kinds_of(totals):
        if len(totals) == 1:
            return totals
        return [totals[0] + totals[1], totals[0] - totals[1]]

    def outgoing(turn, incoming, last):
        stacked = jnp.concatenate([v.astype(BF16) for v in incoming], axis=0)
        spread = dot(stacked, both)
        kinds = 2 if last else 1

        def by_major(m):
            return spread[m * D : (m + 1) * D, :DD]

        def by_minor(m):
            return spread[m * D : (m + 1) * D, DD:]

        def normalised(totals, selector, slots):
            blocks = []
            for kind in range(kinds):
                rows_of = jnp.concatenate([t[kind] for t in totals], axis=0)
                blocks.append(select_dot(rows_of, selector, 2))
            out = {}
            for n, slot in enumerate(slots):
                own = [b[n * D : (n + 1) * D] for b in blocks]
                power = jnp.sum(own[0] * own[0], axis=(0, 1), keepdims=True) / DD
                scale = jnp.sqrt(power + EPSILON)
                out[slot] = [v / scale for v in own]
            return out

        firsts = []
        for i in range(cols):
            if turn == 0:
                loads[1 + i].wait()
                unmix(i)
            for path in range(2):
                left, right = (x_ref, xt_ref) if path == 0 else (xt_ref, x_ref)
                far = i * 4 + 2 * (1 - path)
                near = i * 4 + 2 * path
                slot = i * 2 + path
                build_kron(kron_ref, slot, by_major(far), by_minor(far + 1))
                y = [dot(left[i, s], kron_ref[slot]).astype(BF16) for s in range(2)]
                if last:
                    grams = [dot(y[s], right[i, s]) for s in range(2)]
                else:
                    grams = [dot(y[0], right[i, 0]) + dot(y[1], right[i, 1])]
                for k, gram in enumerate(grams):
                    gram_ref[slot, k] = gram
                firsts.append(kinds_of([reduce_minor(g, by_minor(near + 1)) for g in grams]))

        def seconds(slots):
            totals = []
            for slot in slots:
                weight = by_major((slot // 2) * 4 + 2 * (slot % 2))
                totals.append(
                    kinds_of([reduce_major(gram_ref[slot, k], weight) for k in range(kinds)])
                )
            return normalised(totals, minor_t, slots)

        vertical = normalised(firsts, major_t, list(range(2 * cols)))
        ends = [0, 2 * cols - 1]
        sides = seconds(ends)

        def rest():
            others = [slot for slot in range(2 * cols) if slot not in ends]
            if others:
                sides.update(seconds(others))
            values = []
            for kind in range(kinds):
                blocks = []
                for slot in range(2 * cols):
                    blocks += [vertical[slot][kind], sides[slot][kind]]
                values.append(blocks)
            return values

        return vertical, sides, rest

    def exchange(turn, vertical, sides, kinds):
        width = kinds * cols * D

        def packed(path):
            return jnp.concatenate(
                [vertical[2 * i + path][k] for k in range(kinds) for i in range(cols)], axis=1
            )

        up_src = send_up.at[turn]
        down_src = send_down.at[turn]
        side_src = send_side.at[turn]
        send_up[turn, :, :width] = packed(0)
        send_down[turn, :, :width] = packed(1)
        side_right = jnp.concatenate(sides[2 * cols - 1], axis=1)
        side_left = jnp.concatenate(sides[0], axis=1)
        send_side[turn, :, : kinds * D] = jnp.where(group == 0, side_right, side_left)

        def copy(src, dst, k, device):
            return pltpu.make_async_remote_copy(
                src_ref=src, dst_ref=dst.at[turn], send_sem=send_sem.at[turn, k],
                recv_sem=recv_sem.at[turn, k], device_id=device, device_id_type=MESH,
            )

        to_up = copy(up_src, recv_down, 0, {"tile": tile - 1})
        to_down = copy(down_src, recv_up, 1, {"tile": tile + 1})
        to_side = copy(side_src, recv_side, 2, {"group": 1 - group})

        @pl.when(has_up)
        def _():
            to_up.start()

        @pl.when(has_down)
        def _():
            to_down.start()

        to_side.start()
        return to_up, to_down, to_side

    def finish(turn, copies, values):
        to_up, to_down, to_side = copies
        kinds = len(values)
        width = kinds * cols * D

        def border(leg):
            blocks = [edge[i * 4 + leg] for i in range(cols)]
            if kinds == 2:
                blocks += [jnp.zeros((D, D), F32)] * cols
            return jnp.concatenate(blocks, axis=1)

        @pl.when(has_up)
        def _():
            to_up.wait_send()
            to_down.wait_recv()

        @pl.when(jnp.logical_not(has_up))
        def _():
            recv_up[turn, :, :width] = border(0)

        @pl.when(has_down)
        def _():
            to_down.wait_send()
            to_up.wait_recv()

        @pl.when(jnp.logical_not(has_down))
        def _():
            recv_down[turn, :, :width] = border(2)

        to_side.wait()
        from_up, from_down, from_side = recv_up[turn], recv_down[turn], recv_side[turn]
        routed = []
        for kind in range(kinds):
            blocks = []
            for i in range(cols):
                at = (kind * cols + i) * D
                side = from_side[:, kind * D : (kind + 1) * D]
                zero = jnp.zeros((D, D), F32)
                out_left = edge[i * 4 + 1] if kind == 0 else zero
                out_right = edge[i * 4 + 3] if kind == 0 else zero
                blocks.append(from_up[:, at : at + D])
                if i > 0:
                    blocks.append(values[kind][(i - 1) * 4 + 3])
                else:
                    blocks.append(jnp.where(group == 0, out_left, side))
                blocks.append(from_down[:, at : at + D])
                if i < cols - 1:
                    blocks.append(values[kind][(i + 1) * 4 + 1])
                else:
                    blocks.append(jnp.where(group == groups - 1, out_right, side))
            routed.append(blocks)
        return routed

    incoming = edge
    for turn in range(ITERS):
        last = turn == ITERS - 1
        vertical, sides, rest = outgoing(turn, incoming, last)
        if turn == 0:
            inside = jnp.logical_and(has_up, has_down)

            @pl.when(inside)
            def _():
                pl.semaphore_wait(barrier, 3)

            @pl.when(jnp.logical_not(inside))
            def _():
                pl.semaphore_wait(barrier, 2)

        copies = exchange(turn, vertical, sides, 2 if last else 1)
        values = rest()
        if turn == 0:
            for i in range(cols):
                a0, a1 = x_ref[i, 0].astype(F32), x_ref[i, 1].astype(F32)
                ch, sh = math.cosh(FIELD), math.sinh(FIELD)
                ax_ref[i, 0] = (ch * a0 + sh * a1).astype(BF16)
                ax_ref[i, 1] = (ch * a1 + sh * a0).astype(BF16)
        routed = finish(turn, copies, values)
        incoming = routed[0]

    mout_ref[...] = jnp.concatenate(incoming, axis=0)
    env_ref[0] = jnp.concatenate([o + n for o, n in zip(values[0], routed[0])], axis=1)
    env_ref[1] = jnp.concatenate([o + n for o, n in zip(values[1], routed[1])], axis=1)
    lane_w = iota((D, wide), 1)
    leg_of = (lane_w >> shift) & 3
    col_of = (lane_w >> (shift + 2)) + group * cols
    at_edge = (
        ((leg_of == 0) & (tile == 0))
        | ((leg_of == 2) & (tile == tiles - 1))
        | ((leg_of == 1) & (col_of == 0))
        | ((leg_of == 3) & (col_of == groups * cols - 1))
    )
    env_ref[2] = jnp.where(at_edge, 1.0, 0.0).astype(F32)


def gates_kernel(cols, D, ax_ref, env_ref, in_ref, out_hbm, mout_hbm,
                 kron_ref, out_ref, mout_ref, store_sem):
    DD = D * D
    shift = D.bit_length() - 1
    mixed = 2 * (DD // LANES)
    rows = DD // mixed
    legs = 4 * cols
    wide = legs * D
    lane = iota((D, DD), 1)
    row = iota((D, DD), 0)
    major = one_hot((lane >> shift) == row)
    minor = one_hot((lane & (D - 1)) == row)
    both = jnp.concatenate([major, minor], axis=1)

    spread = select_dot(in_ref[...], minor, 3)
    unfold_mask = (lane >> shift) == row
    flat_rows = [
        jnp.sum(
            jnp.where(unfold_mask, spread[m * D : (m + 1) * D], 0.0), axis=0, keepdims=True
        )
        for m in range(legs)
    ]
    mout_ref[...] = jnp.concatenate(flat_rows, axis=0).reshape(cols, 4, DD)
    store_msg = pltpu.make_async_copy(mout_ref, mout_hbm, store_sem.at[cols])
    store_msg.start()

    g0, g1 = math.cosh(COUPLING), math.sinh(COUPLING)
    cross = math.sqrt(g0 * g1)
    root2 = math.sqrt(2.0)
    msg_sum, twist_sum = env_ref[0], env_ref[1]
    y_top = ((g0 * msg_sum + cross * twist_sum) / root2).astype(BF16)
    y_bot = ((cross * twist_sum + g1 * msg_sum) / root2).astype(BF16)
    y_both = jnp.concatenate([y_top, y_bot], axis=0)
    same = (iota((wide, wide), 0) >> shift) == (iota((wide, wide), 1) >> shift)
    same_bf = one_hot(same)
    lane_w = iota((D, wide), 1)
    unit = jnp.where((lane_w & (D - 1)) == iota((D, wide), 0), 1.0, 0.0).astype(F32)

    def diagonal(value):
        return jnp.concatenate([value] * legs, axis=0) * same_bf

    def times(left, right):
        count = left.shape[0]
        (l_hi, l_lo), (r_hi, r_lo) = parts(left, 2), parts(right, 2)
        main = dot(jnp.concatenate([l_hi, l_lo], axis=0), diagonal(r_hi))
        return main[:count] + (main[count:] + dot(l_hi, diagonal(r_lo)))

    full = jnp.where(same, dot_tn(y_both, y_both), 0.0)
    gram = full[:D]
    for m in range(1, legs):
        gram = gram + full[m * D : (m + 1) * D]
    diag = jnp.sum(gram * unit, axis=0, keepdims=True)
    trace = select_dot(jnp.broadcast_to(diag, (8, wide)), same_bf, 3)[0:1] + EPSILON
    current = gram / trace
    factor = 1.5 * unit - 0.5 * current
    inverse = factor
    current = times(current, factor)
    for step in range(1, NS_STEPS):
        factor = 1.5 * unit - 0.5 * times(inverse, current)
        if step < NS_STEPS - 1:
            stepped = times(jnp.concatenate([inverse, current], axis=0), factor)
            inverse, current = stepped[:D], stepped[D:]
        else:
            inverse = times(inverse, factor)
    q_both = dot(y_both, diagonal(inverse.astype(BF16))) / jnp.sqrt(trace)
    first = math.sqrt(g0) * q_both[:D]
    second = math.sqrt(g1) * q_both[D:]
    at_edge = env_ref[2] > 0.5
    scatter = permutation(DD, rows, mixed, 1)
    spreads = []
    for weight in (first + second, first - second):
        weight = jnp.where(at_edge, unit, weight)
        spreads.append(dot(weight.T.astype(BF16), both))
    stores = [
        pltpu.make_async_copy(out_ref.at[i], out_hbm.at[i], store_sem.at[i]) for i in range(cols)
    ]
    def gate(i):
        m = i * 4
        gated = []
        for s in range(2):
            w = spreads[s]
            slot = (i * 2 + s) * 2
            build_kron(
                kron_ref, slot, w[(m + 2) * D : (m + 3) * D, :DD], w[(m + 3) * D : (m + 4) * D, DD:]
            )
            build_kron(
                kron_ref, slot + 1, w[m * D : (m + 1) * D, :DD], w[(m + 1) * D : (m + 2) * D, DD:]
            )
            half = dot_nt(ax_ref[i, s], kron_ref[slot]).astype(BF16)
            gated.append(dot(kron_ref[slot + 1], half).astype(BF16))
        return gated

    def emit(i, gated):
        for b in range(0, mixed, 2):
            block = jnp.concatenate(
                [
                    jnp.concatenate(
                        [
                            gated[g % 2][
                                (b + c) * rows : (b + c + 1) * rows,
                                (g // 2) * LANES : (g // 2 + 1) * LANES,
                            ]
                            for c in range(2)
                        ],
                        axis=1,
                    )
                    for g in range(mixed)
                ],
                axis=0,
            )
            done = dot(scatter, block).astype(BF16)
            for c in range(2):
                out_ref[i, (b + c) * DD : (b + c + 1) * DD, :] = done[
                    :, c * LANES : (c + 1) * LANES
                ]
        stores[i].start()

    waiting = gate(0)
    for i in range(cols):
        following = gate(i + 1) if i + 1 < cols else None
        emit(i, waiting)
        waiting = following
    for store in stores + [store_msg]:
        store.wait()


def per_device(tiles, groups, site_tensors, msg_in):
    _, cols, _, size = site_tensors.shape
    DD = msg_in.shape[-1]
    D = math.isqrt(DD)
    chunks = size // LANES
    a = site_tensors.reshape(cols, 2, chunks, LANES).transpose(0, 2, 1, 3)
    a = a.reshape(cols, 2 * chunks, LANES)
    wide = 2 * cols * D
    legs = 4 * cols
    vmem = pl.BlockSpec(memory_space=pltpu.VMEM)
    hbm = pl.BlockSpec(memory_space=pltpu.HBM)
    gated, env, stacked = pl.pallas_call(
        functools.partial(messages_kernel, tiles, groups, cols, D),
        out_shape=(
            jax.ShapeDtypeStruct((cols, 2, DD, DD), BF16),
            jax.ShapeDtypeStruct((3, D, legs * D), F32),
            jax.ShapeDtypeStruct((legs * D, D), F32),
        ),
        in_specs=[hbm, hbm],
        out_specs=(vmem, vmem, vmem),
        scratch_shapes=[
            pltpu.VMEM(a.shape, BF16),
            pltpu.VMEM((cols, 4, DD), F32),
            pltpu.VMEM((cols, 2, DD, DD), BF16),
            pltpu.VMEM((cols, 2, DD, DD), BF16),
            pltpu.VMEM((2 * cols, DD, DD), BF16),
            pltpu.VMEM((2 * cols, 2, DD, DD), F32),
            pltpu.VMEM((ITERS, D, wide), F32),
            pltpu.VMEM((ITERS, D, wide), F32),
            pltpu.VMEM((ITERS, D, 2 * D), F32),
            pltpu.VMEM((ITERS, D, wide), F32),
            pltpu.VMEM((ITERS, D, wide), F32),
            pltpu.VMEM((ITERS, D, 2 * D), F32),
            pltpu.SemaphoreType.DMA((ITERS, 3)),
            pltpu.SemaphoreType.DMA((ITERS, 3)),
            pltpu.SemaphoreType.DMA((cols + 1,)),
        ],
        compiler_params=pltpu.CompilerParams(
            collective_id=0, has_side_effects=True, vmem_limit_bytes=24 * 2**20
        ),
    )(a, msg_in[0])
    out, messages = pl.pallas_call(
        functools.partial(gates_kernel, cols, D),
        out_shape=(
            jax.ShapeDtypeStruct(a.shape, BF16),
            jax.ShapeDtypeStruct((cols, 4, DD), F32),
        ),
        in_specs=[vmem, vmem, vmem],
        out_specs=(hbm, hbm),
        scratch_shapes=[
            pltpu.VMEM((4 * cols, DD, DD), BF16),
            pltpu.VMEM(a.shape, BF16),
            pltpu.VMEM((cols, 4, DD), F32),
            pltpu.SemaphoreType.DMA((cols + 1,)),
        ],
        compiler_params=pltpu.CompilerParams(vmem_limit_bytes=24 * 2**20),
    )(gated, env, stacked)
    out = out.reshape(cols, chunks, 2, LANES).transpose(0, 2, 1, 3)
    return out.reshape(1, cols, 2, size), messages[None]


def solution(mesh):
    spec = P("tile", "group", None, None)
    return jax.shard_map(
        functools.partial(per_device, mesh.shape["tile"], mesh.shape["group"]),
        mesh=mesh, in_specs=(spec, spec), out_specs=(spec, spec), check_vma=False,
    )
```

```python
import functools
import math

import jax
import jax.numpy as jnp
from jax import lax
from jax.experimental import pallas as pl
from jax.experimental.pallas import tpu as pltpu
from jax.sharding import PartitionSpec as P

ITERS = 2
NS_STEPS = 6
LANES = 128
EPSILON = 1e-06
COUPLING = 0.5
FIELD = 0.3
F32 = jnp.float32
BF16 = jnp.bfloat16
MESH = pl.DeviceIdType.MESH


def iota(shape, axis):
    return lax.broadcasted_iota(jnp.int32, shape, axis)


def dot(a, b):
    return jnp.dot(a, b, preferred_element_type=F32)


def dot_nt(a, b):
    return lax.dot_general(a, b, (((1,), (1,)), ((), ())), preferred_element_type=F32)


def dot_tn(a, b):
    return lax.dot_general(a, b, (((0,), (0,)), ((), ())), preferred_element_type=F32)


def parts(value, count):
    out = []
    for _ in range(count):
        piece = value.astype(BF16)
        out.append(piece)
        value = value - piece.astype(F32)
    return out


def select_dot(value, selector, count):
    total = None
    for piece in parts(value, count):
        term = dot(piece, selector)
        total = term if total is None else total + term
    return total


def one_hot(mask):
    return jnp.where(mask, 1.0, 0.0).astype(BF16)


def build_kron(kron_ref, slot, first, second):
    D = first.shape[0]
    for d in range(D):
        kron_ref[slot, d * D : (d + 1) * D, :] = (first[d : d + 1, :] * second).astype(BF16)


def permutation(DD, rows, mixed, out_axis):
    p, k = iota((DD, DD), out_axis), iota((DD, DD), 1 - out_axis)
    row_bits = rows.bit_length() - 1
    return one_hot(k == (p & (rows - 1)) * mixed + (p >> row_bits))


def messages_kernel(tiles, groups, cols, D, a_hbm, msg_hbm, ax_ref, env_ref, mout_ref,
           a_ref, msg_ref, x_ref, xt_ref, kron_ref, gram_ref,
           send_up, send_down, send_side, recv_up, recv_down, recv_side,
           send_sem, recv_sem, load_sem):
    loads = [pltpu.make_async_copy(msg_hbm, msg_ref, load_sem.at[cols])]
    loads += [
        pltpu.make_async_copy(a_hbm.at[i], a_ref.at[i], load_sem.at[i]) for i in range(cols)
    ]
    for load in loads:
        load.start()
    tile = lax.axis_index("tile")
    group = lax.axis_index("group")
    DD = D * D
    shift = D.bit_length() - 1
    halves = DD // LANES
    mixed = 2 * halves
    rows = DD // mixed
    legs = 4 * cols
    wide = legs * D
    has_up = tile > 0
    has_down = tile < tiles - 1

    barrier = pltpu.get_barrier_semaphore()

    @pl.when(has_up)
    def _():
        pl.semaphore_signal(barrier, inc=1, device_id={"tile": tile - 1}, device_id_type=MESH)

    @pl.when(has_down)
    def _():
        pl.semaphore_signal(barrier, inc=1, device_id={"tile": tile + 1}, device_id_type=MESH)

    pl.semaphore_signal(barrier, inc=1, device_id={"group": 1 - group}, device_id_type=MESH)

    lane = iota((D, DD), 1)
    row = iota((D, DD), 0)
    major = one_hot((lane >> shift) == row)
    minor = one_hot((lane & (D - 1)) == row)
    both = jnp.concatenate([major, minor], axis=1)
    major_t = one_hot((iota((DD, D), 0) >> shift) == iota((DD, D), 1))
    minor_t = one_hot((iota((DD, D), 0) & (D - 1)) == iota((DD, D), 1))

    unfold_mask = (lane >> shift) == row
    loads[0].wait()
    flat = msg_ref[...].reshape(legs, DD)
    spread = jnp.concatenate(
        [jnp.where(unfold_mask, flat[m : m + 1, :], 0.0) for m in range(legs)], axis=0
    )
    edge_all = select_dot(spread, minor_t, 3)
    edge = [edge_all[m * D : (m + 1) * D] for m in range(legs)]

    gather = permutation(DD, rows, mixed, 0)

    def unmix(i):
        for b in range(0, mixed, 2):
            pair = jnp.concatenate(
                [a_ref[i, b * DD : (b + 1) * DD, :], a_ref[i, (b + 1) * DD : (b + 2) * DD, :]],
                axis=1,
            )
            block = dot(gather, pair).astype(BF16)
            for c in range(2):
                for g in range(mixed):
                    x_ref[
                        i,
                        g % 2,
                        (b + c) * rows : (b + c + 1) * rows,
                        (g // 2) * LANES : (g // 2 + 1) * LANES,
                    ] = block[g * rows : (g + 1) * rows, c * LANES : (c + 1) * LANES]
        for s in range(2):
            xt_ref[i, s] = x_ref[i, s].T

    def reduce_major(gram, weight):
        total = gram[:D] * weight[0:1, :]
        for d in range(1, D):
            total = total + gram[d * D : (d + 1) * D] * weight[d : d + 1, :]
        return total

    def reduce_minor(gram, weight):
        return jnp.concatenate(
            [
                jnp.sum(gram[d * D : (d + 1) * D] * weight, axis=0, keepdims=True)
                for d in range(D)
            ],
            axis=0,
        )

    def kinds_of(totals):
        if len(totals) == 1:
            return totals
        return [totals[0] + totals[1], totals[0] - totals[1]]

    def outgoing(turn, incoming, last):
        stacked = jnp.concatenate([v.astype(BF16) for v in incoming], axis=0)
        spread = dot(stacked, both)
        kinds = 2 if last else 1

        def by_major(m):
            return spread[m * D : (m + 1) * D, :DD]

        def by_minor(m):
            return spread[m * D : (m + 1) * D, DD:]

        def normalised(totals, selector, slots):
            blocks = []
            for kind in range(kinds):
                rows_of = jnp.concatenate([t[kind] for t in totals], axis=0)
                blocks.append(select_dot(rows_of, selector, 2))
            out = {}
            for n, slot in enumerate(slots):
                own = [b[n * D : (n + 1) * D] for b in blocks]
                power = jnp.sum(own[0] * own[0], axis=(0, 1), keepdims=True) / DD
                scale = jnp.sqrt(power + EPSILON)
                out[slot] = [v / scale for v in own]
            return out

        firsts = []
        for i in range(cols):
            if turn == 0:
                loads[1 + i].wait()
                unmix(i)
            for path in range(2):
                left, right = (x_ref, xt_ref) if path == 0 else (xt_ref, x_ref)
                far = i * 4 + 2 * (1 - path)
                near = i * 4 + 2 * path
                slot = i * 2 + path
                build_kron(kron_ref, slot, by_major(far), by_minor(far + 1))
                y = [dot(left[i, s], kron_ref[slot]).astype(BF16) for s in range(2)]
                if last:
                    grams = [dot(y[s], right[i, s]) for s in range(2)]
                else:
                    grams = [dot(y[0], right[i, 0]) + dot(y[1], right[i, 1])]
                for k, gram in enumerate(grams):
                    gram_ref[slot, k] = gram
                firsts.append(kinds_of([reduce_minor(g, by_minor(near + 1)) for g in grams]))

        def seconds(slots):
            totals = []
            for slot in slots:
                weight = by_major((slot // 2) * 4 + 2 * (slot % 2))
                totals.append(
                    kinds_of([reduce_major(gram_ref[slot, k], weight) for k in range(kinds)])
                )
            return normalised(totals, minor_t, slots)

        vertical = normalised(firsts, major_t, list(range(2 * cols)))
        ends = [0, 2 * cols - 1]
        sides = seconds(ends)

        def rest():
            others = [slot for slot in range(2 * cols) if slot not in ends]
            if others:
                sides.update(seconds(others))
            values = []
            for kind in range(kinds):
                blocks = []
                for slot in range(2 * cols):
                    blocks += [vertical[slot][kind], sides[slot][kind]]
                values.append(blocks)
            return values

        return vertical, sides, rest

    def exchange(turn, vertical, sides, kinds):
        width = kinds * cols * D

        def packed(path):
            return jnp.concatenate(
                [vertical[2 * i + path][k] for k in range(kinds) for i in range(cols)], axis=1
            )

        up_src = send_up.at[turn]
        down_src = send_down.at[turn]
        side_src = send_side.at[turn]
        send_up[turn, :, :width] = packed(0)
        send_down[turn, :, :width] = packed(1)
        side_right = jnp.concatenate(sides[2 * cols - 1], axis=1)
        side_left = jnp.concatenate(sides[0], axis=1)
        send_side[turn, :, : kinds * D] = jnp.where(group == 0, side_right, side_left)

        def copy(src, dst, k, device):
            return pltpu.make_async_remote_copy(
                src_ref=src, dst_ref=dst.at[turn], send_sem=send_sem.at[turn, k],
                recv_sem=recv_sem.at[turn, k], device_id=device, device_id_type=MESH,
            )

        to_up = copy(up_src, recv_down, 0, {"tile": tile - 1})
        to_down = copy(down_src, recv_up, 1, {"tile": tile + 1})
        to_side = copy(side_src, recv_side, 2, {"group": 1 - group})

        @pl.when(has_up)
        def _():
            to_up.start()

        @pl.when(has_down)
        def _():
            to_down.start()

        to_side.start()
        return to_up, to_down, to_side

    def finish(turn, copies, values):
        to_up, to_down, to_side = copies
        kinds = len(values)
        width = kinds * cols * D

        def border(leg):
            blocks = [edge[i * 4 + leg] for i in range(cols)]
            if kinds == 2:
                blocks += [jnp.zeros((D, D), F32)] * cols
            return jnp.concatenate(blocks, axis=1)

        @pl.when(has_up)
        def _():
            to_up.wait_send()
            to_down.wait_recv()

        @pl.when(jnp.logical_not(has_up))
        def _():
            recv_up[turn, :, :width] = border(0)

        @pl.when(has_down)
        def _():
            to_down.wait_send()
            to_up.wait_recv()

        @pl.when(jnp.logical_not(has_down))
        def _():
            recv_down[turn, :, :width] = border(2)

        to_side.wait()
        from_up, from_down, from_side = recv_up[turn], recv_down[turn], recv_side[turn]
        routed = []
        for kind in range(kinds):
            blocks = []
            for i in range(cols):
                at = (kind * cols + i) * D
                side = from_side[:, kind * D : (kind + 1) * D]
                zero = jnp.zeros((D, D), F32)
                out_left = edge[i * 4 + 1] if kind == 0 else zero
                out_right = edge[i * 4 + 3] if kind == 0 else zero
                blocks.append(from_up[:, at : at + D])
                if i > 0:
                    blocks.append(values[kind][(i - 1) * 4 + 3])
                else:
                    blocks.append(jnp.where(group == 0, out_left, side))
                blocks.append(from_down[:, at : at + D])
                if i < cols - 1:
                    blocks.append(values[kind][(i + 1) * 4 + 1])
                else:
                    blocks.append(jnp.where(group == groups - 1, out_right, side))
            routed.append(blocks)
        return routed

    incoming = edge
    for turn in range(ITERS):
        last = turn == ITERS - 1
        vertical, sides, rest = outgoing(turn, incoming, last)
        if turn == 0:
            inside = jnp.logical_and(has_up, has_down)

            @pl.when(inside)
            def _():
                pl.semaphore_wait(barrier, 3)

            @pl.when(jnp.logical_not(inside))
            def _():
                pl.semaphore_wait(barrier, 2)

        copies = exchange(turn, vertical, sides, 2 if last else 1)
        values = rest()
        if turn == 0:
            for i in range(cols):
                a0, a1 = x_ref[i, 0].astype(F32), x_ref[i, 1].astype(F32)
                ch, sh = math.cosh(FIELD), math.sinh(FIELD)
                ax_ref[i, 0] = (ch * a0 + sh * a1).astype(BF16)
                ax_ref[i, 1] = (ch * a1 + sh * a0).astype(BF16)
        routed = finish(turn, copies, values)
        incoming = routed[0]

    mout_ref[...] = jnp.concatenate(incoming, axis=0)
    env_ref[0] = jnp.concatenate([o + n for o, n in zip(values[0], routed[0])], axis=1)
    env_ref[1] = jnp.concatenate([o + n for o, n in zip(values[1], routed[1])], axis=1)
    lane_w = iota((D, wide), 1)
    leg_of = (lane_w >> shift) & 3
    col_of = (lane_w >> (shift + 2)) + group * cols
    at_edge = (
        ((leg_of == 0) & (tile == 0))
        | ((leg_of == 2) & (tile == tiles - 1))
        | ((leg_of == 1) & (col_of == 0))
        | ((leg_of == 3) & (col_of == groups * cols - 1))
    )
    env_ref[2] = jnp.where(at_edge, 1.0, 0.0).astype(F32)


def gates_kernel(cols, D, ax_ref, env_ref, in_ref, out_hbm, mout_hbm,
                 kron_ref, out_ref, mout_ref, store_sem):
    DD = D * D
    shift = D.bit_length() - 1
    mixed = 2 * (DD // LANES)
    rows = DD // mixed
    legs = 4 * cols
    wide = legs * D
    lane = iota((D, DD), 1)
    row = iota((D, DD), 0)
    major = one_hot((lane >> shift) == row)
    minor = one_hot((lane & (D - 1)) == row)
    both = jnp.concatenate([major, minor], axis=1)

    spread = select_dot(in_ref[...], minor, 3)
    unfold_mask = (lane >> shift) == row
    flat_rows = [
        jnp.sum(
            jnp.where(unfold_mask, spread[m * D : (m + 1) * D], 0.0), axis=0, keepdims=True
        )
        for m in range(legs)
    ]
    mout_ref[...] = jnp.concatenate(flat_rows, axis=0).reshape(cols, 4, DD)
    store_msg = pltpu.make_async_copy(mout_ref, mout_hbm, store_sem.at[cols])
    store_msg.start()

    g0, g1 = math.cosh(COUPLING), math.sinh(COUPLING)
    cross = math.sqrt(g0 * g1)
    root2 = math.sqrt(2.0)
    msg_sum, twist_sum = env_ref[0], env_ref[1]
    y_top = ((g0 * msg_sum + cross * twist_sum) / root2).astype(BF16)
    y_bot = ((cross * twist_sum + g1 * msg_sum) / root2).astype(BF16)
    y_both = jnp.concatenate([y_top, y_bot], axis=0)
    same = (iota((wide, wide), 0) >> shift) == (iota((wide, wide), 1) >> shift)
    same_bf = one_hot(same)
    lane_w = iota((D, wide), 1)
    unit = jnp.where((lane_w & (D - 1)) == iota((D, wide), 0), 1.0, 0.0).astype(F32)

    def diagonal(value):
        return jnp.concatenate([value] * legs, axis=0) * same_bf

    def times(left, right):
        count = left.shape[0]
        (l_hi, l_lo), (r_hi, r_lo) = parts(left, 2), parts(right, 2)
        main = dot(jnp.concatenate([l_hi, l_lo], axis=0), diagonal(r_hi))
        return main[:count] + (main[count:] + dot(l_hi, diagonal(r_lo)))

    full = jnp.where(same, dot_tn(y_both, y_both), 0.0)
    gram = full[:D]
    for m in range(1, legs):
        gram = gram + full[m * D : (m + 1) * D]
    diag = jnp.sum(gram * unit, axis=0, keepdims=True)
    trace = select_dot(jnp.broadcast_to(diag, (8, wide)), same_bf, 3)[0:1] + EPSILON
    current = gram / trace
    factor = 1.5 * unit - 0.5 * current
    inverse = factor
    current = times(current, factor)
    for step in range(1, NS_STEPS):
        factor = 1.5 * unit - 0.5 * times(inverse, current)
        if step < NS_STEPS - 1:
            stepped = times(jnp.concatenate([inverse, current], axis=0), factor)
            inverse, current = stepped[:D], stepped[D:]
        else:
            inverse = times(inverse, factor)
    q_both = dot(y_both, diagonal(inverse.astype(BF16))) / jnp.sqrt(trace)
    first = math.sqrt(g0) * q_both[:D]
    second = math.sqrt(g1) * q_both[D:]
    at_edge = env_ref[2] > 0.5
    scatter = permutation(DD, rows, mixed, 1)
    spreads = []
    for weight in (first + second, first - second):
        weight = jnp.where(at_edge, unit, weight)
        spreads.append(dot(weight.T.astype(BF16), both))
    stores = [
        pltpu.make_async_copy(out_ref.at[i], out_hbm.at[i], store_sem.at[i]) for i in range(cols)
    ]
    def gate(i):
        m = i * 4
        gated = []
        for s in range(2):
            w = spreads[s]
            slot = (i * 2 + s) * 2
            build_kron(
                kron_ref, slot, w[(m + 2) * D : (m + 3) * D, :DD], w[(m + 3) * D : (m + 4) * D, DD:]
            )
            build_kron(
                kron_ref, slot + 1, w[m * D : (m + 1) * D, :DD], w[(m + 1) * D : (m + 2) * D, DD:]
            )
            half = dot_nt(ax_ref[i, s], kron_ref[slot]).astype(BF16)
            gated.append(dot(kron_ref[slot + 1], half).astype(BF16))
        return gated

    def emit(i, gated):
        for b in range(0, mixed, 2):
            block = jnp.concatenate(
                [
                    jnp.concatenate(
                        [
                            gated[g % 2][
                                (b + c) * rows : (b + c + 1) * rows,
                                (g // 2) * LANES : (g // 2 + 1) * LANES,
                            ]
                            for c in range(2)
                        ],
                        axis=1,
                    )
                    for g in range(mixed)
                ],
                axis=0,
            )
            done = dot(scatter, block).astype(BF16)
            for c in range(2):
                out_ref[i, (b + c) * DD : (b + c + 1) * DD, :] = done[
                    :, c * LANES : (c + 1) * LANES
                ]
        stores[i].start()

    waiting = gate(0)
    for i in range(cols):
        following = gate(i + 1) if i + 1 < cols else None
        emit(i, waiting)
        waiting = following
    for store in stores + [store_msg]:
        store.wait()


def per_device(tiles, groups, site_tensors, msg_in):
    _, cols, _, size = site_tensors.shape
    DD = msg_in.shape[-1]
    D = math.isqrt(DD)
    chunks = size // LANES
    a = site_tensors.reshape(cols, 2, chunks, LANES).transpose(0, 2, 1, 3)
    a = a.reshape(cols, 2 * chunks, LANES)
    wide = 2 * cols * D
    legs = 4 * cols
    vmem = pl.BlockSpec(memory_space=pltpu.VMEM)
    hbm = pl.BlockSpec(memory_space=pltpu.HBM)
    gated, env, stacked = pl.pallas_call(
        functools.partial(messages_kernel, tiles, groups, cols, D),
        out_shape=(
            jax.ShapeDtypeStruct((cols, 2, DD, DD), BF16),
            jax.ShapeDtypeStruct((3, D, legs * D), F32),
            jax.ShapeDtypeStruct((legs * D, D), F32),
        ),
        in_specs=[hbm, hbm],
        out_specs=(vmem, vmem, vmem),
        scratch_shapes=[
            pltpu.VMEM(a.shape, BF16),
            pltpu.VMEM((cols, 4, DD), F32),
            pltpu.VMEM((cols, 2, DD, DD), BF16),
            pltpu.VMEM((cols, 2, DD, DD), BF16),
            pltpu.VMEM((2 * cols, DD, DD), BF16),
            pltpu.VMEM((2 * cols, 2, DD, DD), F32),
            pltpu.VMEM((ITERS, D, wide), F32),
            pltpu.VMEM((ITERS, D, wide), F32),
            pltpu.VMEM((ITERS, D, 2 * D), F32),
            pltpu.VMEM((ITERS, D, wide), F32),
            pltpu.VMEM((ITERS, D, wide), F32),
            pltpu.VMEM((ITERS, D, 2 * D), F32),
            pltpu.SemaphoreType.DMA((ITERS, 3)),
            pltpu.SemaphoreType.DMA((ITERS, 3)),
            pltpu.SemaphoreType.DMA((cols + 1,)),
        ],
        compiler_params=pltpu.CompilerParams(
            collective_id=0, has_side_effects=True, vmem_limit_bytes=24 * 2**20
        ),
    )(
        pltpu.with_memory_space_constraint(a, pltpu.HBM),
        pltpu.with_memory_space_constraint(msg_in[0], pltpu.HBM),
    )
    out, messages = pl.pallas_call(
        functools.partial(gates_kernel, cols, D),
        out_shape=(
            jax.ShapeDtypeStruct(a.shape, BF16),
            jax.ShapeDtypeStruct((cols, 4, DD), F32),
        ),
        in_specs=[vmem, vmem, vmem],
        out_specs=(hbm, hbm),
        scratch_shapes=[
            pltpu.VMEM((4 * cols, DD, DD), BF16),
            pltpu.VMEM(a.shape, BF16),
            pltpu.VMEM((cols, 4, DD), F32),
            pltpu.SemaphoreType.DMA((cols + 1,)),
        ],
        compiler_params=pltpu.CompilerParams(vmem_limit_bytes=24 * 2**20),
    )(gated, env, stacked)
    out = out.reshape(cols, chunks, 2, LANES).transpose(0, 2, 1, 3)
    return out.reshape(1, cols, 2, size), messages[None]


def solution(mesh):
    spec = P("tile", "group", None, None)
    return jax.shard_map(
        functools.partial(per_device, mesh.shape["tile"], mesh.shape["group"]),
        mesh=mesh, in_specs=(spec, spec), out_specs=(spec, spec), check_vma=False,
    )
```

```python
import functools
import math

import jax
import jax.numpy as jnp
from jax import lax
from jax.experimental import pallas as pl
from jax.experimental.pallas import tpu as pltpu
from jax.sharding import PartitionSpec as P

ITERS = 2
NS_STEPS = 6
LANES = 128
EPSILON = 1e-06
COUPLING = 0.5
FIELD = 0.3
F32 = jnp.float32
BF16 = jnp.bfloat16
MESH = pl.DeviceIdType.MESH


def iota(shape, axis):
    return lax.broadcasted_iota(jnp.int32, shape, axis)


def dot(a, b):
    return jnp.dot(a, b, preferred_element_type=F32)


def dot_nt(a, b):
    return lax.dot_general(a, b, (((1,), (1,)), ((), ())), preferred_element_type=F32)


def dot_tn(a, b):
    return lax.dot_general(a, b, (((0,), (0,)), ((), ())), preferred_element_type=F32)


def parts(value, count):
    out = []
    for _ in range(count):
        piece = value.astype(BF16)
        out.append(piece)
        value = value - piece.astype(F32)
    return out


def select_dot(value, selector, count):
    total = None
    for piece in parts(value, count):
        term = dot(piece, selector)
        total = term if total is None else total + term
    return total


def one_hot(mask):
    return jnp.where(mask, 1.0, 0.0).astype(BF16)


def build_kron(kron_ref, slot, first, second):
    D = first.shape[0]
    for d in range(D):
        kron_ref[slot, d * D : (d + 1) * D, :] = (first[d : d + 1, :] * second).astype(BF16)


def permutation(DD, rows, mixed, out_axis):
    p, k = iota((DD, DD), out_axis), iota((DD, DD), 1 - out_axis)
    row_bits = rows.bit_length() - 1
    return one_hot(k == (p & (rows - 1)) * mixed + (p >> row_bits))


def pick(value, index):
    return jnp.take_along_axis(value, index, axis=1, mode="promise_in_bounds")


def row_of(value, k):
    return jnp.broadcast_to(value[k : k + 1, :], value.shape)


def bond_weights(msg_sum, twist_sum):
    D = msg_sum.shape[0]
    lane = iota((D, LANES), 1)
    row = iota((D, LANES), 0)
    inner = lane & (D - 1)
    start = lane - inner
    turned = start + row
    unit = jnp.where(inner == row, 1.0, 0.0).astype(F32)
    g0, g1 = math.cosh(COUPLING), math.sinh(COUPLING)
    cross = math.sqrt(g0 * g1)
    root2 = math.sqrt(2.0)
    halves = [
        ((g0 * msg_sum + cross * twist_sum) / root2).astype(BF16).astype(F32),
        ((cross * twist_sum + g1 * msg_sum) / root2).astype(BF16).astype(F32),
    ]
    squares = halves[0] * halves[0] + halves[1] * halves[1]
    squares = jnp.broadcast_to(jnp.sum(squares, axis=0, keepdims=True), (D, LANES))
    trace = jnp.sum(pick(squares, turned), axis=0, keepdims=True) + EPSILON

    gram = None
    rotated = []
    for half in halves:
        transposed = None
        for k in range(D):
            own = row_of(half, k)
            column = pick(own, turned)
            term = column * own
            gram = term if gram is None else gram + term
            placed = jnp.where(inner == k, column, 0.0)
            transposed = placed if transposed is None else transposed + placed
        rotated.append(transposed)

    def columns(value):
        return [pick(row_of(value, k), turned) for k in range(D)]

    def times(left, right):
        sums = [None] * 4
        for k in range(D):
            term = left[k] * row_of(right, k)
            sums[k % 4] = term if sums[k % 4] is None else sums[k % 4] + term
        return (sums[0] + sums[1]) + (sums[2] + sums[3])

    state = gram / trace
    for step in range(NS_STEPS - 2):
        left = columns(state)
        square = times(left, state)
        rotated = [1.5 * v - 0.5 * times(left, v) for v in rotated]
        state = times(left, 2.25 * unit - 1.5 * state + 0.25 * square)
    left = columns(state)
    rotated = [1.5 * v - 0.5 * times(left, v) for v in rotated]
    again = rotated
    for _ in range(2):
        again = [1.5 * v - 0.5 * times(left, v) for v in again]
    rotated = [1.5 * v - 0.5 * times(left, w) for v, w in zip(rotated, again)]
    scale = 1.0 / jnp.sqrt(trace)
    first = math.sqrt(g0) * rotated[0] * scale
    second = math.sqrt(g1) * rotated[1] * scale
    return [first + second, first - second]


def messages_kernel(tiles, groups, cols, D, a_hbm, msg_hbm, ax_ref, env_ref, inner_ref, mout_ref,
           a_ref, msg_ref, x_ref, xt_ref, kron_ref, gram_ref,
           send_up, send_down, send_side, recv_up, recv_down, recv_side,
           send_sem, recv_sem, load_sem):
    loads = [pltpu.make_async_copy(msg_hbm, msg_ref, load_sem.at[cols])]
    loads += [
        pltpu.make_async_copy(a_hbm.at[i], a_ref.at[i], load_sem.at[i]) for i in range(cols)
    ]
    for load in loads:
        load.start()
    tile = lax.axis_index("tile")
    group = lax.axis_index("group")
    DD = D * D
    shift = D.bit_length() - 1
    halves = DD // LANES
    mixed = 2 * halves
    rows = DD // mixed
    legs = 4 * cols
    wide = legs * D
    has_up = tile > 0
    has_down = tile < tiles - 1

    barrier = pltpu.get_barrier_semaphore()

    @pl.when(has_up)
    def _():
        pl.semaphore_signal(barrier, inc=1, device_id={"tile": tile - 1}, device_id_type=MESH)

    @pl.when(has_down)
    def _():
        pl.semaphore_signal(barrier, inc=1, device_id={"tile": tile + 1}, device_id_type=MESH)

    pl.semaphore_signal(barrier, inc=1, device_id={"group": 1 - group}, device_id_type=MESH)

    lane = iota((D, DD), 1)
    row = iota((D, DD), 0)
    major = one_hot((lane >> shift) == row)
    minor = one_hot((lane & (D - 1)) == row)
    both = jnp.concatenate([major, minor], axis=1)
    major_t = one_hot((iota((DD, D), 0) >> shift) == iota((DD, D), 1))
    minor_t = one_hot((iota((DD, D), 0) & (D - 1)) == iota((DD, D), 1))

    unfold_mask = (lane >> shift) == row
    loads[0].wait()
    flat = msg_ref[...].reshape(legs, DD)
    spread = jnp.concatenate(
        [jnp.where(unfold_mask, flat[m : m + 1, :], 0.0) for m in range(legs)], axis=0
    )
    edge_all = select_dot(spread, minor_t, 3)
    edge = [edge_all[m * D : (m + 1) * D] for m in range(legs)]

    gather = permutation(DD, rows, mixed, 0)

    def unmix(i):
        for b in range(0, mixed, 2):
            pair = jnp.concatenate(
                [a_ref[i, b * DD : (b + 1) * DD, :], a_ref[i, (b + 1) * DD : (b + 2) * DD, :]],
                axis=1,
            )
            block = dot(gather, pair).astype(BF16)
            for c in range(2):
                for g in range(mixed):
                    x_ref[
                        i,
                        g % 2,
                        (b + c) * rows : (b + c + 1) * rows,
                        (g // 2) * LANES : (g // 2 + 1) * LANES,
                    ] = block[g * rows : (g + 1) * rows, c * LANES : (c + 1) * LANES]
        for s in range(2):
            xt_ref[i, s] = x_ref[i, s].T

    def reduce_major(gram, weight):
        total = gram[:D] * weight[0:1, :]
        for d in range(1, D):
            total = total + gram[d * D : (d + 1) * D] * weight[d : d + 1, :]
        return total

    def reduce_minor(gram, weight):
        return jnp.concatenate(
            [
                jnp.sum(gram[d * D : (d + 1) * D] * weight, axis=0, keepdims=True)
                for d in range(D)
            ],
            axis=0,
        )

    def kinds_of(totals):
        if len(totals) == 1:
            return totals
        return [totals[0] + totals[1], totals[0] - totals[1]]

    def outgoing(turn, incoming, last):
        stacked = jnp.concatenate([v.astype(BF16) for v in incoming], axis=0)
        spread = dot(stacked, both)
        kinds = 2 if last else 1

        def by_major(m):
            return spread[m * D : (m + 1) * D, :DD]

        def by_minor(m):
            return spread[m * D : (m + 1) * D, DD:]

        def normalised(totals, selector, slots):
            blocks = []
            for kind in range(kinds):
                rows_of = jnp.concatenate([t[kind] for t in totals], axis=0)
                blocks.append(select_dot(rows_of, selector, 2))
            out = {}
            for n, slot in enumerate(slots):
                own = [b[n * D : (n + 1) * D] for b in blocks]
                power = jnp.sum(own[0] * own[0], axis=(0, 1), keepdims=True) / DD
                scale = jnp.sqrt(power + EPSILON)
                out[slot] = [v / scale for v in own]
            return out

        firsts = []
        for i in range(cols):
            if turn == 0:
                loads[1 + i].wait()
                unmix(i)
            for path in range(2):
                left, right = (x_ref, xt_ref) if path == 0 else (xt_ref, x_ref)
                far = i * 4 + 2 * (1 - path)
                near = i * 4 + 2 * path
                slot = i * 2 + path
                build_kron(kron_ref, slot, by_major(far), by_minor(far + 1))
                y = [dot(left[i, s], kron_ref[slot]).astype(BF16) for s in range(2)]
                if last:
                    grams = [dot(y[s], right[i, s]) for s in range(2)]
                else:
                    grams = [dot(y[0], right[i, 0]) + dot(y[1], right[i, 1])]
                for k, gram in enumerate(grams):
                    gram_ref[slot, k] = gram
                firsts.append(kinds_of([reduce_minor(g, by_minor(near + 1)) for g in grams]))

        def seconds(slots):
            totals = []
            for slot in slots:
                weight = by_major((slot // 2) * 4 + 2 * (slot % 2))
                totals.append(
                    kinds_of([reduce_major(gram_ref[slot, k], weight) for k in range(kinds)])
                )
            return normalised(totals, minor_t, slots)

        vertical = normalised(firsts, major_t, list(range(2 * cols)))
        ends = [0, 2 * cols - 1]
        sides = seconds(ends)

        def rest():
            others = [slot for slot in range(2 * cols) if slot not in ends]
            if others:
                sides.update(seconds(others))
            values = []
            for kind in range(kinds):
                blocks = []
                for slot in range(2 * cols):
                    blocks += [vertical[slot][kind], sides[slot][kind]]
                values.append(blocks)
            return values

        return vertical, sides, rest

    def exchange(turn, vertical, sides, kinds):
        width = kinds * cols * D

        def packed(path):
            return jnp.concatenate(
                [vertical[2 * i + path][k] for k in range(kinds) for i in range(cols)], axis=1
            )

        up_src = send_up.at[turn]
        down_src = send_down.at[turn]
        side_src = send_side.at[turn]
        send_up[turn, :, :width] = packed(0)
        send_down[turn, :, :width] = packed(1)
        side_right = jnp.concatenate(sides[2 * cols - 1], axis=1)
        side_left = jnp.concatenate(sides[0], axis=1)
        send_side[turn, :, : kinds * D] = jnp.where(group == 0, side_right, side_left)

        def copy(src, dst, k, device):
            return pltpu.make_async_remote_copy(
                src_ref=src, dst_ref=dst.at[turn], send_sem=send_sem.at[turn, k],
                recv_sem=recv_sem.at[turn, k], device_id=device, device_id_type=MESH,
            )

        to_up = copy(up_src, recv_down, 0, {"tile": tile - 1})
        to_down = copy(down_src, recv_up, 1, {"tile": tile + 1})
        to_side = copy(side_src, recv_side, 2, {"group": 1 - group})

        @pl.when(has_up)
        def _():
            to_up.start()

        @pl.when(has_down)
        def _():
            to_down.start()

        to_side.start()
        return to_up, to_down, to_side

    def finish(turn, copies, values):
        to_up, to_down, to_side = copies
        kinds = len(values)
        width = kinds * cols * D

        def border(leg):
            blocks = [edge[i * 4 + leg] for i in range(cols)]
            if kinds == 2:
                blocks += [jnp.zeros((D, D), F32)] * cols
            return jnp.concatenate(blocks, axis=1)

        @pl.when(has_up)
        def _():
            to_up.wait_send()
            to_down.wait_recv()

        @pl.when(jnp.logical_not(has_up))
        def _():
            recv_up[turn, :, :width] = border(0)

        @pl.when(has_down)
        def _():
            to_down.wait_send()
            to_up.wait_recv()

        @pl.when(jnp.logical_not(has_down))
        def _():
            recv_down[turn, :, :width] = border(2)

        to_side.wait()
        from_up, from_down, from_side = recv_up[turn], recv_down[turn], recv_side[turn]
        routed = []
        for kind in range(kinds):
            blocks = []
            for i in range(cols):
                at = (kind * cols + i) * D
                side = from_side[:, kind * D : (kind + 1) * D]
                zero = jnp.zeros((D, D), F32)
                out_left = edge[i * 4 + 1] if kind == 0 else zero
                out_right = edge[i * 4 + 3] if kind == 0 else zero
                blocks.append(from_up[:, at : at + D])
                if i > 0:
                    blocks.append(values[kind][(i - 1) * 4 + 3])
                else:
                    blocks.append(jnp.where(group == 0, out_left, side))
                blocks.append(from_down[:, at : at + D])
                if i < cols - 1:
                    blocks.append(values[kind][(i + 1) * 4 + 1])
                else:
                    blocks.append(jnp.where(group == groups - 1, out_right, side))
            routed.append(blocks)
        return routed

    def lined(blocks):
        spare = LANES // D - len(blocks)
        return jnp.concatenate(blocks + [jnp.zeros((D, D), F32)] * spare, axis=1)

    incoming = edge
    for turn in range(ITERS):
        last = turn == ITERS - 1
        vertical, sides, rest = outgoing(turn, incoming, last)
        if turn == 0:
            inside = jnp.logical_and(has_up, has_down)

            @pl.when(inside)
            def _():
                pl.semaphore_wait(barrier, 3)

            @pl.when(jnp.logical_not(inside))
            def _():
                pl.semaphore_wait(barrier, 2)

        copies = exchange(turn, vertical, sides, 2 if last else 1)
        values = rest()
        if turn == 0:
            for i in range(cols):
                a0, a1 = x_ref[i, 0].astype(F32), x_ref[i, 1].astype(F32)
                ch, sh = math.cosh(FIELD), math.sinh(FIELD)
                ax_ref[i, 0] = (ch * a0 + sh * a1).astype(BF16)
                ax_ref[i, 1] = (ch * a1 + sh * a0).astype(BF16)
        if last:
            sums = [
                lined([v[i * 4 + 3] + v[i * 4 + 5] for i in range(cols - 1)]) for v in values
            ]
            for s, weight in enumerate(bond_weights(*sums)):
                inner_ref[s] = weight.astype(BF16).astype(F32)
        routed = finish(turn, copies, values)
        incoming = routed[0]

    outer = [i * 4 for i in range(cols)] + [i * 4 + 2 for i in range(cols)]
    outer += [1, 4 * cols - 1]
    for kind in range(2):
        env_ref[kind] = lined([values[kind][m] + routed[kind][m] for m in outer])
    for t in range(mout_ref.shape[0]):
        mout_ref[t] = lined(incoming[t * 8 : t * 8 + 8])


def gates_kernel(tiles, groups, cols, D, ax_ref, env_ref, inner_ref, in_ref, out_hbm, mout_hbm,
                 kron_ref, out_ref, mout_ref, store_sem):
    tile = lax.axis_index("tile")
    group = lax.axis_index("group")
    DD = D * D
    shift = D.bit_length() - 1
    halves = DD // LANES
    mixed = 2 * halves
    rows = DD // mixed
    lane = iota((D, LANES), 1)
    row = iota((D, LANES), 0)
    inner = lane & (D - 1)
    start = lane - inner
    slot = lane >> shift

    unit = jnp.where(inner == row, 1.0, 0.0).astype(F32)
    at_edge = (
        ((slot < cols) & (tile == 0))
        | ((slot >= cols) & (slot < 2 * cols) & (tile == tiles - 1))
        | ((slot == 2 * cols) & (group == 0))
        | ((slot == 2 * cols + 1) & (group == groups - 1))
    )
    late = [
        jnp.where(at_edge, unit, w).astype(BF16).astype(F32)
        for w in bond_weights(env_ref[0], env_ref[1])
    ]
    early = [inner_ref[s] for s in range(2)]

    unfold_mask = slot == (row & (LANES // D - 1))
    flat_rows = []
    for m in range(4 * cols):
        value = in_ref[m // 8]
        tiled = jnp.where(unfold_mask, pick(value, inner + (m % 8) * D), 0.0)
        step = D // halves
        flat_rows.append(
            jnp.concatenate(
                [
                    jnp.sum(tiled[h * step : (h + 1) * step], axis=0, keepdims=True)
                    for h in range(halves)
                ],
                axis=1,
            )
        )
    mout_ref[...] = jnp.concatenate(flat_rows, axis=0).reshape(cols, 4, DD)
    store_msg = pltpu.make_async_copy(mout_ref, mout_hbm, store_sem.at[cols])
    store_msg.start()

    def by_major(value, m):
        return jnp.concatenate(
            [pick(value, m * D + slot + h * (LANES // D)) for h in range(halves)], axis=1
        )

    def by_minor(value, m):
        part = pick(value, m * D + inner)
        return jnp.concatenate([part] * halves, axis=1)

    scatter = permutation(DD, rows, mixed, 1)
    stores = [
        pltpu.make_async_copy(out_ref.at[i], out_hbm.at[i], store_sem.at[i]) for i in range(cols)
    ]

    def gate(i):
        gated = []
        for s in range(2):
            left = by_minor(late[s], 2 * cols) if i == 0 else by_minor(early[s], i - 1)
            right = by_minor(late[s], 2 * cols + 1) if i == cols - 1 else by_minor(early[s], i)
            at = (i * 2 + s) * 2
            build_kron(kron_ref, at, by_major(late[s], cols + i), right)
            build_kron(kron_ref, at + 1, by_major(late[s], i), left)
            half = dot_nt(ax_ref[i, s], kron_ref[at]).astype(BF16)
            gated.append(dot(kron_ref[at + 1], half).astype(BF16))
        return gated

    def emit(i, gated):
        for b in range(0, mixed, 2):
            block = jnp.concatenate(
                [
                    jnp.concatenate(
                        [
                            gated[g % 2][
                                (b + c) * rows : (b + c + 1) * rows,
                                (g // 2) * LANES : (g // 2 + 1) * LANES,
                            ]
                            for c in range(2)
                        ],
                        axis=1,
                    )
                    for g in range(mixed)
                ],
                axis=0,
            )
            done = dot(scatter, block).astype(BF16)
            for c in range(2):
                out_ref[i, (b + c) * DD : (b + c + 1) * DD, :] = done[
                    :, c * LANES : (c + 1) * LANES
                ]
        stores[i].start()

    waiting = gate(0)
    for i in range(cols):
        following = gate(i + 1) if i + 1 < cols else None
        emit(i, waiting)
        waiting = following
    for store in stores + [store_msg]:
        store.wait()


def per_device(tiles, groups, site_tensors, msg_in):
    _, cols, _, size = site_tensors.shape
    DD = msg_in.shape[-1]
    D = math.isqrt(DD)
    chunks = size // LANES
    a = site_tensors.reshape(cols, 2, chunks, LANES).transpose(0, 2, 1, 3)
    a = a.reshape(cols, 2 * chunks, LANES)
    wide = 2 * cols * D
    legs = 4 * cols
    vmem = pl.BlockSpec(memory_space=pltpu.VMEM)
    hbm = pl.BlockSpec(memory_space=pltpu.HBM)
    gated, env, inner, stacked = pl.pallas_call(
        functools.partial(messages_kernel, tiles, groups, cols, D),
        out_shape=(
            jax.ShapeDtypeStruct((cols, 2, DD, DD), BF16),
            jax.ShapeDtypeStruct((2, D, LANES), F32),
            jax.ShapeDtypeStruct((2, D, LANES), F32),
            jax.ShapeDtypeStruct((pl.cdiv(legs, LANES // D), D, LANES), F32),
        ),
        in_specs=[hbm, hbm],
        out_specs=(vmem, vmem, vmem, vmem),
        scratch_shapes=[
            pltpu.VMEM(a.shape, BF16),
            pltpu.VMEM((cols, 4, DD), F32),
            pltpu.VMEM((cols, 2, DD, DD), BF16),
            pltpu.VMEM((cols, 2, DD, DD), BF16),
            pltpu.VMEM((2 * cols, DD, DD), BF16),
            pltpu.VMEM((2 * cols, 2, DD, DD), F32),
            pltpu.VMEM((ITERS, D, wide), F32),
            pltpu.VMEM((ITERS, D, wide), F32),
            pltpu.VMEM((ITERS, D, 2 * D), F32),
            pltpu.VMEM((ITERS, D, wide), F32),
            pltpu.VMEM((ITERS, D, wide), F32),
            pltpu.VMEM((ITERS, D, 2 * D), F32),
            pltpu.SemaphoreType.DMA((ITERS, 3)),
            pltpu.SemaphoreType.DMA((ITERS, 3)),
            pltpu.SemaphoreType.DMA((cols + 1,)),
        ],
        compiler_params=pltpu.CompilerParams(
            collective_id=0, has_side_effects=True, vmem_limit_bytes=24 * 2**20
        ),
    )(
        pltpu.with_memory_space_constraint(a, pltpu.HBM),
        pltpu.with_memory_space_constraint(msg_in[0], pltpu.HBM),
    )
    out, messages = pl.pallas_call(
        functools.partial(gates_kernel, tiles, groups, cols, D),
        out_shape=(
            jax.ShapeDtypeStruct(a.shape, BF16),
            jax.ShapeDtypeStruct((cols, 4, DD), F32),
        ),
        in_specs=[vmem, vmem, vmem, vmem],
        out_specs=(hbm, hbm),
        scratch_shapes=[
            pltpu.VMEM((4 * cols, DD, DD), BF16),
            pltpu.VMEM(a.shape, BF16),
            pltpu.VMEM((cols, 4, DD), F32),
            pltpu.SemaphoreType.DMA((cols + 1,)),
        ],
        compiler_params=pltpu.CompilerParams(vmem_limit_bytes=24 * 2**20),
    )(gated, env, inner, stacked)
    out = out.reshape(cols, chunks, 2, LANES).transpose(0, 2, 1, 3)
    return out.reshape(1, cols, 2, size), messages[None]


def solution(mesh):
    spec = P("tile", "group", None, None)
    return jax.shard_map(
        functools.partial(per_device, mesh.shape["tile"], mesh.shape["group"]),
        mesh=mesh, in_specs=(spec, spec), out_specs=(spec, spec), check_vma=False,
    )
```

```python
import functools
import math

import jax
import jax.numpy as jnp
from jax import lax
from jax.experimental import pallas as pl
from jax.experimental.pallas import tpu as pltpu
from jax.sharding import PartitionSpec as P

ITERS = 2
NS_STEPS = 6
LANES = 128
EPSILON = 1e-06
COUPLING = 0.5
FIELD = 0.3
F32 = jnp.float32
BF16 = jnp.bfloat16
MESH = pl.DeviceIdType.MESH


def iota(shape, axis):
    return lax.broadcasted_iota(jnp.int32, shape, axis)


def dot(a, b):
    return jnp.dot(a, b, preferred_element_type=F32)


def dot_nt(a, b):
    return lax.dot_general(a, b, (((1,), (1,)), ((), ())), preferred_element_type=F32)


def dot_tn(a, b):
    return lax.dot_general(a, b, (((0,), (0,)), ((), ())), preferred_element_type=F32)


def parts(value, count):
    out = []
    for _ in range(count):
        piece = value.astype(BF16)
        out.append(piece)
        value = value - piece.astype(F32)
    return out


def select_dot(value, selector, count):
    total = None
    for piece in parts(value, count):
        term = dot(piece, selector)
        total = term if total is None else total + term
    return total


def one_hot(mask):
    return jnp.where(mask, 1.0, 0.0).astype(BF16)


def build_kron(kron_ref, slot, first, second):
    D = first.shape[0]
    for d in range(D):
        kron_ref[slot, d * D : (d + 1) * D, :] = (first[d : d + 1, :] * second).astype(BF16)


def pick(value, index):
    return jnp.take_along_axis(value, index, axis=1, mode="promise_in_bounds")


def row_of(value, k):
    return jnp.broadcast_to(value[k : k + 1, :], value.shape)


def bond_weights(msg_sum, twist_sum):
    D = msg_sum.shape[0]
    lane = iota((D, LANES), 1)
    row = iota((D, LANES), 0)
    inner = lane & (D - 1)
    start = lane - inner
    turned = start + row
    unit = jnp.where(inner == row, 1.0, 0.0).astype(F32)
    g0, g1 = math.cosh(COUPLING), math.sinh(COUPLING)
    cross = math.sqrt(g0 * g1)
    root2 = math.sqrt(2.0)
    halves = [
        ((g0 * msg_sum + cross * twist_sum) / root2).astype(BF16).astype(F32),
        ((cross * twist_sum + g1 * msg_sum) / root2).astype(BF16).astype(F32),
    ]
    squares = halves[0] * halves[0] + halves[1] * halves[1]
    squares = jnp.broadcast_to(jnp.sum(squares, axis=0, keepdims=True), (D, LANES))
    trace = jnp.sum(pick(squares, turned), axis=0, keepdims=True) + EPSILON

    gram = None
    rotated = []
    for half in halves:
        transposed = None
        for k in range(D):
            own = row_of(half, k)
            column = pick(own, turned)
            term = column * own
            gram = term if gram is None else gram + term
            placed = jnp.where(inner == k, column, 0.0)
            transposed = placed if transposed is None else transposed + placed
        rotated.append(transposed)

    def columns(value):
        return [pick(row_of(value, k), turned) for k in range(D)]

    def times(left, right):
        sums = [None] * 4
        for k in range(D):
            term = left[k] * row_of(right, k)
            sums[k % 4] = term if sums[k % 4] is None else sums[k % 4] + term
        return (sums[0] + sums[1]) + (sums[2] + sums[3])

    state = gram / trace
    for step in range(NS_STEPS - 2):
        left = columns(state)
        square = times(left, state)
        rotated = [1.5 * v - 0.5 * times(left, v) for v in rotated]
        state = times(left, 2.25 * unit - 1.5 * state + 0.25 * square)
    left = columns(state)
    rotated = [1.5 * v - 0.5 * times(left, v) for v in rotated]
    again = rotated
    for _ in range(2):
        again = [1.5 * v - 0.5 * times(left, v) for v in again]
    rotated = [1.5 * v - 0.5 * times(left, w) for v, w in zip(rotated, again)]
    scale = 1.0 / jnp.sqrt(trace)
    first = math.sqrt(g0) * rotated[0] * scale
    second = math.sqrt(g1) * rotated[1] * scale
    return [first + second, first - second]


def unmixing(D, mixed, out_axis):
    DD = D * D
    sub = D // mixed
    p, k = iota((DD, DD), out_axis), iota((DD, DD), 1 - out_axis)
    low = p & (D - 1)
    mid = (p >> (D.bit_length() - 1)) & (sub - 1)
    top = p >> (D * sub).bit_length() - 1
    return one_hot(k == low * D + mid * mixed + top)


def messages_kernel(tiles, groups, cols, D, a_hbm, msg_hbm, ax_ref, env_ref, inner_ref, mout_ref,
           a_ref, msg_ref, x_ref, xt_ref, x2_ref, x2t_ref, kron_ref, gram_ref,
           send_v0, send_v1, send_s0, send_s1, up_0, up_1, down_0, down_1, side_0, side_1,
           send_sem, recv_sem, load_sem):
    loads = [pltpu.make_async_copy(msg_hbm, msg_ref, load_sem.at[cols])]
    loads += [
        pltpu.make_async_copy(a_hbm.at[i], a_ref.at[i], load_sem.at[i]) for i in range(cols)
    ]
    for load in loads:
        load.start()
    tile = lax.axis_index("tile")
    group = lax.axis_index("group")
    DD = D * D
    shift = D.bit_length() - 1
    halves = DD // LANES
    mixed = 2 * halves
    sub = D // mixed
    per = LANES // D
    legs = 4 * cols
    crossing = jnp.where(group == 0, cols - 1, 0)
    closed = jnp.where(group == 0, 0, cols - 1)
    order = list(range(1, cols - 1)) + [closed, crossing]
    has_up = tile > 0
    has_down = tile < tiles - 1

    barrier = pltpu.get_barrier_semaphore()

    @pl.when(has_up)
    def _():
        pl.semaphore_signal(barrier, inc=1, device_id={"tile": tile - 1}, device_id_type=MESH)

    @pl.when(has_down)
    def _():
        pl.semaphore_signal(barrier, inc=1, device_id={"tile": tile + 1}, device_id_type=MESH)

    pl.semaphore_signal(barrier, inc=1, device_id={"group": 1 - group}, device_id_type=MESH)

    lane = iota((D, LANES), 1)
    row = iota((D, LANES), 0)
    within = lane & (D - 1)
    turned = lane - within + row
    slot = lane >> shift
    gather = unmixing(D, mixed, 0)
    fold_minor = one_hot((iota((LANES, LANES), 0) & (D - 1)) == (iota((LANES, LANES), 1) & (D - 1)))
    fold_major = one_hot((iota((DD, LANES), 0) >> shift) == (iota((DD, LANES), 1) & (D - 1)))

    def placed(entries):
        total = jnp.zeros((D, LANES), F32)
        for where, value in entries:
            total = jnp.where(slot == where, value, total)
        return total

    def by_major(value, m):
        return jnp.concatenate([pick(value, m * D + slot + h * per) for h in range(halves)], axis=1)

    def by_minor(value, m):
        return jnp.concatenate([pick(value, m * D + within)] * halves, axis=1)

    def rounded(value):
        return value.astype(BF16).astype(F32)

    def reduce_major(gram, weight):
        total = gram[:D] * weight[0:1, :]
        for d in range(1, D):
            total = total + gram[d * D : (d + 1) * D] * weight[d : d + 1, :]
        return total

    def reduce_minor(gram, weight):
        return jnp.concatenate(
            [
                jnp.sum(gram[d * D : (d + 1) * D] * weight, axis=0, keepdims=True)
                for d in range(D)
            ],
            axis=0,
        )

    def kinds_of(totals):
        if len(totals) == 1:
            return totals
        return [totals[0] + totals[1], totals[0] - totals[1]]

    def folded(totals, selector):
        pieces = []
        for total in totals:
            if selector is fold_minor:
                joined = total[:, :LANES]
                for h in range(1, halves):
                    joined = joined + total[:, h * LANES : (h + 1) * LANES]
                total = joined
            pieces += parts(total, 2)
        out = dot(jnp.concatenate(pieces, axis=0), selector)
        return [
            out[2 * n * D : (2 * n + 1) * D] + out[(2 * n + 1) * D : (2 * n + 2) * D]
            for n in range(len(totals))
        ]

    def minors(totals):
        count = len(totals[0])
        flat = folded([v for t in totals for v in t], fold_minor)
        return [flat[n * count : (n + 1) * count] for n in range(len(totals))]

    def majors(totals):
        count = len(totals[0])
        flat = folded([v for t in totals for v in t], fold_major)
        return [flat[n * count : (n + 1) * count] for n in range(len(totals))]

    def normalised(values):
        power = jnp.sum(values[0] * values[0], axis=0, keepdims=True)
        power = pick(jnp.broadcast_to(power, (D, LANES)), turned)
        power = jnp.sum(power, axis=0, keepdims=True) / DD
        scale = 1.0 / jnp.sqrt(power + EPSILON)
        return [v * scale for v in values]

    def upright(ups, downs, kind):
        return placed(
            [(i, ups[i][kind]) for i in range(cols)]
            + [(cols + i, downs[i][kind]) for i in range(cols)]
        )

    def copy(src, dst, turn, k, device):
        return pltpu.make_async_remote_copy(
            src_ref=src, dst_ref=dst, send_sem=send_sem.at[turn, k],
            recv_sem=recv_sem.at[turn, k], device_id=device, device_id_type=MESH,
        )

    def rows_copies(turn, src, up_dst, down_dst):
        to_up = copy(src, down_dst, turn, 0, {"tile": tile - 1})
        to_down = copy(src, up_dst, turn, 1, {"tile": tile + 1})

        @pl.when(has_up)
        def _():
            to_up.start()

        @pl.when(has_down)
        def _():
            to_down.start()

        return to_up, to_down

    def rows_arrive(copies, up_dst, down_dst, edges):
        to_up, to_down = copies

        @pl.when(has_up)
        def _():
            to_up.wait_send()
            to_down.wait_recv()

        @pl.when(jnp.logical_not(has_up))
        def _():
            up_dst[...] = edges

        @pl.when(has_down)
        def _():
            to_down.wait_send()
            to_up.wait_recv()

        @pl.when(jnp.logical_not(has_down))
        def _():
            down_dst[...] = edges

        above, below = up_dst[...], down_dst[...]
        return [
            jnp.where(slot < cols, above[k * D : (k + 1) * D], below[k * D : (k + 1) * D])
            for k in range(above.shape[0] // D)
        ]

    from_left = (slot == 0) | (slot == 2 * cols)
    from_right = (slot == 2 * cols - 1) | (slot == 2 * cols + 1)

    def sides_arrive(to_side, dst, local, edges):
        to_side.wait()
        got = dst[...]
        out = []
        for k, (value, edge) in enumerate(zip(local, edges)):
            other = got[k * D : (k + 1) * D]
            value = jnp.where(from_left, jnp.where(group == 0, edge, other), value)
            out.append(
                jnp.where(from_right, jnp.where(group == groups - 1, edge, other), value)
            )
        return out

    loads[0].wait()
    spot = (row & (per - 1)) * D + within
    flat = msg_ref[...].reshape(legs, DD)

    def unfolded(m):
        source = jnp.concatenate(
            [
                jnp.broadcast_to(flat[m : m + 1, h * LANES : (h + 1) * LANES], (per, LANES))
                for h in range(halves)
            ],
            axis=0,
        )
        return pick(source, spot)

    singles = [unfolded(m) for m in range(legs)]
    edge_rows = placed(
        [(i, singles[4 * i]) for i in range(cols)]
        + [(cols + i, singles[4 * i + 2]) for i in range(cols)]
    )
    edge_sides = placed(
        [(i, singles[4 * i + 1]) for i in range(cols)]
        + [(cols + i, singles[4 * i + 3]) for i in range(cols)]
    )

    def unmix(i):
        for b in range(0, mixed, 2):
            pair = jnp.concatenate(
                [
                    jnp.concatenate(
                        [
                            a_ref[i, u * D * mixed + (b + c) * D : u * D * mixed + (b + c + 1) * D]
                            for u in range(D)
                        ],
                        axis=0,
                    )
                    for c in range(2)
                ],
                axis=1,
            )
            block = dot(gather, pair).astype(BF16)
            span = sub * D
            for c in range(2):
                for g in range(mixed):
                    x_ref[
                        i,
                        g % 2,
                        (b + c) * span : (b + c + 1) * span,
                        (g // 2) * LANES : (g // 2 + 1) * LANES,
                    ] = block[g * span : (g + 1) * span, c * LANES : (c + 1) * LANES]
        for s in range(2):
            xt_ref[i, s] = x_ref[i, s].T

    def relayout(i, s):
        for h in range(halves):
            for lh in range(halves):
                values = [
                    x_ref[
                        i, s, (lh * per + k) * D : (lh * per + k + 1) * D,
                        h * LANES : (h + 1) * LANES,
                    ]
                    for k in range(per)
                ]
                step = 1
                while step < per:
                    high = (slot & step) != 0
                    out = list(values)
                    for a in range(per):
                        if a & step:
                            continue
                        b = a | step
                        low_up = pltpu.roll(values[b], D * step, 1)
                        high_down = pltpu.roll(values[a], LANES - D * step, 1)
                        out[a] = jnp.where(high, low_up, values[a])
                        out[b] = jnp.where(high, values[b], high_down)
                    values = out
                    step *= 2
                for d in range(per):
                    x2_ref[
                        i, s, (h * per + d) * D : (h * per + d + 1) * D,
                        lh * LANES : (lh + 1) * LANES,
                    ] = values[d]
        x2t_ref[i, s] = x2_ref[i, s].T

    v_rows, v_sides = rounded(edge_rows), rounded(edge_sides)
    ups, downs = [], []
    weights = []
    for i in range(cols):
        loads[1 + i].wait()
        unmix(i)
        w_up, w_down = by_minor(v_rows, i), by_major(v_rows, cols + i)
        w_left, w_right = by_major(v_sides, i), by_minor(v_sides, cols + i)
        weights.append((w_up, w_down))
        build_kron(kron_ref, 2 * i, w_down, w_right)
        build_kron(kron_ref, 2 * i + 1, w_left, w_up)
        for path, (left, right) in enumerate(((x_ref, xt_ref), (xt_ref, x_ref))):
            y = [dot(left[i, s], kron_ref[2 * i + path]).astype(BF16) for s in range(2)]
            gram_ref[2 * i + path, 0] = dot(y[0], right[i, 0]) + dot(y[1], right[i, 1])
        ups.append([reduce_major(gram_ref[2 * i, 0], w_left)])
        downs.append([reduce_minor(gram_ref[2 * i + 1, 0], w_right)])
    ups, downs = minors(ups), majors(downs)
    send_v0[...] = normalised([upright(downs, ups, 0)])[0]

    inside = jnp.logical_and(has_up, has_down)

    @pl.when(inside)
    def _():
        pl.semaphore_wait(barrier, 3)

    @pl.when(jnp.logical_not(inside))
    def _():
        pl.semaphore_wait(barrier, 2)

    rows_0 = rows_copies(0, send_v0, up_0, down_0)

    lefts = majors([[reduce_minor(gram_ref[2 * i, 0], weights[i][0])] for i in range(cols)])
    rights = minors([[reduce_major(gram_ref[2 * i + 1, 0], weights[i][1])] for i in range(cols)])
    send_s0[...] = normalised([jnp.where(from_left, rights[cols - 1][0], lefts[0][0])])[0]
    sides_0 = copy(send_s0, side_0, 0, 2, {"group": 1 - group})
    sides_0.start()

    def inner_view(lefts, rights, kind):
        return placed(
            [(i, rights[i - 1][kind]) for i in range(1, cols)]
            + [(cols + i, lefts[i + 1][kind]) for i in range(cols - 1)]
        )

    n_sides = normalised([inner_view(lefts, rights, 0)])
    for i in range(cols):
        for s in range(2):
            relayout(i, s)
    for i in range(cols):
        a0, a1 = x_ref[i, 0].astype(F32), x_ref[i, 1].astype(F32)
        ch, sh = math.cosh(FIELD), math.sinh(FIELD)
        ax_ref[i, 0] = (ch * a0 + sh * a1).astype(BF16)
        ax_ref[i, 1] = (ch * a1 + sh * a0).astype(BF16)

    side_weights = []

    def paired(j, kron, left, right, at):
        i = order[j]
        for s in range(2):
            y = dot(left[i, s], kron_ref[kron]).astype(BF16)
            gram_ref[at, s] = dot(y, right[i, s])

    for j in range(cols):
        if j == cols - 1:
            n_sides = sides_arrive(sides_0, side_0, n_sides, [edge_sides])
        v_sides = rounded(n_sides[0]) if j == cols - 1 else rounded(jnp.where(
            from_left | from_right, edge_sides, n_sides[0]
        ))
        i = order[j]
        w_left, w_right = by_major(v_sides, i), by_minor(v_sides, cols + i)
        side_weights.append((w_left, w_right))
        build_kron(kron_ref, 2 * j, w_left, w_right)
        paired(j, 2 * j, x2_ref, x2t_ref, 2 * j)

    n_rows = rows_arrive(rows_0, up_0, down_0, edge_rows)
    v_rows = rounded(n_rows[0])
    ups, downs, weights = [], [], []
    for j in range(cols):
        i = order[j]
        w_up, w_down = by_minor(v_rows, i), by_major(v_rows, cols + i)
        weights.append((w_up, w_down))
        ups.append(kinds_of([reduce_major(gram_ref[2 * j, s], w_down) for s in range(2)]))
        downs.append(kinds_of([reduce_minor(gram_ref[2 * j, s], w_up) for s in range(2)]))
    ups, downs = minors(ups), majors(downs)

    def ordered(above, below, kind):
        return placed(
            [(order[j], above[j][kind]) for j in range(cols)]
            + [(cols + order[j], below[j][kind]) for j in range(cols)]
        )

    out_rows = normalised([ordered(downs, ups, k) for k in range(2)])
    for k in range(2):
        send_v1[k * D : (k + 1) * D] = out_rows[k]
    rows_1 = rows_copies(1, send_v1, up_1, down_1)
    o_rows = normalised([ordered(ups, downs, k) for k in range(2)])

    def horizontal(j):
        build_kron(kron_ref, 2 * j + 1, weights[j][1], weights[j][0])
        paired(j, 2 * j + 1, x2t_ref, x2_ref, 2 * j + 1)
        w_left, w_right = side_weights[j]
        left = kinds_of([reduce_minor(gram_ref[2 * j + 1, s], w_right) for s in range(2)])
        right = kinds_of([reduce_major(gram_ref[2 * j + 1, s], w_left) for s in range(2)])
        return left, right

    left, right = horizontal(cols - 1)
    (left,), (right,) = majors([left]), minors([right])
    out_sides = normalised([jnp.where(from_left, right[k], left[k]) for k in range(2)])
    for k in range(2):
        send_s1[k * D : (k + 1) * D] = out_sides[k]
    sides_1 = copy(send_s1, side_1, 1, 2, {"group": 1 - group})
    sides_1.start()
    others = [horizontal(j) for j in range(cols - 1)]
    lefts = majors([o[0] for o in others]) + [left]
    rights = minors([o[1] for o in others]) + [right]

    def own_sides(kind):
        base = placed(
            [(order[j], lefts[j][kind]) for j in range(cols)]
            + [(cols + order[j], rights[j][kind]) for j in range(cols)]
        )
        base = jnp.where((slot == 2 * cols) & (group == groups - 1), lefts[-1][kind], base)
        return jnp.where((slot == 2 * cols + 1) & (group == 0), rights[-1][kind], base)

    def other_sides(kind):
        entries = []
        for j, i in enumerate(order):
            entries.append((jnp.where(i == 0, -1, cols + i - 1), lefts[j][kind]))
            entries.append((jnp.where(i == cols - 1, -1, i + 1), rights[j][kind]))
        return placed(entries)

    o_sides = normalised([own_sides(k) for k in range(2)])
    n_sides = normalised([other_sides(k) for k in range(2)])
    for s, weight in enumerate(bond_weights(*[o + n for o, n in zip(o_sides, n_sides)])):
        inner_ref[s] = rounded(weight)
    zero = jnp.zeros((D, LANES), F32)
    n_sides = sides_arrive(sides_1, side_1, n_sides, [edge_sides, zero])
    n_rows = rows_arrive(rows_1, up_1, down_1, jnp.concatenate([edge_rows, zero], axis=0))
    for k in range(2):
        env_ref[k] = jnp.where(
            slot < 2 * cols, o_rows[k] + n_rows[k], o_sides[k] + n_sides[k]
        )
    mout_ref[0] = n_rows[0]
    mout_ref[1] = n_sides[0]


def gates_kernel(tiles, groups, cols, D, ax_ref, env_ref, inner_ref, in_ref, out_hbm, mout_hbm,
                 kron_ref, out_ref, mout_ref, store_sem):
    tile = lax.axis_index("tile")
    group = lax.axis_index("group")
    DD = D * D
    shift = D.bit_length() - 1
    halves = DD // LANES
    mixed = 2 * halves
    rows = DD // mixed
    lane = iota((D, LANES), 1)
    row = iota((D, LANES), 0)
    inner = lane & (D - 1)
    start = lane - inner
    slot = lane >> shift

    unit = jnp.where(inner == row, 1.0, 0.0).astype(F32)
    at_edge = (
        ((slot < cols) & (tile == 0))
        | ((slot >= cols) & (slot < 2 * cols) & (tile == tiles - 1))
        | ((slot == 2 * cols) & (group == 0))
        | ((slot == 2 * cols + 1) & (group == groups - 1))
    )
    late = [
        jnp.where(at_edge, unit, w).astype(BF16).astype(F32)
        for w in bond_weights(env_ref[0], env_ref[1])
    ]
    early = [inner_ref[s] for s in range(2)]

    unfold_mask = slot == (row & (LANES // D - 1))
    flat_rows = []
    for m in range(4 * cols):
        at = m // 4 + (cols if m % 4 >= 2 else 0)
        tiled = jnp.where(unfold_mask, pick(in_ref[m % 2], inner + at * D), 0.0)
        step = D // halves
        flat_rows.append(
            jnp.concatenate(
                [
                    jnp.sum(tiled[h * step : (h + 1) * step], axis=0, keepdims=True)
                    for h in range(halves)
                ],
                axis=1,
            )
        )
    mout_ref[...] = jnp.concatenate(flat_rows, axis=0).reshape(cols, 4, DD)
    store_msg = pltpu.make_async_copy(mout_ref, mout_hbm, store_sem.at[cols])
    store_msg.start()

    def by_major(value, m):
        return jnp.concatenate(
            [pick(value, m * D + slot + h * (LANES // D)) for h in range(halves)], axis=1
        )

    def by_minor(value, m):
        part = pick(value, m * D + inner)
        return jnp.concatenate([part] * halves, axis=1)

    scatter = unmixing(D, mixed, 1)
    stores = [
        pltpu.make_async_copy(out_ref.at[i], out_hbm.at[i], store_sem.at[i]) for i in range(cols)
    ]

    def gate(i):
        gated = []
        for s in range(2):
            left = by_major(late[s], 2 * cols) if i == 0 else by_major(early[s], i)
            right = (
                by_minor(late[s], 2 * cols + 1) if i == cols - 1 else by_minor(early[s], i + 1)
            )
            at = (i * 2 + s) * 2
            build_kron(kron_ref, at, by_major(late[s], cols + i), right)
            build_kron(kron_ref, at + 1, left, by_minor(late[s], i))
            half = dot_nt(ax_ref[i, s], kron_ref[at]).astype(BF16)
            gated.append(dot(kron_ref[at + 1], half).astype(BF16))
        return gated

    def emit(i, gated):
        for b in range(0, mixed, 2):
            block = jnp.concatenate(
                [
                    jnp.concatenate(
                        [
                            gated[g % 2][
                                (b + c) * rows : (b + c + 1) * rows,
                                (g // 2) * LANES : (g // 2 + 1) * LANES,
                            ]
                            for c in range(2)
                        ],
                        axis=1,
                    )
                    for g in range(mixed)
                ],
                axis=0,
            )
            done = dot(scatter, block).astype(BF16)
            for c in range(2):
                for u in range(D):
                    at = u * D * mixed + (b + c) * D
                    out_ref[i, at : at + D, :] = done[
                        u * D : (u + 1) * D, c * LANES : (c + 1) * LANES
                    ]
        stores[i].start()

    waiting = gate(0)
    for i in range(cols):
        following = gate(i + 1) if i + 1 < cols else None
        emit(i, waiting)
        waiting = following
    for store in stores + [store_msg]:
        store.wait()


def per_device(tiles, groups, site_tensors, msg_in):
    _, cols, _, size = site_tensors.shape
    DD = msg_in.shape[-1]
    D = math.isqrt(DD)
    chunks = size // LANES
    a = site_tensors.reshape(cols, 2, chunks, LANES).transpose(0, 2, 1, 3)
    a = a.reshape(cols, 2 * chunks, LANES)
    vmem = pl.BlockSpec(memory_space=pltpu.VMEM)
    hbm = pl.BlockSpec(memory_space=pltpu.HBM)
    gated, env, inner, stacked = pl.pallas_call(
        functools.partial(messages_kernel, tiles, groups, cols, D),
        out_shape=(
            jax.ShapeDtypeStruct((cols, 2, DD, DD), BF16),
            jax.ShapeDtypeStruct((2, D, LANES), F32),
            jax.ShapeDtypeStruct((2, D, LANES), F32),
            jax.ShapeDtypeStruct((2, D, LANES), F32),
        ),
        in_specs=[hbm, hbm],
        out_specs=(vmem, vmem, vmem, vmem),
        scratch_shapes=[
            pltpu.VMEM(a.shape, BF16),
            pltpu.VMEM((cols, 4, DD), F32),
            pltpu.VMEM((cols, 2, DD, DD), BF16),
            pltpu.VMEM((cols, 2, DD, DD), BF16),
            pltpu.VMEM((cols, 2, DD, DD), BF16),
            pltpu.VMEM((cols, 2, DD, DD), BF16),
            pltpu.VMEM((2 * cols, DD, DD), BF16),
            pltpu.VMEM((2 * cols, 2, DD, DD), F32),
        ]
        + [
            pltpu.VMEM(((1 + turn) * D, LANES), F32) for _ in range(5) for turn in range(ITERS)
        ]
        + [
            pltpu.SemaphoreType.DMA((ITERS, 3)),
            pltpu.SemaphoreType.DMA((ITERS, 3)),
            pltpu.SemaphoreType.DMA((cols + 1,)),
        ],
        compiler_params=pltpu.CompilerParams(
            collective_id=0, has_side_effects=True, vmem_limit_bytes=24 * 2**20
        ),
    )(
        pltpu.with_memory_space_constraint(a, pltpu.HBM),
        pltpu.with_memory_space_constraint(msg_in[0], pltpu.HBM),
    )
    out, messages = pl.pallas_call(
        functools.partial(gates_kernel, tiles, groups, cols, D),
        out_shape=(
            jax.ShapeDtypeStruct(a.shape, BF16),
            jax.ShapeDtypeStruct((cols, 4, DD), F32),
        ),
        in_specs=[vmem, vmem, vmem, vmem],
        out_specs=(hbm, hbm),
        scratch_shapes=[
            pltpu.VMEM((4 * cols, DD, DD), BF16),
            pltpu.VMEM(a.shape, BF16),
            pltpu.VMEM((cols, 4, DD), F32),
            pltpu.SemaphoreType.DMA((cols + 1,)),
        ],
        compiler_params=pltpu.CompilerParams(vmem_limit_bytes=24 * 2**20),
    )(gated, env, inner, stacked)
    out = out.reshape(cols, chunks, 2, LANES).transpose(0, 2, 1, 3)
    return out.reshape(1, cols, 2, size), messages[None]


def solution(mesh):
    spec = P("tile", "group", None, None)
    return jax.shard_map(
        functools.partial(per_device, mesh.shape["tile"], mesh.shape["group"]),
        mesh=mesh, in_specs=(spec, spec), out_specs=(spec, spec), check_vma=False,
    )
```

```python
import functools
import math

import jax
import jax.numpy as jnp
from jax import lax
from jax.experimental import pallas as pl
from jax.experimental.pallas import tpu as pltpu
from jax.sharding import PartitionSpec as P

ITERS = 2
NS_STEPS = 6
LANES = 128
EPSILON = 1e-06
COUPLING = 0.5
FIELD = 0.3
F32 = jnp.float32
BF16 = jnp.bfloat16
MESH = pl.DeviceIdType.MESH


def iota(shape, axis):
    return lax.broadcasted_iota(jnp.int32, shape, axis)


def dot(a, b):
    return jnp.dot(a, b, preferred_element_type=F32)


def dot_nt(a, b):
    return lax.dot_general(a, b, (((1,), (1,)), ((), ())), preferred_element_type=F32)


def dot_tn(a, b):
    return lax.dot_general(a, b, (((0,), (0,)), ((), ())), preferred_element_type=F32)


def parts(value, count):
    out = []
    for _ in range(count):
        piece = value.astype(BF16)
        out.append(piece)
        value = value - piece.astype(F32)
    return out


def select_dot(value, selector, count):
    total = None
    for piece in parts(value, count):
        term = dot(piece, selector)
        total = term if total is None else total + term
    return total


def one_hot(mask):
    return jnp.where(mask, 1.0, 0.0).astype(BF16)


def build_kron(kron_ref, slot, first, second):
    D = first.shape[0]
    for d in range(D):
        kron_ref[slot, d * D : (d + 1) * D, :] = (first[d : d + 1, :] * second).astype(BF16)


def pick(value, index):
    return jnp.take_along_axis(value, index, axis=1, mode="promise_in_bounds")


def row_of(value, k):
    return jnp.broadcast_to(value[k : k + 1, :], value.shape)


def bond_weights(msg_sum, twist_sum):
    D = msg_sum.shape[0]
    lane = iota((D, LANES), 1)
    row = iota((D, LANES), 0)
    inner = lane & (D - 1)
    start = lane - inner
    turned = start + row
    unit = jnp.where(inner == row, 1.0, 0.0).astype(F32)
    g0, g1 = math.cosh(COUPLING), math.sinh(COUPLING)
    cross = math.sqrt(g0 * g1)
    root2 = math.sqrt(2.0)
    halves = [
        ((g0 * msg_sum + cross * twist_sum) / root2).astype(BF16).astype(F32),
        ((cross * twist_sum + g1 * msg_sum) / root2).astype(BF16).astype(F32),
    ]
    squares = halves[0] * halves[0] + halves[1] * halves[1]
    squares = jnp.broadcast_to(jnp.sum(squares, axis=0, keepdims=True), (D, LANES))
    trace = jnp.sum(pick(squares, turned), axis=0, keepdims=True) + EPSILON

    gram = None
    rotated = []
    for half in halves:
        transposed = None
        for k in range(D):
            own = row_of(half, k)
            column = pick(own, turned)
            term = column * own
            gram = term if gram is None else gram + term
            placed = jnp.where(inner == k, column, 0.0)
            transposed = placed if transposed is None else transposed + placed
        rotated.append(transposed)

    def columns(value):
        return [pick(row_of(value, k), turned) for k in range(D)]

    def times(left, right):
        sums = [None] * 4
        for k in range(D):
            term = left[k] * row_of(right, k)
            sums[k % 4] = term if sums[k % 4] is None else sums[k % 4] + term
        return (sums[0] + sums[1]) + (sums[2] + sums[3])

    state = gram / trace
    for step in range(NS_STEPS - 2):
        left = columns(state)
        square = times(left, state)
        rotated = [1.5 * v - 0.5 * times(left, v) for v in rotated]
        state = times(left, 2.25 * unit - 1.5 * state + 0.25 * square)
    left = columns(state)
    rotated = [1.5 * v - 0.5 * times(left, v) for v in rotated]
    again = rotated
    for _ in range(2):
        again = [1.5 * v - 0.5 * times(left, v) for v in again]
    rotated = [1.5 * v - 0.5 * times(left, w) for v, w in zip(rotated, again)]
    scale = 1.0 / jnp.sqrt(trace)
    first = math.sqrt(g0) * rotated[0] * scale
    second = math.sqrt(g1) * rotated[1] * scale
    return [first + second, first - second]


def unmixing(D, mixed, out_axis):
    DD = D * D
    sub = D // mixed
    p, k = iota((DD, DD), out_axis), iota((DD, DD), 1 - out_axis)
    low = p & (D - 1)
    mid = (p >> (D.bit_length() - 1)) & (sub - 1)
    top = p >> (D * sub).bit_length() - 1
    return one_hot(k == low * D + mid * mixed + top)


def messages_kernel(tiles, groups, cols, D, a_hbm, msg_hbm, ax_ref, env_ref, inner_ref, mout_ref,
           a_ref, msg_ref, x_ref, xt_ref, x2_ref, x2t_ref, kron_ref, gram_ref,
           send_v0, send_v1, send_s0, send_s1, up_0, up_1, down_0, down_1, side_0, side_1,
           send_sem, recv_sem, load_sem):
    loads = [pltpu.make_async_copy(msg_hbm, msg_ref, load_sem.at[cols])]
    loads += [
        pltpu.make_async_copy(a_hbm.at[i], a_ref.at[i], load_sem.at[i]) for i in range(cols)
    ]
    for load in loads:
        load.start()
    tile = lax.axis_index("tile")
    group = lax.axis_index("group")
    DD = D * D
    shift = D.bit_length() - 1
    halves = DD // LANES
    mixed = 2 * halves
    sub = D // mixed
    per = LANES // D
    legs = 4 * cols
    crossing = jnp.where(group == 0, cols - 1, 0)
    closed = jnp.where(group == 0, 0, cols - 1)
    order = list(range(1, cols - 1)) + [closed, crossing]
    has_up = tile > 0
    has_down = tile < tiles - 1

    barrier = pltpu.get_barrier_semaphore()

    @pl.when(has_up)
    def _():
        pl.semaphore_signal(barrier, inc=1, device_id={"tile": tile - 1}, device_id_type=MESH)

    @pl.when(has_down)
    def _():
        pl.semaphore_signal(barrier, inc=1, device_id={"tile": tile + 1}, device_id_type=MESH)

    pl.semaphore_signal(barrier, inc=1, device_id={"group": 1 - group}, device_id_type=MESH)

    lane = iota((D, LANES), 1)
    row = iota((D, LANES), 0)
    within = lane & (D - 1)
    turned = lane - within + row
    slot = lane >> shift
    gather = unmixing(D, mixed, 0)
    fold_minor = one_hot((iota((LANES, LANES), 0) & (D - 1)) == (iota((LANES, LANES), 1) & (D - 1)))
    fold_major = one_hot((iota((DD, LANES), 0) >> shift) == (iota((DD, LANES), 1) & (D - 1)))

    def placed(entries):
        total = jnp.zeros((D, LANES), F32)
        for where, value in entries:
            total = jnp.where(slot == where, value, total)
        return total

    def by_major(value, m):
        return jnp.concatenate([pick(value, m * D + slot + h * per) for h in range(halves)], axis=1)

    def by_minor(value, m):
        return jnp.concatenate([pick(value, m * D + within)] * halves, axis=1)

    def rounded(value):
        return value.astype(BF16).astype(F32)

    def reduce_major(gram, weight):
        total = gram[:D] * weight[0:1, :]
        for d in range(1, D):
            total = total + gram[d * D : (d + 1) * D] * weight[d : d + 1, :]
        return total

    sublane = iota((8, DD), 0)

    def reduce_minor(gram, weight):
        blocks = []
        for d in range(D):
            block = gram[d * D : (d + 1) * D] * weight
            total = block[:8]
            for h in range(1, D // 8):
                total = total + block[h * 8 : (h + 1) * 8]
            blocks.append(total)
        out = []
        for base in range(0, D, 8):
            level = blocks[base : base + 8]
            step = 1
            while len(level) > 1:
                low = (sublane & step) == 0
                level = [
                    jnp.where(low, level[n], level[n + 1])
                    + pltpu.roll(jnp.where(low, level[n + 1], level[n]), step, 0)
                    for n in range(0, len(level), 2)
                ]
                step *= 2
            out.append(level[0])
        return jnp.concatenate(out, axis=0)

    def kinds_of(totals):
        if len(totals) == 1:
            return totals
        return [totals[0] + totals[1], totals[0] - totals[1]]

    def folded(totals, selector):
        pieces = []
        for total in totals:
            if selector is fold_minor:
                joined = total[:, :LANES]
                for h in range(1, halves):
                    joined = joined + total[:, h * LANES : (h + 1) * LANES]
                total = joined
            pieces += parts(total, 2)
        out = dot(jnp.concatenate(pieces, axis=0), selector)
        return [
            out[2 * n * D : (2 * n + 1) * D] + out[(2 * n + 1) * D : (2 * n + 2) * D]
            for n in range(len(totals))
        ]

    def minors(totals):
        count = len(totals[0])
        flat = folded([v for t in totals for v in t], fold_minor)
        return [flat[n * count : (n + 1) * count] for n in range(len(totals))]

    def majors(totals):
        count = len(totals[0])
        flat = folded([v for t in totals for v in t], fold_major)
        return [flat[n * count : (n + 1) * count] for n in range(len(totals))]

    def normalised(values):
        power = jnp.sum(values[0] * values[0], axis=0, keepdims=True)
        power = pick(jnp.broadcast_to(power, (D, LANES)), turned)
        power = jnp.sum(power, axis=0, keepdims=True) / DD
        scale = 1.0 / jnp.sqrt(power + EPSILON)
        return [v * scale for v in values]

    def upright(ups, downs, kind):
        return placed(
            [(i, ups[i][kind]) for i in range(cols)]
            + [(cols + i, downs[i][kind]) for i in range(cols)]
        )

    def copy(src, dst, turn, k, device):
        return pltpu.make_async_remote_copy(
            src_ref=src, dst_ref=dst, send_sem=send_sem.at[turn, k],
            recv_sem=recv_sem.at[turn, k], device_id=device, device_id_type=MESH,
        )

    def rows_copies(turn, src, up_dst, down_dst):
        to_up = copy(src, down_dst, turn, 0, {"tile": tile - 1})
        to_down = copy(src, up_dst, turn, 1, {"tile": tile + 1})

        @pl.when(has_up)
        def _():
            to_up.start()

        @pl.when(has_down)
        def _():
            to_down.start()

        return to_up, to_down

    def rows_arrive(copies, up_dst, down_dst, edges):
        to_up, to_down = copies

        @pl.when(has_up)
        def _():
            to_up.wait_send()
            to_down.wait_recv()

        @pl.when(jnp.logical_not(has_up))
        def _():
            up_dst[...] = edges

        @pl.when(has_down)
        def _():
            to_down.wait_send()
            to_up.wait_recv()

        @pl.when(jnp.logical_not(has_down))
        def _():
            down_dst[...] = edges

        above, below = up_dst[...], down_dst[...]
        return [
            jnp.where(slot < cols, above[k * D : (k + 1) * D], below[k * D : (k + 1) * D])
            for k in range(above.shape[0] // D)
        ]

    from_left = (slot == 0) | (slot == 2 * cols)
    from_right = (slot == 2 * cols - 1) | (slot == 2 * cols + 1)

    def sides_arrive(to_side, dst, local, edges):
        to_side.wait()
        got = dst[...]
        out = []
        for k, (value, edge) in enumerate(zip(local, edges)):
            other = got[k * D : (k + 1) * D]
            value = jnp.where(from_left, jnp.where(group == 0, edge, other), value)
            out.append(
                jnp.where(from_right, jnp.where(group == groups - 1, edge, other), value)
            )
        return out

    loads[0].wait()
    spot = (row & (per - 1)) * D + within
    flat = msg_ref[...].reshape(legs, DD)

    def unfolded(m):
        source = jnp.concatenate(
            [
                jnp.broadcast_to(flat[m : m + 1, h * LANES : (h + 1) * LANES], (per, LANES))
                for h in range(halves)
            ],
            axis=0,
        )
        return pick(source, spot)

    singles = [unfolded(m) for m in range(legs)]
    edge_rows = placed(
        [(i, singles[4 * i]) for i in range(cols)]
        + [(cols + i, singles[4 * i + 2]) for i in range(cols)]
    )
    edge_sides = placed(
        [(i, singles[4 * i + 1]) for i in range(cols)]
        + [(cols + i, singles[4 * i + 3]) for i in range(cols)]
    )

    def unmix(i):
        for b in range(0, mixed, 2):
            pair = jnp.concatenate(
                [
                    jnp.concatenate(
                        [
                            a_ref[i, u * D * mixed + (b + c) * D : u * D * mixed + (b + c + 1) * D]
                            for u in range(D)
                        ],
                        axis=0,
                    )
                    for c in range(2)
                ],
                axis=1,
            )
            block = dot(gather, pair).astype(BF16)
            span = sub * D
            for c in range(2):
                for g in range(mixed):
                    x_ref[
                        i,
                        g % 2,
                        (b + c) * span : (b + c + 1) * span,
                        (g // 2) * LANES : (g // 2 + 1) * LANES,
                    ] = block[g * span : (g + 1) * span, c * LANES : (c + 1) * LANES]

    def relayout(i, s):
        for h in range(halves):
            for lh in range(halves):
                values = [
                    x_ref[
                        i, s, (lh * per + k) * D : (lh * per + k + 1) * D,
                        h * LANES : (h + 1) * LANES,
                    ]
                    for k in range(per)
                ]
                step = 1
                while step < per:
                    high = (slot & step) != 0
                    out = list(values)
                    for a in range(per):
                        if a & step:
                            continue
                        b = a | step
                        low_up = pltpu.roll(values[b], D * step, 1)
                        high_down = pltpu.roll(values[a], LANES - D * step, 1)
                        out[a] = jnp.where(high, low_up, values[a])
                        out[b] = jnp.where(high, values[b], high_down)
                    values = out
                    step *= 2
                for d in range(per):
                    x2_ref[
                        i, s, (h * per + d) * D : (h * per + d + 1) * D,
                        lh * LANES : (lh + 1) * LANES,
                    ] = values[d]
        x2t_ref[i, s] = x2_ref[i, s].T

    v_rows, v_sides = rounded(edge_rows), rounded(edge_sides)
    weights = []
    for i in range(cols):
        w_up, w_down = by_minor(v_rows, i), by_major(v_rows, cols + i)
        w_left, w_right = by_major(v_sides, i), by_minor(v_sides, cols + i)
        weights.append((w_up, w_down, w_left, w_right))
        build_kron(kron_ref, 2 * i, w_down, w_right)
        build_kron(kron_ref, 2 * i + 1, w_left, w_up)
    for load in loads[1:]:
        load.wait()
    for i in range(cols):
        unmix(i)
    for i in range(cols):
        for s in range(2):
            xt_ref[i, s] = x_ref[i, s].T
    sides_of = ((x_ref, xt_ref), (xt_ref, x_ref))
    for path, (left, right) in enumerate(sides_of):
        for i in range(cols):
            y = [dot(left[i, s], kron_ref[2 * i + path]).astype(BF16) for s in range(2)]
            gram_ref[2 * i + path, 0] = dot(
                jnp.concatenate(y, axis=1), right[i].reshape(2 * DD, DD)
            )

    def outer(i, leg):
        w_up, w_down, w_left, w_right = weights[i]
        if leg == 0:
            return [reduce_major(gram_ref[2 * i, 0], w_left)]
        if leg == 1:
            return [reduce_minor(gram_ref[2 * i, 0], w_up)]
        if leg == 2:
            return [reduce_minor(gram_ref[2 * i + 1, 0], w_right)]
        return [reduce_major(gram_ref[2 * i + 1, 0], w_down)]

    first_minors = minors([outer(i, 0) for i in range(cols)] + [outer(cols - 1, 3)])
    first_majors = majors([outer(i, 2) for i in range(cols)] + [outer(0, 1)])
    ups, right_last = first_minors[:cols], first_minors[cols]
    downs, left_first = first_majors[:cols], first_majors[cols]
    send_v0[...] = normalised([upright(downs, ups, 0)])[0]
    send_s0[...] = normalised([jnp.where(from_left, right_last[0], left_first[0])])[0]

    inside = jnp.logical_and(has_up, has_down)

    @pl.when(inside)
    def _():
        pl.semaphore_wait(barrier, 3)

    @pl.when(jnp.logical_not(inside))
    def _():
        pl.semaphore_wait(barrier, 2)

    rows_0 = rows_copies(0, send_v0, up_0, down_0)
    sides_0 = copy(send_s0, side_0, 0, 2, {"group": 1 - group})
    sides_0.start()

    for i in range(cols):
        for s in range(2):
            relayout(i, s)

    lefts = [left_first] + majors([outer(i, 1) for i in range(1, cols)])
    rights = minors([outer(i, 3) for i in range(cols - 1)]) + [right_last]

    def inner_view(lefts, rights, kind):
        return placed(
            [(i, rights[i - 1][kind]) for i in range(1, cols)]
            + [(cols + i, lefts[i + 1][kind]) for i in range(cols - 1)]
        )

    n_sides = normalised([inner_view(lefts, rights, 0)])

    side_weights = []

    def paired(j, kron, left, right, at):
        i = order[j]
        for s in range(2):
            y = dot(left[i, s], kron_ref[kron]).astype(BF16)
            gram_ref[at, s] = dot(y, right[i, s])

    for j in range(cols):
        if j == cols - 1:
            n_sides = sides_arrive(sides_0, side_0, n_sides, [edge_sides])
        v_sides = rounded(n_sides[0]) if j == cols - 1 else rounded(jnp.where(
            from_left | from_right, edge_sides, n_sides[0]
        ))
        i = order[j]
        w_left, w_right = by_major(v_sides, i), by_minor(v_sides, cols + i)
        side_weights.append((w_left, w_right))
        build_kron(kron_ref, 2 * j, w_left, w_right)
        paired(j, 2 * j, x2_ref, x2t_ref, 2 * j)

    mix = jnp.full((D, DD), math.tanh(FIELD), BF16)
    for i in range(cols):
        for d in range(0, DD, D):
            a0, a1 = (x_ref[i, s, d : d + D] for s in range(2))
            ax_ref[i, 0, d : d + D] = a0 + mix * a1
            ax_ref[i, 1, d : d + D] = a1 + mix * a0

    n_rows = rows_arrive(rows_0, up_0, down_0, edge_rows)
    v_rows = rounded(n_rows[0])
    ups, downs, weights = [], [], []
    for j in range(cols):
        i = order[j]
        w_up, w_down = by_minor(v_rows, i), by_major(v_rows, cols + i)
        weights.append((w_up, w_down))
        ups.append(kinds_of([reduce_major(gram_ref[2 * j, s], w_down) for s in range(2)]))
        downs.append(kinds_of([reduce_minor(gram_ref[2 * j, s], w_up) for s in range(2)]))
    ups, downs = minors(ups), majors(downs)

    def ordered(above, below, kind):
        return placed(
            [(order[j], above[j][kind]) for j in range(cols)]
            + [(cols + order[j], below[j][kind]) for j in range(cols)]
        )

    out_rows = normalised([ordered(downs, ups, k) for k in range(2)])
    for k in range(2):
        send_v1[k * D : (k + 1) * D] = out_rows[k]
    rows_1 = rows_copies(1, send_v1, up_1, down_1)
    o_rows = normalised([ordered(ups, downs, k) for k in range(2)])

    def horizontal(j):
        build_kron(kron_ref, 2 * j + 1, weights[j][1], weights[j][0])
        paired(j, 2 * j + 1, x2t_ref, x2_ref, 2 * j + 1)
        w_left, w_right = side_weights[j]
        left = kinds_of([reduce_minor(gram_ref[2 * j + 1, s], w_right) for s in range(2)])
        right = kinds_of([reduce_major(gram_ref[2 * j + 1, s], w_left) for s in range(2)])
        return left, right

    left, right = horizontal(cols - 1)
    (left,), (right,) = majors([left]), minors([right])
    out_sides = normalised([jnp.where(from_left, right[k], left[k]) for k in range(2)])
    for k in range(2):
        send_s1[k * D : (k + 1) * D] = out_sides[k]
    sides_1 = copy(send_s1, side_1, 1, 2, {"group": 1 - group})
    sides_1.start()
    others = [horizontal(j) for j in range(cols - 1)]
    lefts = majors([o[0] for o in others]) + [left]
    rights = minors([o[1] for o in others]) + [right]

    def own_sides(kind):
        base = placed(
            [(order[j], lefts[j][kind]) for j in range(cols)]
            + [(cols + order[j], rights[j][kind]) for j in range(cols)]
        )
        base = jnp.where((slot == 2 * cols) & (group == groups - 1), lefts[-1][kind], base)
        return jnp.where((slot == 2 * cols + 1) & (group == 0), rights[-1][kind], base)

    def other_sides(kind):
        entries = []
        for j, i in enumerate(order):
            entries.append((jnp.where(i == 0, -1, cols + i - 1), lefts[j][kind]))
            entries.append((jnp.where(i == cols - 1, -1, i + 1), rights[j][kind]))
        return placed(entries)

    o_sides = normalised([own_sides(k) for k in range(2)])
    n_sides = normalised([other_sides(k) for k in range(2)])
    for s, weight in enumerate(bond_weights(*[o + n for o, n in zip(o_sides, n_sides)])):
        inner_ref[s] = rounded(weight)
    zero = jnp.zeros((D, LANES), F32)
    n_sides = sides_arrive(sides_1, side_1, n_sides, [edge_sides, zero])
    n_rows = rows_arrive(rows_1, up_1, down_1, jnp.concatenate([edge_rows, zero], axis=0))
    for k in range(2):
        env_ref[k] = jnp.where(
            slot < 2 * cols, o_rows[k] + n_rows[k], o_sides[k] + n_sides[k]
        )
    mout_ref[0] = n_rows[0]
    mout_ref[1] = n_sides[0]


def gates_kernel(tiles, groups, cols, D, ax_ref, env_ref, inner_ref, in_ref, out_hbm, mout_hbm,
                 kron_ref, out_ref, mout_ref, store_sem):
    tile = lax.axis_index("tile")
    group = lax.axis_index("group")
    DD = D * D
    shift = D.bit_length() - 1
    halves = DD // LANES
    mixed = 2 * halves
    rows = DD // mixed
    lane = iota((D, LANES), 1)
    row = iota((D, LANES), 0)
    inner = lane & (D - 1)
    start = lane - inner
    slot = lane >> shift

    unit = jnp.where(inner == row, 1.0, 0.0).astype(F32)
    at_edge = (
        ((slot < cols) & (tile == 0))
        | ((slot >= cols) & (slot < 2 * cols) & (tile == tiles - 1))
        | ((slot == 2 * cols) & (group == 0))
        | ((slot == 2 * cols + 1) & (group == groups - 1))
    )
    late = [
        jnp.where(at_edge, unit, w).astype(BF16).astype(F32)
        for w in bond_weights(env_ref[0], env_ref[1])
    ]
    early = [inner_ref[s] for s in range(2)]

    unfold_mask = slot == (row & (LANES // D - 1))
    flat_rows = []
    for m in range(4 * cols):
        at = m // 4 + (cols if m % 4 >= 2 else 0)
        tiled = jnp.where(unfold_mask, pick(in_ref[m % 2], inner + at * D), 0.0)
        step = D // halves
        flat_rows.append(
            jnp.concatenate(
                [
                    jnp.sum(tiled[h * step : (h + 1) * step], axis=0, keepdims=True)
                    for h in range(halves)
                ],
                axis=1,
            )
        )
    mout_ref[...] = jnp.concatenate(flat_rows, axis=0).reshape(cols, 4, DD)
    store_msg = pltpu.make_async_copy(mout_ref, mout_hbm, store_sem.at[cols])
    store_msg.start()

    def by_major(value, m):
        return jnp.concatenate(
            [pick(value, m * D + slot + h * (LANES // D)) for h in range(halves)], axis=1
        )

    def by_minor(value, m):
        part = pick(value, m * D + inner)
        return jnp.concatenate([part] * halves, axis=1)

    scatter = unmixing(D, mixed, 1)
    stores = [
        pltpu.make_async_copy(out_ref.at[i], out_hbm.at[i], store_sem.at[i]) for i in range(cols)
    ]

    for i in range(cols):
        for s in range(2):
            left = by_major(late[s], 2 * cols) if i == 0 else by_major(early[s], i)
            right = (
                by_minor(late[s], 2 * cols + 1) if i == cols - 1 else by_minor(early[s], i + 1)
            )
            at = (i * 2 + s) * 2
            down = math.cosh(FIELD) * by_major(late[s], cols + i)
            build_kron(kron_ref, at, down, right)
            build_kron(kron_ref, at + 1, left, by_minor(late[s], i))
    gated = [
        [dot_nt(ax_ref[i, s], kron_ref[(i * 2 + s) * 2]).astype(BF16) for s in range(2)]
        for i in range(cols)
    ]
    gated = [
        [dot(kron_ref[(i * 2 + s) * 2 + 1], gated[i][s]).astype(BF16) for s in range(2)]
        for i in range(cols)
    ]

    def emit(i, gated):
        for b in range(0, mixed, 2):
            block = jnp.concatenate(
                [
                    jnp.concatenate(
                        [
                            gated[g % 2][
                                (b + c) * rows : (b + c + 1) * rows,
                                (g // 2) * LANES : (g // 2 + 1) * LANES,
                            ]
                            for c in range(2)
                        ],
                        axis=1,
                    )
                    for g in range(mixed)
                ],
                axis=0,
            )
            done = dot(scatter, block).astype(BF16)
            for c in range(2):
                for u in range(D):
                    at = u * D * mixed + (b + c) * D
                    out_ref[i, at : at + D, :] = done[
                        u * D : (u + 1) * D, c * LANES : (c + 1) * LANES
                    ]
        stores[i].start()

    for i in range(cols):
        emit(i, gated[i])
    for store in stores + [store_msg]:
        store.wait()


def per_device(tiles, groups, site_tensors, msg_in):
    _, cols, _, size = site_tensors.shape
    DD = msg_in.shape[-1]
    D = math.isqrt(DD)
    chunks = size // LANES
    a = site_tensors.reshape(cols, 2, chunks, LANES).transpose(0, 2, 1, 3)
    a = a.reshape(cols, 2 * chunks, LANES)
    vmem = pl.BlockSpec(memory_space=pltpu.VMEM)
    hbm = pl.BlockSpec(memory_space=pltpu.HBM)
    gated, env, inner, stacked = pl.pallas_call(
        functools.partial(messages_kernel, tiles, groups, cols, D),
        out_shape=(
            jax.ShapeDtypeStruct((cols, 2, DD, DD), BF16),
            jax.ShapeDtypeStruct((2, D, LANES), F32),
            jax.ShapeDtypeStruct((2, D, LANES), F32),
            jax.ShapeDtypeStruct((2, D, LANES), F32),
        ),
        in_specs=[hbm, hbm],
        out_specs=(vmem, vmem, vmem, vmem),
        scratch_shapes=[
            pltpu.VMEM(a.shape, BF16),
            pltpu.VMEM((cols, 4, DD), F32),
            pltpu.VMEM((cols, 2, DD, DD), BF16),
            pltpu.VMEM((cols, 2, DD, DD), BF16),
            pltpu.VMEM((cols, 2, DD, DD), BF16),
            pltpu.VMEM((cols, 2, DD, DD), BF16),
            pltpu.VMEM((2 * cols, DD, DD), BF16),
            pltpu.VMEM((2 * cols, 2, DD, DD), F32),
        ]
        + [
            pltpu.VMEM(((1 + turn) * D, LANES), F32) for _ in range(5) for turn in range(ITERS)
        ]
        + [
            pltpu.SemaphoreType.DMA((ITERS, 3)),
            pltpu.SemaphoreType.DMA((ITERS, 3)),
            pltpu.SemaphoreType.DMA((cols + 1,)),
        ],
        compiler_params=pltpu.CompilerParams(
            collective_id=0, has_side_effects=True, vmem_limit_bytes=24 * 2**20
        ),
    )(
        pltpu.with_memory_space_constraint(a, pltpu.HBM),
        pltpu.with_memory_space_constraint(msg_in[0], pltpu.HBM),
    )
    out, messages = pl.pallas_call(
        functools.partial(gates_kernel, tiles, groups, cols, D),
        out_shape=(
            jax.ShapeDtypeStruct(a.shape, BF16),
            jax.ShapeDtypeStruct((cols, 4, DD), F32),
        ),
        in_specs=[vmem, vmem, vmem, vmem],
        out_specs=(hbm, hbm),
        scratch_shapes=[
            pltpu.VMEM((4 * cols, DD, DD), BF16),
            pltpu.VMEM(a.shape, BF16),
            pltpu.VMEM((cols, 4, DD), F32),
            pltpu.SemaphoreType.DMA((cols + 1,)),
        ],
        compiler_params=pltpu.CompilerParams(vmem_limit_bytes=24 * 2**20),
    )(gated, env, inner, stacked)
    out = out.reshape(cols, chunks, 2, LANES).transpose(0, 2, 1, 3)
    return out.reshape(1, cols, 2, size), messages[None]


def solution(mesh):
    spec = P("tile", "group", None, None)
    return jax.shard_map(
        functools.partial(per_device, mesh.shape["tile"], mesh.shape["group"]),
        mesh=mesh, in_specs=(spec, spec), out_specs=(spec, spec), check_vma=False,
    )
```

```python
import functools
import math

import jax
import jax.numpy as jnp
from jax import lax
from jax.experimental import pallas as pl
from jax.experimental.pallas import tpu as pltpu
from jax.sharding import PartitionSpec as P

ITERS = 2
NS_STEPS = 6
LANES = 128
EPSILON = 1e-06
COUPLING = 0.5
FIELD = 0.3
F32 = jnp.float32
BF16 = jnp.bfloat16
MESH = pl.DeviceIdType.MESH


def iota(shape, axis):
    return lax.broadcasted_iota(jnp.int32, shape, axis)


def dot(a, b):
    return jnp.dot(a, b, preferred_element_type=F32)


def dot_nt(a, b):
    return lax.dot_general(a, b, (((1,), (1,)), ((), ())), preferred_element_type=F32)


def dot_tn(a, b):
    return lax.dot_general(a, b, (((0,), (0,)), ((), ())), preferred_element_type=F32)


def parts(value, count):
    out = []
    for _ in range(count):
        piece = value.astype(BF16)
        out.append(piece)
        value = value - piece.astype(F32)
    return out


def select_dot(value, selector, count):
    total = None
    for piece in parts(value, count):
        term = dot(piece, selector)
        total = term if total is None else total + term
    return total


def one_hot(mask):
    return jnp.where(mask, 1.0, 0.0).astype(BF16)


def build_kron(kron_ref, slot, first, second):
    D = first.shape[0]
    for d in range(D):
        kron_ref[slot, d * D : (d + 1) * D, :] = (first[d : d + 1, :] * second).astype(BF16)


def pick(value, index):
    return jnp.take_along_axis(value, index, axis=1, mode="promise_in_bounds")


def row_of(value, k):
    return jnp.broadcast_to(value[k : k + 1, :], value.shape)


def bond_weights(msg_sum, twist_sum):
    D = msg_sum.shape[0]
    lane = iota((D, LANES), 1)
    row = iota((D, LANES), 0)
    inner = lane & (D - 1)
    start = lane - inner
    turned = start + row
    unit = jnp.where(inner == row, 1.0, 0.0).astype(F32)
    g0, g1 = math.cosh(COUPLING), math.sinh(COUPLING)
    cross = math.sqrt(g0 * g1)
    root2 = math.sqrt(2.0)
    halves = [
        ((g0 * msg_sum + cross * twist_sum) / root2).astype(BF16).astype(F32),
        ((cross * twist_sum + g1 * msg_sum) / root2).astype(BF16).astype(F32),
    ]
    squares = halves[0] * halves[0] + halves[1] * halves[1]
    squares = jnp.broadcast_to(jnp.sum(squares, axis=0, keepdims=True), (D, LANES))
    trace = jnp.sum(pick(squares, turned), axis=0, keepdims=True) + EPSILON

    gram = None
    rotated = []
    for half in halves:
        transposed = None
        for k in range(D):
            own = row_of(half, k)
            column = pick(own, turned)
            term = column * own
            gram = term if gram is None else gram + term
            placed = jnp.where(inner == k, column, 0.0)
            transposed = placed if transposed is None else transposed + placed
        rotated.append(transposed)

    def columns(value):
        return [pick(row_of(value, k), turned) for k in range(D)]

    def times(left, right):
        sums = [None] * 4
        for k in range(D):
            term = left[k] * row_of(right, k)
            sums[k % 4] = term if sums[k % 4] is None else sums[k % 4] + term
        return (sums[0] + sums[1]) + (sums[2] + sums[3])

    state = gram / trace
    for step in range(NS_STEPS - 2):
        left = columns(state)
        square = times(left, state)
        rotated = [1.5 * v - 0.5 * times(left, v) for v in rotated]
        state = times(left, 2.25 * unit - 1.5 * state + 0.25 * square)
    left = columns(state)
    rotated = [1.5 * v - 0.5 * times(left, v) for v in rotated]
    again = rotated
    for _ in range(2):
        again = [1.5 * v - 0.5 * times(left, v) for v in again]
    rotated = [1.5 * v - 0.5 * times(left, w) for v, w in zip(rotated, again)]
    scale = 1.0 / jnp.sqrt(trace)
    first = math.sqrt(g0) * rotated[0] * scale
    second = math.sqrt(g1) * rotated[1] * scale
    return [first + second, first - second]


def unmixing(D, mixed, out_axis):
    DD = D * D
    sub = D // mixed
    p, k = iota((DD, DD), out_axis), iota((DD, DD), 1 - out_axis)
    low = p & (D - 1)
    mid = (p >> (D.bit_length() - 1)) & (sub - 1)
    top = p >> (D * sub).bit_length() - 1
    return one_hot(k == low * D + mid * mixed + top)


def messages_kernel(tiles, groups, cols, D, a_hbm, msg_hbm, ax_ref, env_ref, inner_ref, mout_ref,
           a_ref, msg_ref, x_ref, xt_ref, x2_ref, x2t_ref, kron_ref, gram_ref,
           send_v0, send_v1, send_s0, send_s1, _, send_f1, up_0, up_1, down_0, down_1, side_0, side_1,
           send_sem, recv_sem, load_sem):
    loads = [pltpu.make_async_copy(msg_hbm, msg_ref, load_sem.at[cols])]
    loads += [
        pltpu.make_async_copy(a_hbm.at[i], a_ref.at[i], load_sem.at[i]) for i in range(cols)
    ]
    for load in loads:
        load.start()
    tile = lax.axis_index("tile")
    group = lax.axis_index("group")
    DD = D * D
    shift = D.bit_length() - 1
    halves = DD // LANES
    mixed = 2 * halves
    sub = D // mixed
    per = LANES // D
    legs = 4 * cols
    crossing = jnp.where(group == 0, cols - 1, 0)
    closed = jnp.where(group == 0, 0, cols - 1)
    order = list(range(1, cols - 1)) + [closed, crossing]
    has_up = tile > 0
    has_down = tile < tiles - 1

    barrier = pltpu.get_barrier_semaphore()

    @pl.when(has_up)
    def _():
        pl.semaphore_signal(barrier, inc=1, device_id={"tile": tile - 1}, device_id_type=MESH)

    @pl.when(has_down)
    def _():
        pl.semaphore_signal(barrier, inc=1, device_id={"tile": tile + 1}, device_id_type=MESH)

    pl.semaphore_signal(barrier, inc=1, device_id={"group": 1 - group}, device_id_type=MESH)

    lane = iota((D, LANES), 1)
    row = iota((D, LANES), 0)
    within = lane & (D - 1)
    turned = lane - within + row
    slot = lane >> shift
    gather = unmixing(D, mixed, 0)
    fold_minor = one_hot((iota((LANES, LANES), 0) & (D - 1)) == (iota((LANES, LANES), 1) & (D - 1)))
    fold_major = one_hot((iota((DD, LANES), 0) >> shift) == (iota((DD, LANES), 1) & (D - 1)))

    def placed(entries):
        total = jnp.zeros((D, LANES), F32)
        for where, value in entries:
            total = jnp.where(slot == where, value, total)
        return total

    def by_major(value, m):
        return jnp.concatenate([pick(value, m * D + slot + h * per) for h in range(halves)], axis=1)

    def by_minor(value, m):
        return jnp.concatenate([pick(value, m * D + within)] * halves, axis=1)

    def rounded(value):
        return value.astype(BF16).astype(F32)

    def reduce_major(gram, weight):
        total = gram[:D] * weight[0:1, :]
        for d in range(1, D):
            total = total + gram[d * D : (d + 1) * D] * weight[d : d + 1, :]
        return total

    sublane = iota((8, DD), 0)

    def reduce_minor(gram, weight):
        blocks = []
        for d in range(D):
            block = gram[d * D : (d + 1) * D] * weight
            total = block[:8]
            for h in range(1, D // 8):
                total = total + block[h * 8 : (h + 1) * 8]
            blocks.append(total)
        out = []
        for base in range(0, D, 8):
            level = blocks[base : base + 8]
            step = 1
            while len(level) > 1:
                low = (sublane & step) == 0
                level = [
                    jnp.where(low, level[n], level[n + 1])
                    + pltpu.roll(jnp.where(low, level[n + 1], level[n]), step, 0)
                    for n in range(0, len(level), 2)
                ]
                step *= 2
            out.append(level[0])
        return jnp.concatenate(out, axis=0)

    def kinds_of(totals):
        if len(totals) == 1:
            return totals
        return [totals[0] + totals[1], totals[0] - totals[1]]

    def folded(totals, selector):
        pieces = []
        for total in totals:
            if selector is fold_minor:
                joined = total[:, :LANES]
                for h in range(1, halves):
                    joined = joined + total[:, h * LANES : (h + 1) * LANES]
                total = joined
            pieces += parts(total, 2)
        out = dot(jnp.concatenate(pieces, axis=0), selector)
        return [
            out[2 * n * D : (2 * n + 1) * D] + out[(2 * n + 1) * D : (2 * n + 2) * D]
            for n in range(len(totals))
        ]

    def minors(totals):
        count = len(totals[0])
        flat = folded([v for t in totals for v in t], fold_minor)
        return [flat[n * count : (n + 1) * count] for n in range(len(totals))]

    def majors(totals):
        count = len(totals[0])
        flat = folded([v for t in totals for v in t], fold_major)
        return [flat[n * count : (n + 1) * count] for n in range(len(totals))]

    def normalised(values):
        power = jnp.sum(values[0] * values[0], axis=0, keepdims=True)
        power = pick(jnp.broadcast_to(power, (D, LANES)), turned)
        power = jnp.sum(power, axis=0, keepdims=True) / DD
        scale = 1.0 / jnp.sqrt(power + EPSILON)
        return [v * scale for v in values]

    def upright(ups, downs, kind):
        return placed(
            [(i, ups[i][kind]) for i in range(cols)]
            + [(cols + i, downs[i][kind]) for i in range(cols)]
        )

    def copy(src, dst, turn, k, device):
        return pltpu.make_async_remote_copy(
            src_ref=src, dst_ref=dst, send_sem=send_sem.at[turn, k],
            recv_sem=recv_sem.at[turn, k], device_id=device, device_id_type=MESH,
        )

    def above_arrives(sent, arriving, dst, edges):
        @pl.when(has_up)
        def _():
            sent.wait_send()
            arriving.wait_recv()

        @pl.when(jnp.logical_not(has_up))
        def _():
            dst[...] = edges

    def below_arrives(sent, arriving, dst, edges):
        @pl.when(has_down)
        def _():
            sent.wait_send()
            arriving.wait_recv()

        @pl.when(jnp.logical_not(has_down))
        def _():
            dst[...] = edges

    def joined_rows(above, below):
        return [
            jnp.where(slot < cols, above[k * D : (k + 1) * D], below[k * D : (k + 1) * D])
            for k in range(above.shape[0] // D)
        ]

    from_left = (slot == 0) | (slot == 2 * cols)
    from_right = (slot == 2 * cols - 1) | (slot == 2 * cols + 1)

    def sides_arrive(to_side, dst, local, edges):
        to_side.wait()
        got = dst[...]
        out = []
        for k, (value, edge) in enumerate(zip(local, edges)):
            other = got[k * D : (k + 1) * D]
            value = jnp.where(from_left, jnp.where(group == 0, edge, other), value)
            out.append(
                jnp.where(from_right, jnp.where(group == groups - 1, edge, other), value)
            )
        return out

    loads[0].wait()
    spot = (row & (per - 1)) * D + within
    flat = msg_ref[...].reshape(legs, DD)

    def unfolded(m):
        source = jnp.concatenate(
            [
                jnp.broadcast_to(flat[m : m + 1, h * LANES : (h + 1) * LANES], (per, LANES))
                for h in range(halves)
            ],
            axis=0,
        )
        return pick(source, spot)

    singles = [unfolded(m) for m in range(legs)]
    edge_rows = placed(
        [(i, singles[4 * i]) for i in range(cols)]
        + [(cols + i, singles[4 * i + 2]) for i in range(cols)]
    )
    edge_sides = placed(
        [(i, singles[4 * i + 1]) for i in range(cols)]
        + [(cols + i, singles[4 * i + 3]) for i in range(cols)]
    )

    def unmix(i):
        for b in range(0, mixed, 2):
            pair = jnp.concatenate(
                [
                    jnp.concatenate(
                        [
                            a_ref[i, u * D * mixed + (b + c) * D : u * D * mixed + (b + c + 1) * D]
                            for u in range(D)
                        ],
                        axis=0,
                    )
                    for c in range(2)
                ],
                axis=1,
            )
            block = dot(gather, pair).astype(BF16)
            span = sub * D
            for c in range(2):
                for g in range(mixed):
                    x_ref[
                        i,
                        g % 2,
                        (b + c) * span : (b + c + 1) * span,
                        (g // 2) * LANES : (g // 2 + 1) * LANES,
                    ] = block[g * span : (g + 1) * span, c * LANES : (c + 1) * LANES]

    def relayout(i, s):
        for h in range(halves):
            for lh in range(halves):
                values = [
                    x_ref[
                        i, s, (lh * per + k) * D : (lh * per + k + 1) * D,
                        h * LANES : (h + 1) * LANES,
                    ]
                    for k in range(per)
                ]
                step = 1
                while step < per:
                    high = (slot & step) != 0
                    out = list(values)
                    for a in range(per):
                        if a & step:
                            continue
                        b = a | step
                        low_up = pltpu.roll(values[b], D * step, 1)
                        high_down = pltpu.roll(values[a], LANES - D * step, 1)
                        out[a] = jnp.where(high, low_up, values[a])
                        out[b] = jnp.where(high, values[b], high_down)
                    values = out
                    step *= 2
                for d in range(per):
                    x2_ref[
                        i, s, (h * per + d) * D : (h * per + d + 1) * D,
                        lh * LANES : (lh + 1) * LANES,
                    ] = values[d]
        x2t_ref[i, s] = x2_ref[i, s].T

    v_rows, v_sides = rounded(edge_rows), rounded(edge_sides)
    weights = []
    for i in range(cols):
        w_up, w_down = by_minor(v_rows, i), by_major(v_rows, cols + i)
        w_left, w_right = by_major(v_sides, i), by_minor(v_sides, cols + i)
        weights.append((w_up, w_down, w_left, w_right))
        build_kron(kron_ref, 2 * i, w_down, w_right)
        build_kron(kron_ref, 2 * i + 1, w_left, w_up)
    for load in loads[1:]:
        load.wait()
    for i in range(cols):
        unmix(i)
    for i in range(cols):
        for s in range(2):
            xt_ref[i, s] = x_ref[i, s].T
    sides_of = ((x_ref, xt_ref), (xt_ref, x_ref))

    def first_gram(path, i):
        left, right = sides_of[path]
        y = [dot(left[i, s], kron_ref[2 * i + path]).astype(BF16) for s in range(2)]
        gram_ref[2 * i + path, 0] = dot(
            jnp.concatenate(y, axis=1), right[i].reshape(2 * DD, DD)
        )

    def outer(i, leg):
        w_up, w_down, w_left, w_right = weights[i]
        if leg == 0:
            return [reduce_major(gram_ref[2 * i, 0], w_left)]
        if leg == 1:
            return [reduce_minor(gram_ref[2 * i, 0], w_up)]
        if leg == 2:
            return [reduce_minor(gram_ref[2 * i + 1, 0], w_right)]
        return [reduce_major(gram_ref[2 * i + 1, 0], w_down)]

    first_gram(0, 0)
    first_gram(1, cols - 1)
    for i in range(1, cols):
        first_gram(0, i)
    for i in range(cols - 1):
        first_gram(1, i)
    (left_first,), (right_last,) = majors([outer(0, 1)]), minors([outer(cols - 1, 3)])
    send_s0[...] = normalised([jnp.where(from_left, right_last[0], left_first[0])])[0]
    ups = [outer(i, 0) for i in range(cols)]

    inside = jnp.logical_and(has_up, has_down)

    @pl.when(inside)
    def _():
        pl.semaphore_wait(barrier, 3)

    @pl.when(jnp.logical_not(inside))
    def _():
        pl.semaphore_wait(barrier, 2)

    sides_0 = copy(send_s0, side_0, 0, 2, {"group": 1 - group})
    sides_0.start()
    downs = majors([outer(i, 2) for i in range(cols)])
    ups = minors(ups)
    send_v0[...] = normalised([upright(downs, ups, 0)])[0]
    to_up = copy(send_v0, down_0, 0, 0, {"tile": tile - 1})
    to_down = copy(send_v0, up_0, 0, 1, {"tile": tile + 1})

    @pl.when(has_up)
    def _():
        to_up.start()

    @pl.when(has_down)
    def _():
        to_down.start()

    for i in range(cols):
        for s in range(2):
            relayout(i, s)

    lefts = [left_first] + majors([outer(i, 1) for i in range(1, cols)])
    rights = minors([outer(i, 3) for i in range(cols - 1)]) + [right_last]

    def inner_view(lefts, rights, kind):
        return placed(
            [(i, rights[i - 1][kind]) for i in range(1, cols)]
            + [(cols + i, lefts[i + 1][kind]) for i in range(cols - 1)]
        )

    n_sides = normalised([inner_view(lefts, rights, 0)])

    side_weights = []

    def paired(j, kron, left, right, at):
        i = order[j]
        for s in range(2):
            y = dot(left[i, s], kron_ref[kron]).astype(BF16)
            gram_ref[at, s] = dot(y, right[i, s])

    for j in range(cols):
        if j == cols - 1:
            n_sides = sides_arrive(sides_0, side_0, n_sides, [edge_sides])
        v_sides = rounded(n_sides[0]) if j == cols - 1 else rounded(jnp.where(
            from_left | from_right, edge_sides, n_sides[0]
        ))
        i = order[j]
        w_left, w_right = by_major(v_sides, i), by_minor(v_sides, cols + i)
        side_weights.append((w_left, w_right))
        build_kron(kron_ref, 2 * j, w_left, w_right)
        paired(j, 2 * j, x2_ref, x2t_ref, 2 * j)

    mix = jnp.full((D, DD), math.tanh(FIELD), BF16)
    for i in range(cols):
        for d in range(0, DD, D):
            a0, a1 = (x_ref[i, s, d : d + D] for s in range(2))
            ax_ref[i, 0, d : d + D] = a0 + mix * a1
            ax_ref[i, 1, d : d + D] = a1 + mix * a0

    far_up = lax.rem(tile, 2) == 0
    far_down = jnp.logical_not(far_up)

    def above_0():
        above_arrives(to_up, to_down, up_0, edge_rows)

    def below_0():
        below_arrives(to_down, to_up, down_0, edge_rows)

    def up_legs(rows, j):
        weight = by_major(rows, cols + order[j])
        return kinds_of([reduce_major(gram_ref[2 * j, s], weight) for s in range(2)])

    def down_legs(rows, j):
        weight = by_minor(rows, order[j])
        return kinds_of([reduce_minor(gram_ref[2 * j, s], weight) for s in range(2)])

    def ship(buffer, values):
        for k in range(2):
            buffer[k * D : (k + 1) * D] = values[k]

    def ordered(above, below, kind):
        return placed(
            [(order[j], above[j][kind]) for j in range(cols)]
            + [(cols + order[j], below[j][kind]) for j in range(cols)]
        )

    nothing = [[jnp.zeros((D, LANES), F32)] * 2] * cols
    up_far = copy(send_f1, down_1, 1, 0, {"tile": tile - 1})
    up_near = copy(send_v1, down_1, 1, 0, {"tile": tile - 1})
    down_far = copy(send_f1, up_1, 1, 1, {"tile": tile + 1})
    down_near = copy(send_v1, up_1, 1, 1, {"tile": tile + 1})

    @pl.when(far_up)
    def _():
        below_0()
        rows = rounded(down_0[...])
        legs_up = minors([up_legs(rows, j) for j in range(cols)])
        ship(send_f1, normalised([ordered(nothing, legs_up, k) for k in range(2)]))

        @pl.when(has_up)
        def _():
            up_far.start()

    @pl.when(far_down)
    def _():
        above_0()
        rows = rounded(up_0[...])
        legs_down = majors([down_legs(rows, j) for j in range(cols)])
        ship(send_f1, normalised([ordered(legs_down, nothing, k) for k in range(2)]))

        @pl.when(has_down)
        def _():
            down_far.start()

    @pl.when(far_up)
    def _():
        above_0()

    @pl.when(far_down)
    def _():
        below_0()

    v_rows = rounded(joined_rows(up_0[...], down_0[...])[0])
    weights = []
    for j in range(cols):
        i = order[j]
        weights.append((by_minor(v_rows, i), by_major(v_rows, cols + i)))

    def horizontal(j):
        build_kron(kron_ref, 2 * j + 1, weights[j][1], weights[j][0])
        paired(j, 2 * j + 1, x2t_ref, x2_ref, 2 * j + 1)
        w_left, w_right = side_weights[j]
        left = kinds_of([reduce_minor(gram_ref[2 * j + 1, s], w_right) for s in range(2)])
        right = kinds_of([reduce_major(gram_ref[2 * j + 1, s], w_left) for s in range(2)])
        return left, right

    left, right = horizontal(cols - 1)
    (left,), (right,) = majors([left]), minors([right])
    ship(send_s1, normalised([jnp.where(from_left, right[k], left[k]) for k in range(2)]))
    sides_1 = copy(send_s1, side_1, 1, 2, {"group": 1 - group})

    @pl.when(far_up)
    def _():
        sides_1.start()

    @pl.when(far_down)
    def _():
        sides_1.start()

    ups = minors([up_legs(v_rows, j) for j in range(cols)])
    downs = majors([down_legs(v_rows, j) for j in range(cols)])
    ship(send_v1, normalised([ordered(downs, ups, k) for k in range(2)]))

    @pl.when(far_up & has_down)
    def _():
        down_near.start()

    @pl.when(far_down & has_up)
    def _():
        up_near.start()

    o_rows = normalised([ordered(ups, downs, k) for k in range(2)])
    others = [horizontal(j) for j in range(cols - 1)]
    lefts = majors([o[0] for o in others]) + [left]
    rights = minors([o[1] for o in others]) + [right]

    def own_sides(kind):
        base = placed(
            [(order[j], lefts[j][kind]) for j in range(cols)]
            + [(cols + order[j], rights[j][kind]) for j in range(cols)]
        )
        base = jnp.where((slot == 2 * cols) & (group == groups - 1), lefts[-1][kind], base)
        return jnp.where((slot == 2 * cols + 1) & (group == 0), rights[-1][kind], base)

    def other_sides(kind):
        entries = []
        for j, i in enumerate(order):
            entries.append((jnp.where(i == 0, -1, cols + i - 1), lefts[j][kind]))
            entries.append((jnp.where(i == cols - 1, -1, i + 1), rights[j][kind]))
        return placed(entries)

    o_sides = normalised([own_sides(k) for k in range(2)])
    n_sides = normalised([other_sides(k) for k in range(2)])
    for s, weight in enumerate(bond_weights(*[o + n for o, n in zip(o_sides, n_sides)])):
        inner_ref[s] = rounded(weight)
    zero = jnp.zeros((D, LANES), F32)
    n_sides = sides_arrive(sides_1, side_1, n_sides, [edge_sides, zero])
    rows_edges = jnp.concatenate([edge_rows, zero], axis=0)
    above_arrives(up_near, down_near, up_1, rows_edges)
    below_arrives(down_near, up_near, down_1, rows_edges)
    n_rows = joined_rows(up_1[...], down_1[...])
    for k in range(2):
        env_ref[k] = jnp.where(
            slot < 2 * cols, o_rows[k] + n_rows[k], o_sides[k] + n_sides[k]
        )
    mout_ref[0] = n_rows[0]
    mout_ref[1] = n_sides[0]


def gates_kernel(tiles, groups, cols, D, ax_ref, env_ref, inner_ref, in_ref, out_hbm, mout_hbm,
                 kron_ref, out_ref, mout_ref, store_sem):
    tile = lax.axis_index("tile")
    group = lax.axis_index("group")
    DD = D * D
    shift = D.bit_length() - 1
    halves = DD // LANES
    mixed = 2 * halves
    rows = DD // mixed
    lane = iota((D, LANES), 1)
    row = iota((D, LANES), 0)
    inner = lane & (D - 1)
    start = lane - inner
    slot = lane >> shift

    unit = jnp.where(inner == row, 1.0, 0.0).astype(F32)
    at_edge = (
        ((slot < cols) & (tile == 0))
        | ((slot >= cols) & (slot < 2 * cols) & (tile == tiles - 1))
        | ((slot == 2 * cols) & (group == 0))
        | ((slot == 2 * cols + 1) & (group == groups - 1))
    )
    late = [
        jnp.where(at_edge, unit, w).astype(BF16).astype(F32)
        for w in bond_weights(env_ref[0], env_ref[1])
    ]
    early = [inner_ref[s] for s in range(2)]

    unfold_mask = slot == (row & (LANES // D - 1))
    flat_rows = []
    for m in range(4 * cols):
        at = m // 4 + (cols if m % 4 >= 2 else 0)
        tiled = jnp.where(unfold_mask, pick(in_ref[m % 2], inner + at * D), 0.0)
        step = D // halves
        flat_rows.append(
            jnp.concatenate(
                [
                    jnp.sum(tiled[h * step : (h + 1) * step], axis=0, keepdims=True)
                    for h in range(halves)
                ],
                axis=1,
            )
        )
    mout_ref[...] = jnp.concatenate(flat_rows, axis=0).reshape(cols, 4, DD)
    store_msg = pltpu.make_async_copy(mout_ref, mout_hbm, store_sem.at[cols])
    store_msg.start()

    def by_major(value, m):
        return jnp.concatenate(
            [pick(value, m * D + slot + h * (LANES // D)) for h in range(halves)], axis=1
        )

    def by_minor(value, m):
        part = pick(value, m * D + inner)
        return jnp.concatenate([part] * halves, axis=1)

    scatter = unmixing(D, mixed, 1)
    stores = [
        pltpu.make_async_copy(out_ref.at[i], out_hbm.at[i], store_sem.at[i]) for i in range(cols)
    ]

    for i in range(cols):
        for s in range(2):
            left = by_major(late[s], 2 * cols) if i == 0 else by_major(early[s], i)
            right = (
                by_minor(late[s], 2 * cols + 1) if i == cols - 1 else by_minor(early[s], i + 1)
            )
            at = (i * 2 + s) * 2
            down = math.cosh(FIELD) * by_major(late[s], cols + i)
            build_kron(kron_ref, at, down, right)
            build_kron(kron_ref, at + 1, left, by_minor(late[s], i))
    gated = [
        [dot_nt(ax_ref[i, s], kron_ref[(i * 2 + s) * 2]).astype(BF16) for s in range(2)]
        for i in range(cols)
    ]
    gated = [
        [dot(kron_ref[(i * 2 + s) * 2 + 1], gated[i][s]).astype(BF16) for s in range(2)]
        for i in range(cols)
    ]

    def emit(i, gated):
        for b in range(0, mixed, 2):
            block = jnp.concatenate(
                [
                    jnp.concatenate(
                        [
                            gated[g % 2][
                                (b + c) * rows : (b + c + 1) * rows,
                                (g // 2) * LANES : (g // 2 + 1) * LANES,
                            ]
                            for c in range(2)
                        ],
                        axis=1,
                    )
                    for g in range(mixed)
                ],
                axis=0,
            )
            done = dot(scatter, block).astype(BF16)
            for c in range(2):
                for u in range(D):
                    at = u * D * mixed + (b + c) * D
                    out_ref[i, at : at + D, :] = done[
                        u * D : (u + 1) * D, c * LANES : (c + 1) * LANES
                    ]
        stores[i].start()

    for i in range(cols):
        emit(i, gated[i])
    for store in stores + [store_msg]:
        store.wait()


def per_device(tiles, groups, site_tensors, msg_in):
    _, cols, _, size = site_tensors.shape
    DD = msg_in.shape[-1]
    D = math.isqrt(DD)
    chunks = size // LANES
    a = site_tensors.reshape(cols, 2, chunks, LANES).transpose(0, 2, 1, 3)
    a = a.reshape(cols, 2 * chunks, LANES)
    vmem = pl.BlockSpec(memory_space=pltpu.VMEM)
    hbm = pl.BlockSpec(memory_space=pltpu.HBM)
    gated, env, inner, stacked = pl.pallas_call(
        functools.partial(messages_kernel, tiles, groups, cols, D),
        out_shape=(
            jax.ShapeDtypeStruct((cols, 2, DD, DD), BF16),
            jax.ShapeDtypeStruct((2, D, LANES), F32),
            jax.ShapeDtypeStruct((2, D, LANES), F32),
            jax.ShapeDtypeStruct((2, D, LANES), F32),
        ),
        in_specs=[hbm, hbm],
        out_specs=(vmem, vmem, vmem, vmem),
        scratch_shapes=[
            pltpu.VMEM(a.shape, BF16),
            pltpu.VMEM((cols, 4, DD), F32),
            pltpu.VMEM((cols, 2, DD, DD), BF16),
            pltpu.VMEM((cols, 2, DD, DD), BF16),
            pltpu.VMEM((cols, 2, DD, DD), BF16),
            pltpu.VMEM((cols, 2, DD, DD), BF16),
            pltpu.VMEM((2 * cols, DD, DD), BF16),
            pltpu.VMEM((2 * cols, 2, DD, DD), F32),
        ]
        + [
            pltpu.VMEM(((1 + turn) * D, LANES), F32) for _ in range(6) for turn in range(ITERS)
        ]
        + [
            pltpu.SemaphoreType.DMA((ITERS, 3)),
            pltpu.SemaphoreType.DMA((ITERS, 3)),
            pltpu.SemaphoreType.DMA((cols + 1,)),
        ],
        compiler_params=pltpu.CompilerParams(
            collective_id=0, has_side_effects=True, vmem_limit_bytes=24 * 2**20
        ),
    )(
        pltpu.with_memory_space_constraint(a, pltpu.HBM),
        pltpu.with_memory_space_constraint(msg_in[0], pltpu.HBM),
    )
    out, messages = pl.pallas_call(
        functools.partial(gates_kernel, tiles, groups, cols, D),
        out_shape=(
            jax.ShapeDtypeStruct(a.shape, BF16),
            jax.ShapeDtypeStruct((cols, 4, DD), F32),
        ),
        in_specs=[vmem, vmem, vmem, vmem],
        out_specs=(hbm, hbm),
        scratch_shapes=[
            pltpu.VMEM((4 * cols, DD, DD), BF16),
            pltpu.VMEM(a.shape, BF16),
            pltpu.VMEM((cols, 4, DD), F32),
            pltpu.SemaphoreType.DMA((cols + 1,)),
        ],
        compiler_params=pltpu.CompilerParams(vmem_limit_bytes=24 * 2**20),
    )(gated, env, inner, stacked)
    out = out.reshape(cols, chunks, 2, LANES).transpose(0, 2, 1, 3)
    return out.reshape(1, cols, 2, size), messages[None]


def solution(mesh):
    spec = P("tile", "group", None, None)
    return jax.shard_map(
        functools.partial(per_device, mesh.shape["tile"], mesh.shape["group"]),
        mesh=mesh, in_specs=(spec, spec), out_specs=(spec, spec), check_vma=False,
    )
```

```python
import functools
import math

import jax
import jax.numpy as jnp
from jax import lax
from jax.experimental import pallas as pl
from jax.experimental.pallas import tpu as pltpu
from jax.sharding import PartitionSpec as P

ITERS = 2
NS_STEPS = 6
LANES = 128
EPSILON = 1e-06
COUPLING = 0.5
FIELD = 0.3
F32 = jnp.float32
BF16 = jnp.bfloat16
MESH = pl.DeviceIdType.MESH


def iota(shape, axis):
    return lax.broadcasted_iota(jnp.int32, shape, axis)


def dot(a, b):
    return jnp.dot(a, b, preferred_element_type=F32)


def dot_nt(a, b):
    return lax.dot_general(a, b, (((1,), (1,)), ((), ())), preferred_element_type=F32)


def dot_tn(a, b):
    return lax.dot_general(a, b, (((0,), (0,)), ((), ())), preferred_element_type=F32)


def parts(value, count):
    out = []
    for _ in range(count):
        piece = value.astype(BF16)
        out.append(piece)
        value = value - piece.astype(F32)
    return out


def select_dot(value, selector, count):
    total = None
    for piece in parts(value, count):
        term = dot(piece, selector)
        total = term if total is None else total + term
    return total


def one_hot(mask):
    return jnp.where(mask, 1.0, 0.0).astype(BF16)


def build_kron(kron_ref, slot, first, second):
    D = first.shape[0]
    for d in range(D):
        kron_ref[slot, d * D : (d + 1) * D, :] = (first[d : d + 1, :] * second).astype(BF16)


def pick(value, index):
    return jnp.take_along_axis(value, index, axis=1, mode="promise_in_bounds")


def row_of(value, k):
    return jnp.broadcast_to(value[k : k + 1, :], value.shape)


def bond_weights(msg_sum, twist_sum):
    D = msg_sum.shape[0]
    lane = iota((D, LANES), 1)
    row = iota((D, LANES), 0)
    inner = lane & (D - 1)
    start = lane - inner
    turned = start + row
    unit = jnp.where(inner == row, 1.0, 0.0).astype(F32)
    g0, g1 = math.cosh(COUPLING), math.sinh(COUPLING)
    cross = math.sqrt(g0 * g1)
    root2 = math.sqrt(2.0)
    halves = [
        ((g0 * msg_sum + cross * twist_sum) / root2).astype(BF16).astype(F32),
        ((cross * twist_sum + g1 * msg_sum) / root2).astype(BF16).astype(F32),
    ]
    squares = halves[0] * halves[0] + halves[1] * halves[1]
    squares = jnp.broadcast_to(jnp.sum(squares, axis=0, keepdims=True), (D, LANES))
    trace = jnp.sum(pick(squares, turned), axis=0, keepdims=True) + EPSILON

    gram = None
    rotated = []
    for half in halves:
        transposed = None
        for k in range(D):
            own = row_of(half, k)
            column = pick(own, turned)
            term = column * own
            gram = term if gram is None else gram + term
            placed = jnp.where(inner == k, column, 0.0)
            transposed = placed if transposed is None else transposed + placed
        rotated.append(transposed)

    def columns(value):
        return [pick(row_of(value, k), turned) for k in range(D)]

    def times(left, right):
        sums = [None] * 4
        for k in range(D):
            term = left[k] * row_of(right, k)
            sums[k % 4] = term if sums[k % 4] is None else sums[k % 4] + term
        return (sums[0] + sums[1]) + (sums[2] + sums[3])

    state = gram / trace
    for step in range(NS_STEPS - 2):
        left = columns(state)
        square = times(left, state)
        rotated = [1.5 * v - 0.5 * times(left, v) for v in rotated]
        state = times(left, 2.25 * unit - 1.5 * state + 0.25 * square)
    left = columns(state)
    rotated = [1.5 * v - 0.5 * times(left, v) for v in rotated]
    again = rotated
    for _ in range(2):
        again = [1.5 * v - 0.5 * times(left, v) for v in again]
    rotated = [1.5 * v - 0.5 * times(left, w) for v, w in zip(rotated, again)]
    scale = 1.0 / jnp.sqrt(trace)
    first = math.sqrt(g0) * rotated[0] * scale
    second = math.sqrt(g1) * rotated[1] * scale
    return [first + second, first - second]


def unmixing(D, mixed, out_axis):
    DD = D * D
    sub = D // mixed
    p, k = iota((DD, DD), out_axis), iota((DD, DD), 1 - out_axis)
    low = p & (D - 1)
    mid = (p >> (D.bit_length() - 1)) & (sub - 1)
    top = p >> (D * sub).bit_length() - 1
    return one_hot(k == low * D + mid * mixed + top)


def messages_kernel(tiles, groups, cols, D, a_hbm, msg_hbm, ax_ref, env_ref, inner_ref, mout_ref,
           a_ref, msg_ref, near_ref, x_ref, xt_ref, x2_ref, x2t_ref, kron_ref, gram_ref,
           send_v0, send_v1, send_s0, send_s1, _, send_f1, up_0, up_1, down_0, down_1, side_0, side_1,
           send_sem, recv_sem, load_sem):
    loads = [pltpu.make_async_copy(msg_hbm, msg_ref, load_sem.at[cols])]
    loads += [
        pltpu.make_async_copy(a_hbm.at[i], a_ref.at[i], load_sem.at[i]) for i in range(cols)
    ]
    for load in loads:
        load.start()
    tile = lax.axis_index("tile")
    group = lax.axis_index("group")
    DD = D * D
    shift = D.bit_length() - 1
    halves = DD // LANES
    mixed = 2 * halves
    sub = D // mixed
    per = LANES // D
    legs = 4 * cols
    crossing = jnp.where(group == 0, cols - 1, 0)
    closed = jnp.where(group == 0, 0, cols - 1)
    order = list(range(1, cols - 1)) + [closed, crossing]
    has_up = tile > 0
    has_down = tile < tiles - 1

    barrier = pltpu.get_barrier_semaphore()

    @pl.when(has_up)
    def _():
        pl.semaphore_signal(barrier, inc=1, device_id={"tile": tile - 1}, device_id_type=MESH)

    @pl.when(has_down)
    def _():
        pl.semaphore_signal(barrier, inc=1, device_id={"tile": tile + 1}, device_id_type=MESH)

    pl.semaphore_signal(barrier, inc=1, device_id={"group": 1 - group}, device_id_type=MESH)

    lane = iota((D, LANES), 1)
    row = iota((D, LANES), 0)
    within = lane & (D - 1)
    turned = lane - within + row
    slot = lane >> shift
    gather = unmixing(D, mixed, 0)
    fold_minor = one_hot((iota((LANES, LANES), 0) & (D - 1)) == (iota((LANES, LANES), 1) & (D - 1)))
    fold_major = one_hot((iota((DD, LANES), 0) >> shift) == (iota((DD, LANES), 1) & (D - 1)))

    def placed(entries):
        total = jnp.zeros((D, LANES), F32)
        for where, value in entries:
            total = jnp.where(slot == where, value, total)
        return total

    def by_major(value, m):
        return jnp.concatenate([pick(value, m * D + slot + h * per) for h in range(halves)], axis=1)

    def by_minor(value, m):
        return jnp.concatenate([pick(value, m * D + within)] * halves, axis=1)

    def rounded(value):
        return value.astype(BF16).astype(F32)

    def reduce_major(gram, weight):
        total = gram[:D] * weight[0:1, :]
        for d in range(1, D):
            total = total + gram[d * D : (d + 1) * D] * weight[d : d + 1, :]
        return total

    sublane = iota((8, DD), 0)

    def reduce_minor(gram, weight):
        blocks = []
        for d in range(D):
            block = gram[d * D : (d + 1) * D] * weight
            total = block[:8]
            for h in range(1, D // 8):
                total = total + block[h * 8 : (h + 1) * 8]
            blocks.append(total)
        out = []
        for base in range(0, D, 8):
            level = blocks[base : base + 8]
            step = 1
            while len(level) > 1:
                low = (sublane & step) == 0
                level = [
                    jnp.where(low, level[n], level[n + 1])
                    + pltpu.roll(jnp.where(low, level[n + 1], level[n]), step, 0)
                    for n in range(0, len(level), 2)
                ]
                step *= 2
            out.append(level[0])
        return jnp.concatenate(out, axis=0)

    def kinds_of(totals):
        if len(totals) == 1:
            return totals
        return [totals[0] + totals[1], totals[0] - totals[1]]

    def folded(totals, selector):
        pieces = []
        for total in totals:
            if selector is fold_minor:
                joined = total[:, :LANES]
                for h in range(1, halves):
                    joined = joined + total[:, h * LANES : (h + 1) * LANES]
                total = joined
            pieces += parts(total, 2)
        out = dot(jnp.concatenate(pieces, axis=0), selector)
        return [
            out[2 * n * D : (2 * n + 1) * D] + out[(2 * n + 1) * D : (2 * n + 2) * D]
            for n in range(len(totals))
        ]

    def minors(totals):
        count = len(totals[0])
        flat = folded([v for t in totals for v in t], fold_minor)
        return [flat[n * count : (n + 1) * count] for n in range(len(totals))]

    def majors(totals):
        count = len(totals[0])
        flat = folded([v for t in totals for v in t], fold_major)
        return [flat[n * count : (n + 1) * count] for n in range(len(totals))]

    def normalised(values):
        power = jnp.sum(values[0] * values[0], axis=0, keepdims=True)
        power = pick(jnp.broadcast_to(power, (D, LANES)), turned)
        power = jnp.sum(power, axis=0, keepdims=True) / DD
        scale = 1.0 / jnp.sqrt(power + EPSILON)
        return [v * scale for v in values]

    def upright(ups, downs, kind):
        return placed(
            [(i, ups[i][kind]) for i in range(cols)]
            + [(cols + i, downs[i][kind]) for i in range(cols)]
        )

    def copy(src, dst, turn, k, device):
        return pltpu.make_async_remote_copy(
            src_ref=src, dst_ref=dst, send_sem=send_sem.at[turn, k],
            recv_sem=recv_sem.at[turn, k], device_id=device, device_id_type=MESH,
        )

    def above_arrives(sent, arriving, dst, edges):
        @pl.when(has_up)
        def _():
            sent.wait_send()
            arriving.wait_recv()

        @pl.when(jnp.logical_not(has_up))
        def _():
            dst[...] = edges

    def below_arrives(sent, arriving, dst, edges):
        @pl.when(has_down)
        def _():
            sent.wait_send()
            arriving.wait_recv()

        @pl.when(jnp.logical_not(has_down))
        def _():
            dst[...] = edges

    def joined_rows(above, below):
        return [
            jnp.where(slot < cols, above[k * D : (k + 1) * D], below[k * D : (k + 1) * D])
            for k in range(above.shape[0] // D)
        ]

    from_left = (slot == 0) | (slot == 2 * cols)
    from_right = (slot == 2 * cols - 1) | (slot == 2 * cols + 1)

    def sides_arrive(to_side, dst, local, edges):
        to_side.wait()
        got = dst[...]
        out = []
        for k, (value, edge) in enumerate(zip(local, edges)):
            other = got[k * D : (k + 1) * D]
            value = jnp.where(from_left, jnp.where(group == 0, edge, other), value)
            out.append(
                jnp.where(from_right, jnp.where(group == groups - 1, edge, other), value)
            )
        return out

    loads[0].wait()
    spot = (row & (per - 1)) * D + within
    flat = msg_ref[...].reshape(legs, DD)

    def unfolded(m):
        source = jnp.concatenate(
            [
                jnp.broadcast_to(flat[m : m + 1, h * LANES : (h + 1) * LANES], (per, LANES))
                for h in range(halves)
            ],
            axis=0,
        )
        return pick(source, spot)

    singles = [unfolded(m) for m in range(legs)]
    edge_rows = placed(
        [(i, singles[4 * i]) for i in range(cols)]
        + [(cols + i, singles[4 * i + 2]) for i in range(cols)]
    )
    edge_sides = placed(
        [(i, singles[4 * i + 1]) for i in range(cols)]
        + [(cols + i, singles[4 * i + 3]) for i in range(cols)]
    )

    def unmix(i):
        for b in range(0, mixed, 2):
            pair = jnp.concatenate(
                [
                    jnp.concatenate(
                        [
                            a_ref[i, u * D * mixed + (b + c) * D : u * D * mixed + (b + c + 1) * D]
                            for u in range(D)
                        ],
                        axis=0,
                    )
                    for c in range(2)
                ],
                axis=1,
            )
            block = dot(gather, pair).astype(BF16)
            span = sub * D
            for c in range(2):
                for g in range(mixed):
                    x_ref[
                        i,
                        g % 2,
                        (b + c) * span : (b + c + 1) * span,
                        (g // 2) * LANES : (g // 2 + 1) * LANES,
                    ] = block[g * span : (g + 1) * span, c * LANES : (c + 1) * LANES]

    def relayout(i, s):
        for h in range(halves):
            for lh in range(halves):
                values = [
                    x_ref[
                        i, s, (lh * per + k) * D : (lh * per + k + 1) * D,
                        h * LANES : (h + 1) * LANES,
                    ]
                    for k in range(per)
                ]
                step = 1
                while step < per:
                    high = (slot & step) != 0
                    out = list(values)
                    for a in range(per):
                        if a & step:
                            continue
                        b = a | step
                        low_up = pltpu.roll(values[b], D * step, 1)
                        high_down = pltpu.roll(values[a], LANES - D * step, 1)
                        out[a] = jnp.where(high, low_up, values[a])
                        out[b] = jnp.where(high, values[b], high_down)
                    values = out
                    step *= 2
                for d in range(per):
                    x2_ref[
                        i, s, (h * per + d) * D : (h * per + d + 1) * D,
                        lh * LANES : (lh + 1) * LANES,
                    ] = values[d]
        x2t_ref[i, s] = x2_ref[i, s].T

    v_rows, v_sides = rounded(edge_rows), rounded(edge_sides)
    weights = []
    for i in range(cols):
        w_up, w_down = by_minor(v_rows, i), by_major(v_rows, cols + i)
        w_left, w_right = by_major(v_sides, i), by_minor(v_sides, cols + i)
        weights.append((w_up, w_down, w_left, w_right))
        build_kron(kron_ref, 2 * i, w_down, w_right)
        build_kron(kron_ref, 2 * i + 1, w_left, w_up)
    for load in loads[1:]:
        load.wait()
    for i in range(cols):
        unmix(i)
    for i in range(cols):
        for s in range(2):
            xt_ref[i, s] = x_ref[i, s].T
    sides_of = ((x_ref, xt_ref), (xt_ref, x_ref))

    def first_gram(path, i):
        left, right = sides_of[path]
        y = [dot(left[i, s], kron_ref[2 * i + path]).astype(BF16) for s in range(2)]
        gram_ref[2 * i + path, 0] = dot(
            jnp.concatenate(y, axis=1), right[i].reshape(2 * DD, DD)
        )

    def outer(i, leg):
        w_up, w_down, w_left, w_right = weights[i]
        if leg == 0:
            return [reduce_major(gram_ref[2 * i, 0], w_left)]
        if leg == 1:
            return [reduce_minor(gram_ref[2 * i, 0], w_up)]
        if leg == 2:
            return [reduce_minor(gram_ref[2 * i + 1, 0], w_right)]
        return [reduce_major(gram_ref[2 * i + 1, 0], w_down)]

    first_gram(0, 0)
    first_gram(1, cols - 1)
    for i in range(1, cols):
        first_gram(0, i)
    for i in range(cols - 1):
        first_gram(1, i)
    (left_first,), (right_last,) = majors([outer(0, 1)]), minors([outer(cols - 1, 3)])
    send_s0[...] = normalised([jnp.where(from_left, right_last[0], left_first[0])])[0]
    ups = [outer(i, 0) for i in range(cols)]

    mix = jnp.full((D, DD), math.tanh(FIELD), BF16)
    for i in range(cols):
        for d in range(0, DD, D):
            a0, a1 = (x_ref[i, s, d : d + D] for s in range(2))
            ax_ref[i, 0, d : d + D] = a0 + mix * a1
            ax_ref[i, 1, d : d + D] = a1 + mix * a0

    inside = jnp.logical_and(has_up, has_down)

    @pl.when(inside)
    def _():
        pl.semaphore_wait(barrier, 3)

    @pl.when(jnp.logical_not(inside))
    def _():
        pl.semaphore_wait(barrier, 2)

    sides_0 = copy(send_s0, side_0, 0, 2, {"group": 1 - group})
    sides_0.start()
    downs = majors([outer(i, 2) for i in range(cols)])
    ups = minors(ups)
    send_v0[...] = normalised([upright(downs, ups, 0)])[0]
    to_up = copy(send_v0, down_0, 0, 0, {"tile": tile - 1})
    to_down = copy(send_v0, up_0, 0, 1, {"tile": tile + 1})

    @pl.when(has_up)
    def _():
        to_up.start()

    @pl.when(has_down)
    def _():
        to_down.start()

    for i in range(cols):
        for s in range(2):
            relayout(i, s)

    lefts = [left_first] + majors([outer(i, 1) for i in range(1, cols)])
    rights = minors([outer(i, 3) for i in range(cols - 1)]) + [right_last]

    def inner_view(lefts, rights, kind):
        return placed(
            [(i, rights[i - 1][kind]) for i in range(1, cols)]
            + [(cols + i, lefts[i + 1][kind]) for i in range(cols - 1)]
        )

    n_sides = normalised([inner_view(lefts, rights, 0)])

    far_up = lax.rem(tile, 2) == 0
    far_down = jnp.logical_not(far_up)

    def above_0():
        above_arrives(to_up, to_down, up_0, edge_rows)

    def below_0():
        below_arrives(to_down, to_up, down_0, edge_rows)

    side_weights = []

    def paired(j, kron, left, right, at):
        i = order[j]
        for s in range(2):
            y = dot(left[i, s], kron_ref[kron]).astype(BF16)
            gram_ref[at, s] = dot(y, right[i, s])

    for j in range(cols):
        if j == cols - 1:
            @pl.when(far_up)
            def _():
                below_0()
                near_ref[...] = down_0[...]

            @pl.when(far_down)
            def _():
                above_0()
                near_ref[...] = up_0[...]

            n_sides = sides_arrive(sides_0, side_0, n_sides, [edge_sides])
            near_rows = rounded(near_ref[...])
            near_weights = [
                (by_minor(near_rows, order[n]), by_major(near_rows, cols + order[n]))
                for n in range(cols)
            ]
        v_sides = rounded(n_sides[0]) if j == cols - 1 else rounded(jnp.where(
            from_left | from_right, edge_sides, n_sides[0]
        ))
        i = order[j]
        w_left, w_right = by_major(v_sides, i), by_minor(v_sides, cols + i)
        side_weights.append((w_left, w_right))
        build_kron(kron_ref, 2 * j, w_left, w_right)
        paired(j, 2 * j, x2_ref, x2t_ref, 2 * j)

    def up_legs(weight, j):
        return kinds_of([reduce_major(gram_ref[2 * j, s], weight) for s in range(2)])

    def down_legs(weight, j):
        return kinds_of([reduce_minor(gram_ref[2 * j, s], weight) for s in range(2)])

    def ship(buffer, values):
        for k in range(2):
            buffer[k * D : (k + 1) * D] = values[k]

    def ordered(above, below, kind):
        return placed(
            [(order[j], above[j][kind]) for j in range(cols)]
            + [(cols + order[j], below[j][kind]) for j in range(cols)]
        )

    nothing = [[jnp.zeros((D, LANES), F32)] * 2] * cols
    up_far = copy(send_f1, down_1, 1, 0, {"tile": tile - 1})
    up_near = copy(send_v1, down_1, 1, 0, {"tile": tile - 1})
    down_far = copy(send_f1, up_1, 1, 1, {"tile": tile + 1})
    down_near = copy(send_v1, up_1, 1, 1, {"tile": tile + 1})

    @pl.when(far_up)
    def _():
        legs_up = minors([up_legs(near_weights[j][1], j) for j in range(cols)])
        ship(send_f1, normalised([ordered(nothing, legs_up, k) for k in range(2)]))

        @pl.when(has_up)
        def _():
            up_far.start()

    @pl.when(far_down)
    def _():
        legs_down = majors([down_legs(near_weights[j][0], j) for j in range(cols)])
        ship(send_f1, normalised([ordered(legs_down, nothing, k) for k in range(2)]))

        @pl.when(has_down)
        def _():
            down_far.start()

    @pl.when(far_up)
    def _():
        above_0()

    @pl.when(far_down)
    def _():
        below_0()

    v_rows = rounded(joined_rows(up_0[...], down_0[...])[0])
    weights = []
    for j in range(cols):
        i = order[j]
        weights.append((by_minor(v_rows, i), by_major(v_rows, cols + i)))

    def horizontal_gram(j):
        build_kron(kron_ref, 2 * j + 1, weights[j][1], weights[j][0])
        paired(j, 2 * j + 1, x2t_ref, x2_ref, 2 * j + 1)

    def horizontal(j):
        w_left, w_right = side_weights[j]
        left = kinds_of([reduce_minor(gram_ref[2 * j + 1, s], w_right) for s in range(2)])
        right = kinds_of([reduce_major(gram_ref[2 * j + 1, s], w_left) for s in range(2)])
        return left, right

    horizontal_gram(cols - 1)
    left, right = horizontal(cols - 1)
    (left,), (right,) = majors([left]), minors([right])
    ship(send_s1, normalised([jnp.where(from_left, right[k], left[k]) for k in range(2)]))
    sides_1 = copy(send_s1, side_1, 1, 2, {"group": 1 - group})
    sides_1.start()
    @pl.when(far_up)
    def _():
        for j in range(cols - 1):
            horizontal_gram(j)
        near = majors([down_legs(weights[j][0], j) for j in range(cols)])
        ship(send_v1, normalised([ordered(near, nothing, k) for k in range(2)]))

        @pl.when(has_down)
        def _():
            down_near.start()

    @pl.when(far_down)
    def _():
        for j in range(cols - 1):
            horizontal_gram(j)
        near = minors([up_legs(weights[j][1], j) for j in range(cols)])
        ship(send_v1, normalised([ordered(nothing, near, k) for k in range(2)]))

        @pl.when(has_up)
        def _():
            up_near.start()

    half = cols * D
    swapped = jnp.where(
        slot < cols, lane + half, jnp.where(slot < 2 * cols, lane - half, lane)
    )
    o_rows = [
        pick(send_f1[k * D : (k + 1) * D] + send_v1[k * D : (k + 1) * D], swapped)
        for k in range(2)
    ]
    others = [horizontal(j) for j in range(cols - 1)]
    lefts = majors([o[0] for o in others]) + [left]
    rights = minors([o[1] for o in others]) + [right]

    def own_sides(kind):
        base = placed(
            [(order[j], lefts[j][kind]) for j in range(cols)]
            + [(cols + order[j], rights[j][kind]) for j in range(cols)]
        )
        base = jnp.where((slot == 2 * cols) & (group == groups - 1), lefts[-1][kind], base)
        return jnp.where((slot == 2 * cols + 1) & (group == 0), rights[-1][kind], base)

    def other_sides(kind):
        entries = []
        for j, i in enumerate(order):
            entries.append((jnp.where(i == 0, -1, cols + i - 1), lefts[j][kind]))
            entries.append((jnp.where(i == cols - 1, -1, i + 1), rights[j][kind]))
        return placed(entries)

    o_sides = normalised([own_sides(k) for k in range(2)])
    n_sides = normalised([other_sides(k) for k in range(2)])
    for s, weight in enumerate(bond_weights(*[o + n for o, n in zip(o_sides, n_sides)])):
        inner_ref[s] = rounded(weight)
    zero = jnp.zeros((D, LANES), F32)
    n_sides = sides_arrive(sides_1, side_1, n_sides, [edge_sides, zero])
    rows_edges = jnp.concatenate([edge_rows, zero], axis=0)
    above_arrives(up_near, down_near, up_1, rows_edges)
    below_arrives(down_near, up_near, down_1, rows_edges)
    n_rows = joined_rows(up_1[...], down_1[...])
    for k in range(2):
        env_ref[k] = jnp.where(
            slot < 2 * cols, o_rows[k] + n_rows[k], o_sides[k] + n_sides[k]
        )
    mout_ref[0] = n_rows[0]
    mout_ref[1] = n_sides[0]


def gates_kernel(tiles, groups, cols, D, ax_ref, env_ref, inner_ref, in_ref, out_hbm, mout_hbm,
                 kron_ref, out_ref, mout_ref, store_sem):
    tile = lax.axis_index("tile")
    group = lax.axis_index("group")
    DD = D * D
    shift = D.bit_length() - 1
    halves = DD // LANES
    mixed = 2 * halves
    rows = DD // mixed
    lane = iota((D, LANES), 1)
    row = iota((D, LANES), 0)
    inner = lane & (D - 1)
    start = lane - inner
    slot = lane >> shift

    unit = jnp.where(inner == row, 1.0, 0.0).astype(F32)
    at_edge = (
        ((slot < cols) & (tile == 0))
        | ((slot >= cols) & (slot < 2 * cols) & (tile == tiles - 1))
        | ((slot == 2 * cols) & (group == 0))
        | ((slot == 2 * cols + 1) & (group == groups - 1))
    )
    late = [
        jnp.where(at_edge, unit, w).astype(BF16).astype(F32)
        for w in bond_weights(env_ref[0], env_ref[1])
    ]
    early = [inner_ref[s] for s in range(2)]

    unfold_mask = slot == (row & (LANES // D - 1))
    flat_rows = []
    for m in range(4 * cols):
        at = m // 4 + (cols if m % 4 >= 2 else 0)
        tiled = jnp.where(unfold_mask, pick(in_ref[m % 2], inner + at * D), 0.0)
        step = D // halves
        flat_rows.append(
            jnp.concatenate(
                [
                    jnp.sum(tiled[h * step : (h + 1) * step], axis=0, keepdims=True)
                    for h in range(halves)
                ],
                axis=1,
            )
        )
    mout_ref[...] = jnp.concatenate(flat_rows, axis=0).reshape(cols, 4, DD)
    store_msg = pltpu.make_async_copy(mout_ref, mout_hbm, store_sem.at[cols])
    store_msg.start()

    def by_major(value, m):
        return jnp.concatenate(
            [pick(value, m * D + slot + h * (LANES // D)) for h in range(halves)], axis=1
        )

    def by_minor(value, m):
        part = pick(value, m * D + inner)
        return jnp.concatenate([part] * halves, axis=1)

    scatter = unmixing(D, mixed, 1)
    stores = [
        pltpu.make_async_copy(out_ref.at[i], out_hbm.at[i], store_sem.at[i]) for i in range(cols)
    ]

    for i in range(cols):
        for s in range(2):
            left = by_major(late[s], 2 * cols) if i == 0 else by_major(early[s], i)
            right = (
                by_minor(late[s], 2 * cols + 1) if i == cols - 1 else by_minor(early[s], i + 1)
            )
            at = (i * 2 + s) * 2
            down = math.cosh(FIELD) * by_major(late[s], cols + i)
            build_kron(kron_ref, at, down, right)
            build_kron(kron_ref, at + 1, left, by_minor(late[s], i))
    gated = [
        [dot_nt(ax_ref[i, s], kron_ref[(i * 2 + s) * 2]).astype(BF16) for s in range(2)]
        for i in range(cols)
    ]
    gated = [
        [dot(kron_ref[(i * 2 + s) * 2 + 1], gated[i][s]).astype(BF16) for s in range(2)]
        for i in range(cols)
    ]

    def emit(i, gated):
        for b in range(0, mixed, 2):
            block = jnp.concatenate(
                [
                    jnp.concatenate(
                        [
                            gated[g % 2][
                                (b + c) * rows : (b + c + 1) * rows,
                                (g // 2) * LANES : (g // 2 + 1) * LANES,
                            ]
                            for c in range(2)
                        ],
                        axis=1,
                    )
                    for g in range(mixed)
                ],
                axis=0,
            )
            done = dot(scatter, block).astype(BF16)
            for c in range(2):
                for u in range(D):
                    at = u * D * mixed + (b + c) * D
                    out_ref[i, at : at + D, :] = done[
                        u * D : (u + 1) * D, c * LANES : (c + 1) * LANES
                    ]
        stores[i].start()

    for i in range(cols):
        emit(i, gated[i])
    for store in stores + [store_msg]:
        store.wait()


def per_device(tiles, groups, site_tensors, msg_in):
    _, cols, _, size = site_tensors.shape
    DD = msg_in.shape[-1]
    D = math.isqrt(DD)
    chunks = size // LANES
    a = site_tensors.reshape(cols, 2, chunks, LANES).transpose(0, 2, 1, 3)
    a = a.reshape(cols, 2 * chunks, LANES)
    vmem = pl.BlockSpec(memory_space=pltpu.VMEM)
    hbm = pl.BlockSpec(memory_space=pltpu.HBM)
    gated, env, inner, stacked = pl.pallas_call(
        functools.partial(messages_kernel, tiles, groups, cols, D),
        out_shape=(
            jax.ShapeDtypeStruct((cols, 2, DD, DD), BF16),
            jax.ShapeDtypeStruct((2, D, LANES), F32),
            jax.ShapeDtypeStruct((2, D, LANES), F32),
            jax.ShapeDtypeStruct((2, D, LANES), F32),
        ),
        in_specs=[hbm, hbm],
        out_specs=(vmem, vmem, vmem, vmem),
        scratch_shapes=[
            pltpu.VMEM(a.shape, BF16),
            pltpu.VMEM((cols, 4, DD), F32),
            pltpu.VMEM((D, LANES), F32),
            pltpu.VMEM((cols, 2, DD, DD), BF16),
            pltpu.VMEM((cols, 2, DD, DD), BF16),
            pltpu.VMEM((cols, 2, DD, DD), BF16),
            pltpu.VMEM((cols, 2, DD, DD), BF16),
            pltpu.VMEM((2 * cols, DD, DD), BF16),
            pltpu.VMEM((2 * cols, 2, DD, DD), F32),
        ]
        + [
            pltpu.VMEM(((1 + turn) * D, LANES), F32) for _ in range(6) for turn in range(ITERS)
        ]
        + [
            pltpu.SemaphoreType.DMA((ITERS, 3)),
            pltpu.SemaphoreType.DMA((ITERS, 3)),
            pltpu.SemaphoreType.DMA((cols + 1,)),
        ],
        compiler_params=pltpu.CompilerParams(
            collective_id=0, has_side_effects=True, vmem_limit_bytes=24 * 2**20
        ),
    )(
        pltpu.with_memory_space_constraint(a, pltpu.HBM),
        pltpu.with_memory_space_constraint(msg_in[0], pltpu.HBM),
    )
    out, messages = pl.pallas_call(
        functools.partial(gates_kernel, tiles, groups, cols, D),
        out_shape=(
            jax.ShapeDtypeStruct(a.shape, BF16),
            jax.ShapeDtypeStruct((cols, 4, DD), F32),
        ),
        in_specs=[vmem, vmem, vmem, vmem],
        out_specs=(hbm, hbm),
        scratch_shapes=[
            pltpu.VMEM((4 * cols, DD, DD), BF16),
            pltpu.VMEM(a.shape, BF16),
            pltpu.VMEM((cols, 4, DD), F32),
            pltpu.SemaphoreType.DMA((cols + 1,)),
        ],
        compiler_params=pltpu.CompilerParams(vmem_limit_bytes=24 * 2**20),
    )(gated, env, inner, stacked)
    out = out.reshape(cols, chunks, 2, LANES).transpose(0, 2, 1, 3)
    return out.reshape(1, cols, 2, size), messages[None]


def solution(mesh):
    spec = P("tile", "group", None, None)
    return jax.shard_map(
        functools.partial(per_device, mesh.shape["tile"], mesh.shape["group"]),
        mesh=mesh, in_specs=(spec, spec), out_specs=(spec, spec), check_vma=False,
    )
```

```python
import functools
import math

import jax
import jax.numpy as jnp
from jax import lax
from jax.experimental import pallas as pl
from jax.experimental.pallas import tpu as pltpu
from jax.sharding import PartitionSpec as P

ITERS = 2
NS_STEPS = 6
EARLY_STEPS = 3
LANES = 128
EPSILON = 1e-06
COUPLING = 0.5
FIELD = 0.3
F32 = jnp.float32
BF16 = jnp.bfloat16
MESH = pl.DeviceIdType.MESH


def iota(shape, axis):
    return lax.broadcasted_iota(jnp.int32, shape, axis)


def dot(a, b):
    return jnp.dot(a, b, preferred_element_type=F32)


def dot_nt(a, b):
    return lax.dot_general(a, b, (((1,), (1,)), ((), ())), preferred_element_type=F32)


def dot_tn(a, b):
    return lax.dot_general(a, b, (((0,), (0,)), ((), ())), preferred_element_type=F32)


def parts(value, count):
    out = []
    for _ in range(count):
        piece = value.astype(BF16)
        out.append(piece)
        value = value - piece.astype(F32)
    return out


def select_dot(value, selector, count):
    total = None
    for piece in parts(value, count):
        term = dot(piece, selector)
        total = term if total is None else total + term
    return total


def one_hot(mask):
    return jnp.where(mask, 1.0, 0.0).astype(BF16)


def build_kron(kron_ref, slot, first, second):
    D = first.shape[0]
    for d in range(D):
        kron_ref[slot, d * D : (d + 1) * D, :] = (first[d : d + 1, :] * second).astype(BF16)


def pick(value, index):
    return jnp.take_along_axis(value, index, axis=1, mode="promise_in_bounds")


def row_of(value, k):
    return jnp.broadcast_to(value[k : k + 1, :], value.shape)


def bond_open(msg_sum, twist_sum):
    D = msg_sum.shape[0]
    lane = iota((D, LANES), 1)
    row = iota((D, LANES), 0)
    inner = lane & (D - 1)
    turned = lane - inner + row
    g0, g1 = math.cosh(COUPLING), math.sinh(COUPLING)
    cross = math.sqrt(g0 * g1)
    root2 = math.sqrt(2.0)
    halves = [
        ((g0 * msg_sum + cross * twist_sum) / root2).astype(BF16).astype(F32),
        ((cross * twist_sum + g1 * msg_sum) / root2).astype(BF16).astype(F32),
    ]
    squares = halves[0] * halves[0] + halves[1] * halves[1]
    squares = jnp.broadcast_to(jnp.sum(squares, axis=0, keepdims=True), (D, LANES))
    trace = jnp.sum(pick(squares, turned), axis=0, keepdims=True) + EPSILON

    gram = None
    rotated = []
    for half in halves:
        transposed = None
        for k in range(D):
            own = row_of(half, k)
            column = pick(own, turned)
            term = column * own
            gram = term if gram is None else gram + term
            placed = jnp.where(inner == k, column, 0.0)
            transposed = placed if transposed is None else transposed + placed
        rotated.append(transposed)

    return gram / trace, rotated, jnp.broadcast_to(trace, (D, LANES))


def bond_tools(D):
    lane = iota((D, LANES), 1)
    row = iota((D, LANES), 0)
    inner = lane & (D - 1)
    turned = lane - inner + row
    unit = jnp.where(inner == row, 1.0, 0.0).astype(F32)

    def columns(value):
        return [pick(row_of(value, k), turned) for k in range(D)]

    def times(left, right):
        sums = [None] * 4
        for k in range(D):
            term = left[k] * row_of(right, k)
            sums[k % 4] = term if sums[k % 4] is None else sums[k % 4] + term
        return (sums[0] + sums[1]) + (sums[2] + sums[3])

    return unit, columns, times


def bond_step(state, rotated):
    unit, columns, times = bond_tools(state.shape[0])
    left = columns(state)
    square = times(left, state)
    rotated = [1.5 * v - 0.5 * times(left, v) for v in rotated]
    state = times(left, 2.25 * unit - 1.5 * state + 0.25 * square)
    return state, rotated


def bond_close(state, rotated, trace):
    _, columns, times = bond_tools(state.shape[0])
    left = columns(state)
    rotated = [1.5 * v - 0.5 * times(left, v) for v in rotated]
    again = rotated
    for _ in range(2):
        again = [1.5 * v - 0.5 * times(left, v) for v in again]
    rotated = [1.5 * v - 0.5 * times(left, w) for v, w in zip(rotated, again)]
    scale = 1.0 / jnp.sqrt(trace)
    first = math.sqrt(math.cosh(COUPLING)) * rotated[0] * scale
    second = math.sqrt(math.sinh(COUPLING)) * rotated[1] * scale
    return [first + second, first - second]


def unmixing(D, mixed, out_axis):
    DD = D * D
    sub = D // mixed
    p, k = iota((DD, DD), out_axis), iota((DD, DD), 1 - out_axis)
    low = p & (D - 1)
    mid = (p >> (D.bit_length() - 1)) & (sub - 1)
    top = p >> (D * sub).bit_length() - 1
    return one_hot(k == low * D + mid * mixed + top)


def messages_kernel(tiles, groups, cols, D, a_hbm, msg_hbm, ax_ref, env_ref, inner_ref, mout_ref,
           a_ref, msg_ref, near_ref, x_ref, xt_ref, x2_ref, x2t_ref, kron_ref, gram_ref,
           send_v0, send_v1, send_s0, send_s1, _, send_f1, up_0, up_1, down_0, down_1, side_0, side_1,
           send_sem, recv_sem, load_sem):
    loads = [pltpu.make_async_copy(msg_hbm, msg_ref, load_sem.at[cols])]
    loads += [
        pltpu.make_async_copy(a_hbm.at[i], a_ref.at[i], load_sem.at[i]) for i in range(cols)
    ]
    for load in loads:
        load.start()
    tile = lax.axis_index("tile")
    group = lax.axis_index("group")
    DD = D * D
    shift = D.bit_length() - 1
    halves = DD // LANES
    mixed = 2 * halves
    sub = D // mixed
    per = LANES // D
    legs = 4 * cols
    crossing = jnp.where(group == 0, cols - 1, 0)
    closed = jnp.where(group == 0, 0, cols - 1)
    order = list(range(1, cols - 1)) + [closed, crossing]
    has_up = tile > 0
    has_down = tile < tiles - 1

    barrier = pltpu.get_barrier_semaphore()

    @pl.when(has_up)
    def _():
        pl.semaphore_signal(barrier, inc=1, device_id={"tile": tile - 1}, device_id_type=MESH)

    @pl.when(has_down)
    def _():
        pl.semaphore_signal(barrier, inc=1, device_id={"tile": tile + 1}, device_id_type=MESH)

    pl.semaphore_signal(barrier, inc=1, device_id={"group": 1 - group}, device_id_type=MESH)

    lane = iota((D, LANES), 1)
    row = iota((D, LANES), 0)
    within = lane & (D - 1)
    turned = lane - within + row
    slot = lane >> shift
    gather = unmixing(D, mixed, 0)
    fold_minor = one_hot((iota((LANES, LANES), 0) & (D - 1)) == (iota((LANES, LANES), 1) & (D - 1)))
    fold_major = one_hot((iota((DD, LANES), 0) >> shift) == (iota((DD, LANES), 1) & (D - 1)))

    def placed(entries):
        total = jnp.zeros((D, LANES), F32)
        for where, value in entries:
            total = jnp.where(slot == where, value, total)
        return total

    def by_major(value, m):
        return jnp.concatenate([pick(value, m * D + slot + h * per) for h in range(halves)], axis=1)

    def by_minor(value, m):
        return jnp.concatenate([pick(value, m * D + within)] * halves, axis=1)

    def rounded(value):
        return value.astype(BF16).astype(F32)

    def reduce_major(gram, weight):
        total = gram[:D] * weight[0:1, :]
        for d in range(1, D):
            total = total + gram[d * D : (d + 1) * D] * weight[d : d + 1, :]
        return total

    sublane = iota((8, DD), 0)

    def reduce_minor(gram, weight):
        blocks = []
        for d in range(D):
            block = gram[d * D : (d + 1) * D] * weight
            total = block[:8]
            for h in range(1, D // 8):
                total = total + block[h * 8 : (h + 1) * 8]
            blocks.append(total)
        out = []
        for base in range(0, D, 8):
            level = blocks[base : base + 8]
            step = 1
            while len(level) > 1:
                low = (sublane & step) == 0
                level = [
                    jnp.where(low, level[n], level[n + 1])
                    + pltpu.roll(jnp.where(low, level[n + 1], level[n]), step, 0)
                    for n in range(0, len(level), 2)
                ]
                step *= 2
            out.append(level[0])
        return jnp.concatenate(out, axis=0)

    def kinds_of(totals):
        if len(totals) == 1:
            return totals
        return [totals[0] + totals[1], totals[0] - totals[1]]

    def folded(totals, selector):
        pieces = []
        for total in totals:
            if selector is fold_minor:
                joined = total[:, :LANES]
                for h in range(1, halves):
                    joined = joined + total[:, h * LANES : (h + 1) * LANES]
                total = joined
            pieces += parts(total, 2)
        out = dot(jnp.concatenate(pieces, axis=0), selector)
        return [
            out[2 * n * D : (2 * n + 1) * D] + out[(2 * n + 1) * D : (2 * n + 2) * D]
            for n in range(len(totals))
        ]

    def minors(totals):
        count = len(totals[0])
        flat = folded([v for t in totals for v in t], fold_minor)
        return [flat[n * count : (n + 1) * count] for n in range(len(totals))]

    def majors(totals):
        count = len(totals[0])
        flat = folded([v for t in totals for v in t], fold_major)
        return [flat[n * count : (n + 1) * count] for n in range(len(totals))]

    def normalised(values):
        power = jnp.sum(values[0] * values[0], axis=0, keepdims=True)
        power = pick(jnp.broadcast_to(power, (D, LANES)), turned)
        power = jnp.sum(power, axis=0, keepdims=True) / DD
        scale = 1.0 / jnp.sqrt(power + EPSILON)
        return [v * scale for v in values]

    def upright(ups, downs, kind):
        return placed(
            [(i, ups[i][kind]) for i in range(cols)]
            + [(cols + i, downs[i][kind]) for i in range(cols)]
        )

    def copy(src, dst, turn, k, device):
        return pltpu.make_async_remote_copy(
            src_ref=src, dst_ref=dst, send_sem=send_sem.at[turn, k],
            recv_sem=recv_sem.at[turn, k], device_id=device, device_id_type=MESH,
        )

    def above_arrives(sent, arriving, dst, edges):
        @pl.when(has_up)
        def _():
            sent.wait_send()
            arriving.wait_recv()

        @pl.when(jnp.logical_not(has_up))
        def _():
            dst[...] = edges

    def below_arrives(sent, arriving, dst, edges):
        @pl.when(has_down)
        def _():
            sent.wait_send()
            arriving.wait_recv()

        @pl.when(jnp.logical_not(has_down))
        def _():
            dst[...] = edges

    def joined_rows(above, below):
        return [
            jnp.where(slot < cols, above[k * D : (k + 1) * D], below[k * D : (k + 1) * D])
            for k in range(above.shape[0] // D)
        ]

    from_left = (slot == 0) | (slot == 2 * cols)
    from_right = (slot == 2 * cols - 1) | (slot == 2 * cols + 1)

    def sides_arrive(to_side, dst, local, edges):
        to_side.wait()
        got = dst[...]
        out = []
        for k, (value, edge) in enumerate(zip(local, edges)):
            other = got[k * D : (k + 1) * D]
            value = jnp.where(from_left, jnp.where(group == 0, edge, other), value)
            out.append(
                jnp.where(from_right, jnp.where(group == groups - 1, edge, other), value)
            )
        return out

    loads[0].wait()
    spot = (row & (per - 1)) * D + within
    flat = msg_ref[...].reshape(legs, DD)

    def unfolded(m):
        source = jnp.concatenate(
            [
                jnp.broadcast_to(flat[m : m + 1, h * LANES : (h + 1) * LANES], (per, LANES))
                for h in range(halves)
            ],
            axis=0,
        )
        return pick(source, spot)

    singles = [unfolded(m) for m in range(legs)]
    edge_rows = placed(
        [(i, singles[4 * i]) for i in range(cols)]
        + [(cols + i, singles[4 * i + 2]) for i in range(cols)]
    )
    edge_sides = placed(
        [(i, singles[4 * i + 1]) for i in range(cols)]
        + [(cols + i, singles[4 * i + 3]) for i in range(cols)]
    )

    def unmix(i):
        for b in range(0, mixed, 2):
            pair = jnp.concatenate(
                [
                    jnp.concatenate(
                        [
                            a_ref[i, u * D * mixed + (b + c) * D : u * D * mixed + (b + c + 1) * D]
                            for u in range(D)
                        ],
                        axis=0,
                    )
                    for c in range(2)
                ],
                axis=1,
            )
            block = dot(gather, pair).astype(BF16)
            span = sub * D
            for c in range(2):
                for g in range(mixed):
                    x_ref[
                        i,
                        g % 2,
                        (b + c) * span : (b + c + 1) * span,
                        (g // 2) * LANES : (g // 2 + 1) * LANES,
                    ] = block[g * span : (g + 1) * span, c * LANES : (c + 1) * LANES]

    def relayout(i, s):
        for h in range(halves):
            for lh in range(halves):
                values = [
                    x_ref[
                        i, s, (lh * per + k) * D : (lh * per + k + 1) * D,
                        h * LANES : (h + 1) * LANES,
                    ]
                    for k in range(per)
                ]
                step = 1
                while step < per:
                    high = (slot & step) != 0
                    out = list(values)
                    for a in range(per):
                        if a & step:
                            continue
                        b = a | step
                        low_up = pltpu.roll(values[b], D * step, 1)
                        high_down = pltpu.roll(values[a], LANES - D * step, 1)
                        out[a] = jnp.where(high, low_up, values[a])
                        out[b] = jnp.where(high, values[b], high_down)
                    values = out
                    step *= 2
                for d in range(per):
                    x2_ref[
                        i, s, (h * per + d) * D : (h * per + d + 1) * D,
                        lh * LANES : (lh + 1) * LANES,
                    ] = values[d]
        x2t_ref[i, s] = x2_ref[i, s].T

    v_rows, v_sides = rounded(edge_rows), rounded(edge_sides)
    weights = []
    for i in range(cols):
        w_up, w_down = by_minor(v_rows, i), by_major(v_rows, cols + i)
        w_left, w_right = by_major(v_sides, i), by_minor(v_sides, cols + i)
        weights.append((w_up, w_down, w_left, w_right))
        build_kron(kron_ref, 2 * i, w_down, w_right)
        build_kron(kron_ref, 2 * i + 1, w_left, w_up)
    for load in loads[1:]:
        load.wait()
    for i in range(cols):
        unmix(i)
    for i in range(cols):
        for s in range(2):
            xt_ref[i, s] = x_ref[i, s].T
    sides_of = ((x_ref, xt_ref), (xt_ref, x_ref))

    def first_gram(path, i):
        left, right = sides_of[path]
        y = [dot(left[i, s], kron_ref[2 * i + path]).astype(BF16) for s in range(2)]
        gram_ref[2 * i + path, 0] = dot(
            jnp.concatenate(y, axis=1), right[i].reshape(2 * DD, DD)
        )

    def outer(i, leg):
        w_up, w_down, w_left, w_right = weights[i]
        if leg == 0:
            return [reduce_major(gram_ref[2 * i, 0], w_left)]
        if leg == 1:
            return [reduce_minor(gram_ref[2 * i, 0], w_up)]
        if leg == 2:
            return [reduce_minor(gram_ref[2 * i + 1, 0], w_right)]
        return [reduce_major(gram_ref[2 * i + 1, 0], w_down)]

    first_gram(0, 0)
    first_gram(1, cols - 1)
    for i in range(1, cols):
        first_gram(0, i)
    for i in range(cols - 1):
        first_gram(1, i)
    (left_first,), (right_last,) = majors([outer(0, 1)]), minors([outer(cols - 1, 3)])
    send_s0[...] = normalised([jnp.where(from_left, right_last[0], left_first[0])])[0]
    ups = [outer(i, 0) for i in range(cols)]

    mix = jnp.full((D, DD), math.tanh(FIELD), BF16)
    for i in range(cols):
        for d in range(0, DD, D):
            a0, a1 = (x_ref[i, s, d : d + D] for s in range(2))
            ax_ref[i, 0, d : d + D] = a0 + mix * a1
            ax_ref[i, 1, d : d + D] = a1 + mix * a0

    inside = jnp.logical_and(has_up, has_down)

    @pl.when(inside)
    def _():
        pl.semaphore_wait(barrier, 3)

    @pl.when(jnp.logical_not(inside))
    def _():
        pl.semaphore_wait(barrier, 2)

    sides_0 = copy(send_s0, side_0, 0, 2, {"group": 1 - group})
    sides_0.start()
    downs = majors([outer(i, 2) for i in range(cols)])
    ups = minors(ups)
    send_v0[...] = normalised([upright(downs, ups, 0)])[0]
    to_up = copy(send_v0, down_0, 0, 0, {"tile": tile - 1})
    to_down = copy(send_v0, up_0, 0, 1, {"tile": tile + 1})

    @pl.when(has_up)
    def _():
        to_up.start()

    @pl.when(has_down)
    def _():
        to_down.start()

    for i in range(cols):
        for s in range(2):
            relayout(i, s)

    lefts = [left_first] + majors([outer(i, 1) for i in range(1, cols)])
    rights = minors([outer(i, 3) for i in range(cols - 1)]) + [right_last]

    def inner_view(lefts, rights, kind):
        return placed(
            [(i, rights[i - 1][kind]) for i in range(1, cols)]
            + [(cols + i, lefts[i + 1][kind]) for i in range(cols - 1)]
        )

    n_sides = normalised([inner_view(lefts, rights, 0)])

    far_up = lax.rem(tile, 2) == 0
    far_down = jnp.logical_not(far_up)

    def above_0():
        above_arrives(to_up, to_down, up_0, edge_rows)

    def below_0():
        below_arrives(to_down, to_up, down_0, edge_rows)

    side_weights = []

    def paired(j, kron, left, right, at):
        i = order[j]
        for s in range(2):
            y = dot(left[i, s], kron_ref[kron]).astype(BF16)
            gram_ref[at, s] = dot(y, right[i, s])

    for j in range(cols):
        if j == cols - 1:
            @pl.when(far_up)
            def _():
                below_0()
                near_ref[...] = down_0[...]

            @pl.when(far_down)
            def _():
                above_0()
                near_ref[...] = up_0[...]

            n_sides = sides_arrive(sides_0, side_0, n_sides, [edge_sides])
            near_rows = rounded(near_ref[...])
            near_weights = [
                (by_minor(near_rows, order[n]), by_major(near_rows, cols + order[n]))
                for n in range(cols)
            ]
        v_sides = rounded(n_sides[0]) if j == cols - 1 else rounded(jnp.where(
            from_left | from_right, edge_sides, n_sides[0]
        ))
        i = order[j]
        w_left, w_right = by_major(v_sides, i), by_minor(v_sides, cols + i)
        side_weights.append((w_left, w_right))
        build_kron(kron_ref, 2 * j, w_left, w_right)
        paired(j, 2 * j, x2_ref, x2t_ref, 2 * j)

    def up_legs(weight, j):
        return kinds_of([reduce_major(gram_ref[2 * j, s], weight) for s in range(2)])

    def down_legs(weight, j):
        return kinds_of([reduce_minor(gram_ref[2 * j, s], weight) for s in range(2)])

    def ship(buffer, values):
        for k in range(2):
            buffer[k * D : (k + 1) * D] = values[k]

    def ordered(above, below, kind):
        return placed(
            [(order[j], above[j][kind]) for j in range(cols)]
            + [(cols + order[j], below[j][kind]) for j in range(cols)]
        )

    nothing = [[jnp.zeros((D, LANES), F32)] * 2] * cols
    up_far = copy(send_f1, down_1, 1, 0, {"tile": tile - 1})
    up_near = copy(send_v1, down_1, 1, 0, {"tile": tile - 1})
    down_far = copy(send_f1, up_1, 1, 1, {"tile": tile + 1})
    down_near = copy(send_v1, up_1, 1, 1, {"tile": tile + 1})

    @pl.when(far_up)
    def _():
        legs_up = minors([up_legs(near_weights[j][1], j) for j in range(cols)])
        ship(send_f1, normalised([ordered(nothing, legs_up, k) for k in range(2)]))

        @pl.when(has_up)
        def _():
            up_far.start()

    @pl.when(far_down)
    def _():
        legs_down = majors([down_legs(near_weights[j][0], j) for j in range(cols)])
        ship(send_f1, normalised([ordered(legs_down, nothing, k) for k in range(2)]))

        @pl.when(has_down)
        def _():
            down_far.start()

    @pl.when(far_up)
    def _():
        above_0()

    @pl.when(far_down)
    def _():
        below_0()

    v_rows = rounded(joined_rows(up_0[...], down_0[...])[0])
    weights = []
    for j in range(cols):
        i = order[j]
        weights.append((by_minor(v_rows, i), by_major(v_rows, cols + i)))

    def horizontal_gram(j):
        build_kron(kron_ref, 2 * j + 1, weights[j][1], weights[j][0])
        paired(j, 2 * j + 1, x2t_ref, x2_ref, 2 * j + 1)

    def horizontal(j):
        w_left, w_right = side_weights[j]
        left = kinds_of([reduce_minor(gram_ref[2 * j + 1, s], w_right) for s in range(2)])
        right = kinds_of([reduce_major(gram_ref[2 * j + 1, s], w_left) for s in range(2)])
        return left, right

    horizontal_gram(cols - 1)
    left, right = horizontal(cols - 1)
    (left,), (right,) = majors([left]), minors([right])
    ship(send_s1, normalised([jnp.where(from_left, right[k], left[k]) for k in range(2)]))
    sides_1 = copy(send_s1, side_1, 1, 2, {"group": 1 - group})
    sides_1.start()
    @pl.when(far_up)
    def _():
        for j in range(cols - 1):
            horizontal_gram(j)
        near = majors([down_legs(weights[j][0], j) for j in range(cols)])
        ship(send_v1, normalised([ordered(near, nothing, k) for k in range(2)]))

        @pl.when(has_down)
        def _():
            down_near.start()

    @pl.when(far_down)
    def _():
        for j in range(cols - 1):
            horizontal_gram(j)
        near = minors([up_legs(weights[j][1], j) for j in range(cols)])
        ship(send_v1, normalised([ordered(nothing, near, k) for k in range(2)]))

        @pl.when(has_up)
        def _():
            up_near.start()

    half = cols * D
    swapped = jnp.where(
        slot < cols, lane + half, jnp.where(slot < 2 * cols, lane - half, lane)
    )
    o_rows = [
        pick(send_f1[k * D : (k + 1) * D] + send_v1[k * D : (k + 1) * D], swapped)
        for k in range(2)
    ]
    others = [horizontal(j) for j in range(cols - 1)]
    lefts = majors([o[0] for o in others]) + [left]
    rights = minors([o[1] for o in others]) + [right]

    def own_sides(kind):
        base = placed(
            [(order[j], lefts[j][kind]) for j in range(cols)]
            + [(cols + order[j], rights[j][kind]) for j in range(cols)]
        )
        base = jnp.where((slot == 2 * cols) & (group == groups - 1), lefts[-1][kind], base)
        return jnp.where((slot == 2 * cols + 1) & (group == 0), rights[-1][kind], base)

    def other_sides(kind):
        entries = []
        for j, i in enumerate(order):
            entries.append((jnp.where(i == 0, -1, cols + i - 1), lefts[j][kind]))
            entries.append((jnp.where(i == cols - 1, -1, i + 1), rights[j][kind]))
        return placed(entries)

    o_sides = normalised([own_sides(k) for k in range(2)])
    n_sides = normalised([other_sides(k) for k in range(2)])
    state, rotated, trace = bond_open(*[o + n for o, n in zip(o_sides, n_sides)])
    for step in range(EARLY_STEPS):
        state, rotated = bond_step(state, rotated)
    for n, value in enumerate([state] + rotated + [trace]):
        inner_ref[n] = value
    zero = jnp.zeros((D, LANES), F32)
    n_sides = sides_arrive(sides_1, side_1, n_sides, [edge_sides, zero])
    rows_edges = jnp.concatenate([edge_rows, zero], axis=0)
    above_arrives(up_near, down_near, up_1, rows_edges)
    below_arrives(down_near, up_near, down_1, rows_edges)
    n_rows = joined_rows(up_1[...], down_1[...])
    for k in range(2):
        env_ref[k] = jnp.where(
            slot < 2 * cols, o_rows[k] + n_rows[k], o_sides[k] + n_sides[k]
        )
    mout_ref[0] = n_rows[0]
    mout_ref[1] = n_sides[0]


def gates_kernel(tiles, groups, cols, D, ax_ref, env_ref, inner_ref, in_ref, out_hbm, mout_hbm,
                 kron_ref, out_ref, mout_ref, store_sem):
    tile = lax.axis_index("tile")
    group = lax.axis_index("group")
    DD = D * D
    shift = D.bit_length() - 1
    halves = DD // LANES
    mixed = 2 * halves
    rows = DD // mixed
    lane = iota((D, LANES), 1)
    row = iota((D, LANES), 0)
    inner = lane & (D - 1)
    start = lane - inner
    slot = lane >> shift

    unit = jnp.where(inner == row, 1.0, 0.0).astype(F32)
    at_edge = (
        ((slot < cols) & (tile == 0))
        | ((slot >= cols) & (slot < 2 * cols) & (tile == tiles - 1))
        | ((slot == 2 * cols) & (group == 0))
        | ((slot == 2 * cols + 1) & (group == groups - 1))
    )
    state, rotated, trace = bond_open(env_ref[0], env_ref[1])
    begun, turning = inner_ref[0], [inner_ref[1], inner_ref[2]]
    early_left = NS_STEPS - 2 - EARLY_STEPS
    for step in range(NS_STEPS - 2):
        if step < early_left:
            begun, turning = bond_step(begun, turning)
        elif step == early_left:
            early = [
                w.astype(BF16).astype(F32) for w in bond_close(begun, turning, inner_ref[3])
            ]
        state, rotated = bond_step(state, rotated)
    late = [
        jnp.where(at_edge, unit, w).astype(BF16).astype(F32)
        for w in bond_close(state, rotated, trace)
    ]

    unfold_mask = slot == (row & (LANES // D - 1))
    flat_rows = []
    for m in range(4 * cols):
        at = m // 4 + (cols if m % 4 >= 2 else 0)
        tiled = jnp.where(unfold_mask, pick(in_ref[m % 2], inner + at * D), 0.0)
        step = D // halves
        flat_rows.append(
            jnp.concatenate(
                [
                    jnp.sum(tiled[h * step : (h + 1) * step], axis=0, keepdims=True)
                    for h in range(halves)
                ],
                axis=1,
            )
        )
    mout_ref[...] = jnp.concatenate(flat_rows, axis=0).reshape(cols, 4, DD)
    store_msg = pltpu.make_async_copy(mout_ref, mout_hbm, store_sem.at[cols])
    store_msg.start()

    def by_major(value, m):
        return jnp.concatenate(
            [pick(value, m * D + slot + h * (LANES // D)) for h in range(halves)], axis=1
        )

    def by_minor(value, m):
        part = pick(value, m * D + inner)
        return jnp.concatenate([part] * halves, axis=1)

    scatter = unmixing(D, mixed, 1)
    stores = [
        pltpu.make_async_copy(out_ref.at[i], out_hbm.at[i], store_sem.at[i]) for i in range(cols)
    ]

    for i in range(cols):
        for s in range(2):
            left = by_major(late[s], 2 * cols) if i == 0 else by_major(early[s], i)
            right = (
                by_minor(late[s], 2 * cols + 1) if i == cols - 1 else by_minor(early[s], i + 1)
            )
            at = (i * 2 + s) * 2
            down = math.cosh(FIELD) * by_major(late[s], cols + i)
            build_kron(kron_ref, at, down, right)
            build_kron(kron_ref, at + 1, left, by_minor(late[s], i))
    gated = [
        [dot_nt(ax_ref[i, s], kron_ref[(i * 2 + s) * 2]).astype(BF16) for s in range(2)]
        for i in range(cols)
    ]
    gated = [
        [dot(kron_ref[(i * 2 + s) * 2 + 1], gated[i][s]).astype(BF16) for s in range(2)]
        for i in range(cols)
    ]

    def emit(i, gated):
        for b in range(0, mixed, 2):
            block = jnp.concatenate(
                [
                    jnp.concatenate(
                        [
                            gated[g % 2][
                                (b + c) * rows : (b + c + 1) * rows,
                                (g // 2) * LANES : (g // 2 + 1) * LANES,
                            ]
                            for c in range(2)
                        ],
                        axis=1,
                    )
                    for g in range(mixed)
                ],
                axis=0,
            )
            done = dot(scatter, block).astype(BF16)
            for c in range(2):
                for u in range(D):
                    at = u * D * mixed + (b + c) * D
                    out_ref[i, at : at + D, :] = done[
                        u * D : (u + 1) * D, c * LANES : (c + 1) * LANES
                    ]
        stores[i].start()

    for i in range(cols):
        emit(i, gated[i])
    for store in stores + [store_msg]:
        store.wait()


def per_device(tiles, groups, site_tensors, msg_in):
    _, cols, _, size = site_tensors.shape
    DD = msg_in.shape[-1]
    D = math.isqrt(DD)
    chunks = size // LANES
    a = site_tensors.reshape(cols, 2, chunks, LANES).transpose(0, 2, 1, 3)
    a = a.reshape(cols, 2 * chunks, LANES)
    vmem = pl.BlockSpec(memory_space=pltpu.VMEM)
    hbm = pl.BlockSpec(memory_space=pltpu.HBM)
    gated, env, inner, stacked = pl.pallas_call(
        functools.partial(messages_kernel, tiles, groups, cols, D),
        out_shape=(
            jax.ShapeDtypeStruct((cols, 2, DD, DD), BF16),
            jax.ShapeDtypeStruct((2, D, LANES), F32),
            jax.ShapeDtypeStruct((4, D, LANES), F32),
            jax.ShapeDtypeStruct((2, D, LANES), F32),
        ),
        in_specs=[hbm, hbm],
        out_specs=(vmem, vmem, vmem, vmem),
        scratch_shapes=[
            pltpu.VMEM(a.shape, BF16),
            pltpu.VMEM((cols, 4, DD), F32),
            pltpu.VMEM((D, LANES), F32),
            pltpu.VMEM((cols, 2, DD, DD), BF16),
            pltpu.VMEM((cols, 2, DD, DD), BF16),
            pltpu.VMEM((cols, 2, DD, DD), BF16),
            pltpu.VMEM((cols, 2, DD, DD), BF16),
            pltpu.VMEM((2 * cols, DD, DD), BF16),
            pltpu.VMEM((2 * cols, 2, DD, DD), F32),
        ]
        + [
            pltpu.VMEM(((1 + turn) * D, LANES), F32) for _ in range(6) for turn in range(ITERS)
        ]
        + [
            pltpu.SemaphoreType.DMA((ITERS, 3)),
            pltpu.SemaphoreType.DMA((ITERS, 3)),
            pltpu.SemaphoreType.DMA((cols + 1,)),
        ],
        compiler_params=pltpu.CompilerParams(
            collective_id=0, has_side_effects=True, vmem_limit_bytes=24 * 2**20
        ),
    )(
        pltpu.with_memory_space_constraint(a, pltpu.HBM),
        pltpu.with_memory_space_constraint(msg_in[0], pltpu.HBM),
    )
    out, messages = pl.pallas_call(
        functools.partial(gates_kernel, tiles, groups, cols, D),
        out_shape=(
            jax.ShapeDtypeStruct(a.shape, BF16),
            jax.ShapeDtypeStruct((cols, 4, DD), F32),
        ),
        in_specs=[vmem, vmem, vmem, vmem],
        out_specs=(hbm, hbm),
        scratch_shapes=[
            pltpu.VMEM((4 * cols, DD, DD), BF16),
            pltpu.VMEM(a.shape, BF16),
            pltpu.VMEM((cols, 4, DD), F32),
            pltpu.SemaphoreType.DMA((cols + 1,)),
        ],
        compiler_params=pltpu.CompilerParams(vmem_limit_bytes=24 * 2**20),
    )(gated, env, inner, stacked)
    out = out.reshape(cols, chunks, 2, LANES).transpose(0, 2, 1, 3)
    return out.reshape(1, cols, 2, size), messages[None]


def solution(mesh):
    spec = P("tile", "group", None, None)
    return jax.shard_map(
        functools.partial(per_device, mesh.shape["tile"], mesh.shape["group"]),
        mesh=mesh, in_specs=(spec, spec), out_specs=(spec, spec), check_vma=False,
    )
```

```python
import functools
import math

import jax
import jax.numpy as jnp
from jax import lax
from jax.experimental import pallas as pl
from jax.experimental.pallas import tpu as pltpu
from jax.sharding import PartitionSpec as P

ITERS = 2
NS_STEPS = 6
EARLY_STEPS = 3
LANES = 128
EPSILON = 1e-06
COUPLING = 0.5
FIELD = 0.3
F32 = jnp.float32
BF16 = jnp.bfloat16
MESH = pl.DeviceIdType.MESH


def iota(shape, axis):
    return lax.broadcasted_iota(jnp.int32, shape, axis)


def dot(a, b):
    return jnp.dot(a, b, preferred_element_type=F32)


def dot_nt(a, b):
    return lax.dot_general(a, b, (((1,), (1,)), ((), ())), preferred_element_type=F32)


def dot_tn(a, b):
    return lax.dot_general(a, b, (((0,), (0,)), ((), ())), preferred_element_type=F32)


def parts(value, count):
    out = []
    for _ in range(count):
        piece = value.astype(BF16)
        out.append(piece)
        value = value - piece.astype(F32)
    return out


def select_dot(value, selector, count):
    total = None
    for piece in parts(value, count):
        term = dot(piece, selector)
        total = term if total is None else total + term
    return total


def one_hot(mask):
    return jnp.where(mask, 1.0, 0.0).astype(BF16)


def build_kron(kron_ref, slot, first, second):
    D = first.shape[0]
    for d in range(D):
        kron_ref[slot, d * D : (d + 1) * D, :] = (first[d : d + 1, :] * second).astype(BF16)


def pick(value, index):
    return jnp.take_along_axis(value, index, axis=1, mode="promise_in_bounds")


def row_of(value, k):
    return jnp.broadcast_to(value[k : k + 1, :], value.shape)


def bond_open(msg_sum, twist_sum):
    D = msg_sum.shape[0]
    lane = iota((D, LANES), 1)
    row = iota((D, LANES), 0)
    inner = lane & (D - 1)
    turned = lane - inner + row
    g0, g1 = math.cosh(COUPLING), math.sinh(COUPLING)
    cross = math.sqrt(g0 * g1)
    root2 = math.sqrt(2.0)
    halves = [
        ((g0 * msg_sum + cross * twist_sum) / root2).astype(BF16).astype(F32),
        ((cross * twist_sum + g1 * msg_sum) / root2).astype(BF16).astype(F32),
    ]
    squares = halves[0] * halves[0] + halves[1] * halves[1]
    squares = jnp.broadcast_to(jnp.sum(squares, axis=0, keepdims=True), (D, LANES))
    trace = jnp.sum(pick(squares, turned), axis=0, keepdims=True) + EPSILON

    gram = None
    rotated = []
    for half in halves:
        transposed = None
        for k in range(D):
            own = row_of(half, k)
            column = pick(own, turned)
            term = column * own
            gram = term if gram is None else gram + term
            placed = jnp.where(inner == k, column, 0.0)
            transposed = placed if transposed is None else transposed + placed
        rotated.append(transposed)

    return gram / trace, rotated, jnp.broadcast_to(trace, (D, LANES))


def bond_tools(D):
    lane = iota((D, LANES), 1)
    row = iota((D, LANES), 0)
    inner = lane & (D - 1)
    turned = lane - inner + row
    unit = jnp.where(inner == row, 1.0, 0.0).astype(F32)

    def columns(value):
        return [pick(row_of(value, k), turned) for k in range(D)]

    def times(left, right):
        sums = [None] * 4
        for k in range(D):
            term = left[k] * row_of(right, k)
            sums[k % 4] = term if sums[k % 4] is None else sums[k % 4] + term
        return (sums[0] + sums[1]) + (sums[2] + sums[3])

    return unit, columns, times


def bond_step(state, rotated):
    unit, columns, times = bond_tools(state.shape[0])
    left = columns(state)
    square = times(left, state)
    rotated = [1.5 * v - 0.5 * times(left, v) for v in rotated]
    state = times(left, 2.25 * unit - 1.5 * state + 0.25 * square)
    return state, rotated


def bond_close(state, rotated, trace):
    _, columns, times = bond_tools(state.shape[0])
    left = columns(state)
    rotated = [1.5 * v - 0.5 * times(left, v) for v in rotated]
    again = rotated
    for _ in range(2):
        again = [1.5 * v - 0.5 * times(left, v) for v in again]
    rotated = [1.5 * v - 0.5 * times(left, w) for v, w in zip(rotated, again)]
    scale = 1.0 / jnp.sqrt(trace)
    first = math.sqrt(math.cosh(COUPLING)) * rotated[0] * scale
    second = math.sqrt(math.sinh(COUPLING)) * rotated[1] * scale
    return [first + second, first - second]


def unmixing(D, mixed, out_axis):
    DD = D * D
    sub = D // mixed
    p, k = iota((DD, DD), out_axis), iota((DD, DD), 1 - out_axis)
    low = p & (D - 1)
    mid = (p >> (D.bit_length() - 1)) & (sub - 1)
    top = p >> (D * sub).bit_length() - 1
    return one_hot(k == low * D + mid * mixed + top)


def messages_kernel(tiles, groups, cols, D, a_hbm, msg_hbm, ax_ref, env_ref, inner_ref, mout_ref,
           a_ref, msg_ref, other_ref, x_ref, xt_ref, xq_ref, x2_ref, x2t_ref, kron_ref, gram_ref,
           send_v0, send_v1, send_s0, send_s1, _, send_f1, up_0, up_1, down_0, down_1, side_0, side_1,
           send_sem, recv_sem, load_sem):
    loads = [pltpu.make_async_copy(msg_hbm, msg_ref, load_sem.at[cols])]
    loads += [
        pltpu.make_async_copy(a_hbm.at[i], a_ref.at[i], load_sem.at[i]) for i in range(cols)
    ]
    for load in loads:
        load.start()
    tile = lax.axis_index("tile")
    group = lax.axis_index("group")
    DD = D * D
    shift = D.bit_length() - 1
    halves = DD // LANES
    mixed = 2 * halves
    sub = D // mixed
    per = LANES // D
    legs = 4 * cols
    crossing = jnp.where(group == 0, cols - 1, 0)
    closed = jnp.where(group == 0, 0, cols - 1)
    order = list(range(1, cols - 1)) + [closed, crossing]
    has_up = tile > 0
    has_down = tile < tiles - 1
    far_path = lax.rem(tile, 2)
    far_up = far_path == 0
    far_down = jnp.logical_not(far_up)
    swap_sides = far_path == group
    cross_slot = jnp.where(group == 0, cols + crossing, crossing)
    other_slot = jnp.where(group == 0, crossing, cols + crossing)

    barrier = pltpu.get_barrier_semaphore()

    @pl.when(has_up)
    def _():
        pl.semaphore_signal(barrier, inc=1, device_id={"tile": tile - 1}, device_id_type=MESH)

    @pl.when(has_down)
    def _():
        pl.semaphore_signal(barrier, inc=1, device_id={"tile": tile + 1}, device_id_type=MESH)

    pl.semaphore_signal(barrier, inc=1, device_id={"group": 1 - group}, device_id_type=MESH)

    lane = iota((D, LANES), 1)
    row = iota((D, LANES), 0)
    within = lane & (D - 1)
    turned = lane - within + row
    slot = lane >> shift
    gather = unmixing(D, mixed, 0)
    fold_minor = one_hot((iota((LANES, LANES), 0) & (D - 1)) == (iota((LANES, LANES), 1) & (D - 1)))
    fold_major = one_hot((iota((DD, LANES), 0) >> shift) == (iota((DD, LANES), 1) & (D - 1)))

    def placed(entries):
        total = jnp.zeros((D, LANES), F32)
        for where, value in entries:
            total = jnp.where(slot == where, value, total)
        return total

    def by_major(value, m):
        return jnp.concatenate([pick(value, m * D + slot + h * per) for h in range(halves)], axis=1)

    def by_minor(value, m):
        return jnp.concatenate([pick(value, m * D + within)] * halves, axis=1)

    def rounded(value):
        return value.astype(BF16).astype(F32)

    def reduce_major(gram, weight):
        total = gram[:D] * weight[0:1, :]
        for d in range(1, D):
            total = total + gram[d * D : (d + 1) * D] * weight[d : d + 1, :]
        return total

    sublane = iota((8, DD), 0)

    def reduce_minor(gram, weight):
        blocks = []
        for d in range(D):
            block = gram[d * D : (d + 1) * D] * weight
            total = block[:8]
            for h in range(1, D // 8):
                total = total + block[h * 8 : (h + 1) * 8]
            blocks.append(total)
        out = []
        for base in range(0, D, 8):
            level = blocks[base : base + 8]
            step = 1
            while len(level) > 1:
                low = (sublane & step) == 0
                level = [
                    jnp.where(low, level[n], level[n + 1])
                    + pltpu.roll(jnp.where(low, level[n + 1], level[n]), step, 0)
                    for n in range(0, len(level), 2)
                ]
                step *= 2
            out.append(level[0])
        return jnp.concatenate(out, axis=0)

    def kinds_of(totals):
        if len(totals) == 1:
            return totals
        return [totals[0] + totals[1], totals[0] - totals[1]]

    def folded(totals, selector):
        pieces = []
        for total in totals:
            if selector is fold_minor:
                joined = total[:, :LANES]
                for h in range(1, halves):
                    joined = joined + total[:, h * LANES : (h + 1) * LANES]
                total = joined
            pieces += parts(total, 2)
        out = dot(jnp.concatenate(pieces, axis=0), selector)
        return [
            out[2 * n * D : (2 * n + 1) * D] + out[(2 * n + 1) * D : (2 * n + 2) * D]
            for n in range(len(totals))
        ]

    def minors(totals):
        count = len(totals[0])
        flat = folded([v for t in totals for v in t], fold_minor)
        return [flat[n * count : (n + 1) * count] for n in range(len(totals))]

    def majors(totals):
        count = len(totals[0])
        flat = folded([v for t in totals for v in t], fold_major)
        return [flat[n * count : (n + 1) * count] for n in range(len(totals))]

    def normalised(values):
        power = jnp.sum(values[0] * values[0], axis=0, keepdims=True)
        power = pick(jnp.broadcast_to(power, (D, LANES)), turned)
        power = jnp.sum(power, axis=0, keepdims=True) / DD
        scale = 1.0 / jnp.sqrt(power + EPSILON)
        return [v * scale for v in values]

    def upright(ups, downs, kind):
        return placed(
            [(i, ups[i][kind]) for i in range(cols)]
            + [(cols + i, downs[i][kind]) for i in range(cols)]
        )

    def copy(src, dst, turn, k, device):
        return pltpu.make_async_remote_copy(
            src_ref=src, dst_ref=dst, send_sem=send_sem.at[turn, k],
            recv_sem=recv_sem.at[turn, k], device_id=device, device_id_type=MESH,
        )

    def above_arrives(sent, arriving, dst, edges):
        @pl.when(has_up)
        def _():
            sent.wait_send()
            arriving.wait_recv()

        @pl.when(jnp.logical_not(has_up))
        def _():
            dst[...] = edges

    def below_arrives(sent, arriving, dst, edges):
        @pl.when(has_down)
        def _():
            sent.wait_send()
            arriving.wait_recv()

        @pl.when(jnp.logical_not(has_down))
        def _():
            dst[...] = edges

    def joined_rows(above, below):
        return [
            jnp.where(slot < cols, above[k * D : (k + 1) * D], below[k * D : (k + 1) * D])
            for k in range(above.shape[0] // D)
        ]

    from_left = (slot == 0) | (slot == 2 * cols)
    from_right = (slot == 2 * cols - 1) | (slot == 2 * cols + 1)

    def joined_sides(dst, local, edges):
        got = dst[...]
        out = []
        for k, (value, edge) in enumerate(zip(local, edges)):
            other = got[k * D : (k + 1) * D]
            value = jnp.where(from_left, jnp.where(group == 0, edge, other), value)
            out.append(
                jnp.where(from_right, jnp.where(group == groups - 1, edge, other), value)
            )
        return out

    loads[0].wait()
    spot = (row & (per - 1)) * D + within
    flat = msg_ref[...].reshape(legs, DD)

    def unfolded(m):
        source = jnp.concatenate(
            [
                jnp.broadcast_to(flat[m : m + 1, h * LANES : (h + 1) * LANES], (per, LANES))
                for h in range(halves)
            ],
            axis=0,
        )
        return pick(source, spot)

    singles = [unfolded(m) for m in range(legs)]
    edge_rows = placed(
        [(i, singles[4 * i]) for i in range(cols)]
        + [(cols + i, singles[4 * i + 2]) for i in range(cols)]
    )
    edge_sides = placed(
        [(i, singles[4 * i + 1]) for i in range(cols)]
        + [(cols + i, singles[4 * i + 3]) for i in range(cols)]
    )

    def unmix(i):
        for b in range(0, mixed, 2):
            pair = jnp.concatenate(
                [
                    jnp.concatenate(
                        [
                            a_ref[i, u * D * mixed + (b + c) * D : u * D * mixed + (b + c + 1) * D]
                            for u in range(D)
                        ],
                        axis=0,
                    )
                    for c in range(2)
                ],
                axis=1,
            )
            block = dot(gather, pair).astype(BF16)
            span = sub * D
            for c in range(2):
                for g in range(mixed):
                    x_ref[
                        i,
                        g % 2,
                        (b + c) * span : (b + c + 1) * span,
                        (g // 2) * LANES : (g // 2 + 1) * LANES,
                    ] = block[g * span : (g + 1) * span, c * LANES : (c + 1) * LANES]

    def exchanged(values, masks, unit_lanes):
        step = 1
        for high in masks:
            out = list(values)
            for a in range(len(values)):
                if a & step:
                    continue
                b = a | step
                low_up = pltpu.roll(values[b], unit_lanes * step, 1)
                high_down = pltpu.roll(values[a], LANES - unit_lanes * step, 1)
                out[a] = jnp.where(high[0], low_up, values[a])
                out[b] = jnp.where(high[1], values[b], high_down)
            values = out
            step *= 2
        return values

    def relayout(j, s):
        bits = per.bit_length() - 1
        masks = [((slot & (1 << n)) != 0,) * 2 for n in range(bits)]
        for h in range(halves):
            for lh in range(halves):
                values = [
                    x_ref[
                        order[j], s, (lh * per + k) * D : (lh * per + k + 1) * D,
                        h * LANES : (h + 1) * LANES,
                    ]
                    for k in range(per)
                ]
                values = exchanged(values, masks, D)
                for d in range(per):
                    x2_ref[
                        j, s, (h * per + d) * D : (h * per + d + 1) * D,
                        lh * LANES : (lh + 1) * LANES,
                    ] = values[d]
        x2t_ref[j, s] = x2_ref[j, s].T

    def cross_layout(s):
        shut = jnp.where(swap_sides, 0, 1)
        masks = []
        for n in range(shift):
            bit = (lane >> n) & 1
            masks.append(((bit & (1 - shut)) != 0, (bit | shut) != 0))
        for h in range(halves):
            values = [
                x_ref[crossing, s, k * D : (k + 1) * D, h * LANES : (h + 1) * LANES]
                for k in range(D)
            ]
            values = exchanged(values, masks, 1)
            for k in range(D):
                xq_ref[0, s, k * D : (k + 1) * D, h * LANES : (h + 1) * LANES] = values[k]
        xq_ref[1, s] = xq_ref[0, s].T

    v_rows, v_sides = rounded(edge_rows), rounded(edge_sides)
    weights = []
    for i in range(cols):
        w_up, w_down = by_minor(v_rows, i), by_major(v_rows, cols + i)
        w_left, w_right = by_major(v_sides, i), by_minor(v_sides, cols + i)
        weights.append((w_up, w_down, w_left, w_right))
        build_kron(kron_ref, 2 * i, w_down, w_right)
        build_kron(kron_ref, 2 * i + 1, w_left, w_up)
    for load in loads[1:]:
        load.wait()
    for i in range(cols):
        unmix(i)
    for i in range(cols):
        for s in range(2):
            xt_ref[i, s] = x_ref[i, s].T
    sides_of = ((x_ref, xt_ref), (xt_ref, x_ref))

    def first_gram(path, i):
        left, right = sides_of[path]
        y = [dot(left[i, s], kron_ref[2 * i + path]).astype(BF16) for s in range(2)]
        gram_ref[2 * i + path, 0] = dot(
            jnp.concatenate(y, axis=1), right[i].reshape(2 * DD, DD)
        )

    def outer(i, leg):
        w_up, w_down, w_left, w_right = weights[i]
        if leg == 0:
            return [reduce_major(gram_ref[2 * i, 0], w_left)]
        if leg == 1:
            return [reduce_minor(gram_ref[2 * i, 0], w_up)]
        if leg == 2:
            return [reduce_minor(gram_ref[2 * i + 1, 0], w_right)]
        return [reduce_major(gram_ref[2 * i + 1, 0], w_down)]

    first_gram(0, 0)
    first_gram(1, cols - 1)
    for i in range(1, cols):
        first_gram(0, i)
    for i in range(cols - 1):
        first_gram(1, i)
    (left_first,), (right_last,) = majors([outer(0, 1)]), minors([outer(cols - 1, 3)])
    send_s0[...] = normalised([jnp.where(from_left, right_last[0], left_first[0])])[0]
    ups = [outer(i, 0) for i in range(cols)]

    mix = jnp.full((D, DD), math.tanh(FIELD), BF16)
    for i in range(cols):
        for d in range(0, DD, D):
            a0, a1 = (x_ref[i, s, d : d + D] for s in range(2))
            ax_ref[i, 0, d : d + D] = a0 + mix * a1
            ax_ref[i, 1, d : d + D] = a1 + mix * a0

    inside = jnp.logical_and(has_up, has_down)

    @pl.when(inside)
    def _():
        pl.semaphore_wait(barrier, 3)

    @pl.when(jnp.logical_not(inside))
    def _():
        pl.semaphore_wait(barrier, 2)

    sides_0 = copy(send_s0, side_0, 0, 2, {"group": 1 - group})
    sides_0.start()
    downs = majors([outer(i, 2) for i in range(cols)])
    ups = minors(ups)
    send_v0[...] = normalised([upright(downs, ups, 0)])[0]
    to_up = copy(send_v0, down_0, 0, 0, {"tile": tile - 1})
    to_down = copy(send_v0, up_0, 0, 1, {"tile": tile + 1})

    @pl.when(has_up)
    def _():
        to_up.start()

    @pl.when(has_down)
    def _():
        to_down.start()

    for s in range(2):
        for j in range(cols - 1):
            relayout(j, s)
        cross_layout(s)

    lefts = [left_first] + majors([outer(i, 1) for i in range(1, cols)])
    rights = minors([outer(i, 3) for i in range(cols - 1)]) + [right_last]

    def inner_view(lefts, rights, kind):
        return placed(
            [(i, rights[i - 1][kind]) for i in range(1, cols)]
            + [(cols + i, lefts[i + 1][kind]) for i in range(cols - 1)]
        )

    n_sides = normalised([inner_view(lefts, rights, 0)])

    def above_0():
        above_arrives(to_up, to_down, up_0, edge_rows)

    def below_0():
        below_arrives(to_down, to_up, down_0, edge_rows)

    side_weights = []

    def paired(j, kron, left, right, at):
        for s in range(2):
            y = dot(left[j, s], kron_ref[kron]).astype(BF16)
            gram_ref[at, s] = dot(y, right[j, s])

    v_sides = rounded(jnp.where(from_left | from_right, edge_sides, n_sides[0]))
    for j in range(cols - 1):
        i = order[j]
        w_left, w_right = by_major(v_sides, i), by_minor(v_sides, cols + i)
        side_weights.append((w_left, w_right))
        build_kron(kron_ref, 2 * j, w_left, w_right)
        paired(j, 2 * j, x2_ref, x2t_ref, 2 * j)
    other_major, other_minor = by_major(v_sides, other_slot), by_minor(v_sides, other_slot)

    final = 2 * (cols - 1)

    def crossing_gram(first, second, path):
        build_kron(kron_ref, final, first, second)
        for s in range(2):
            y = dot(xq_ref[path, s], kron_ref[final]).astype(BF16)
            gram_ref[final, s] = dot(y, xq_ref[1 - path, s])

    def all_sides():
        return rounded(joined_sides(side_0, n_sides, [edge_sides])[0])

    def up_legs(weight, j):
        return kinds_of([reduce_major(gram_ref[2 * j, s], weight) for s in range(2)])

    def down_legs(weight, j):
        return kinds_of([reduce_minor(gram_ref[2 * j, s], weight) for s in range(2)])

    def ship(buffer, values):
        for k in range(2):
            buffer[k * D : (k + 1) * D] = values[k]

    def ordered(above, below, kind):
        return placed(
            [(order[j], above[j][kind]) for j in range(cols)]
            + [(cols + order[j], below[j][kind]) for j in range(cols)]
        )

    nothing = [[jnp.zeros((D, LANES), F32)] * 2] * cols
    up_far = copy(send_f1, down_1, 1, 0, {"tile": tile - 1})
    up_near = copy(send_v1, down_1, 1, 0, {"tile": tile - 1})
    down_far = copy(send_f1, up_1, 1, 1, {"tile": tile + 1})
    down_near = copy(send_v1, up_1, 1, 1, {"tile": tile + 1})

    sides_1 = copy(send_s1, side_1, 1, 2, {"group": 1 - group})

    def cross_major(at, weight):
        return kinds_of([reduce_major(gram_ref[at, s], weight) for s in range(2)])

    def cross_minor(at, weight):
        return kinds_of([reduce_minor(gram_ref[at, s], weight) for s in range(2)])

    @pl.when(far_up)
    def _():
        below_0()
        near = rounded(down_0[...])
        crossing_gram(by_major(near, cols + crossing), other_minor, 0)
        early = [up_legs(by_major(near, cols + order[j]), j) for j in range(cols - 1)]
        early = minors(early)
        sides_0.wait()
        weight = by_major(all_sides(), cross_slot)
        legs_up = early + minors([cross_major(final, weight)])
        ship(send_f1, normalised([ordered(nothing, legs_up, k) for k in range(2)]))

        @pl.when(has_up)
        def _():
            up_far.start()

        above_0()
        weight = by_minor(rounded(up_0[...]), crossing)
        (cross,) = majors([cross_minor(final, weight)])
        ship(send_s1, normalised(cross))
        sides_1.start()

    @pl.when(far_down)
    def _():
        above_0()
        near = rounded(up_0[...])
        crossing_gram(other_major, by_minor(near, crossing), 1)
        early = [down_legs(by_minor(near, order[j]), j) for j in range(cols - 1)]
        early = majors(early)
        sides_0.wait()
        weight = by_minor(all_sides(), cross_slot)
        legs_down = early + majors([cross_minor(final, weight)])
        ship(send_f1, normalised([ordered(legs_down, nothing, k) for k in range(2)]))

        @pl.when(has_down)
        def _():
            down_far.start()

        below_0()
        weight = by_major(rounded(down_0[...]), cols + crossing)
        (cross,) = minors([cross_major(final, weight)])
        ship(send_s1, normalised(cross))
        sides_1.start()

    v_rows = rounded(joined_rows(up_0[...], down_0[...])[0])
    weights = []
    for j in range(cols):
        i = order[j]
        weights.append((by_minor(v_rows, i), by_major(v_rows, cols + i)))
    v_sides = all_sides()
    cross_first, cross_second = by_major(v_sides, cross_slot), by_minor(v_sides, cross_slot)

    def horizontal_gram(j):
        build_kron(kron_ref, 2 * j + 1, weights[j][1], weights[j][0])
        paired(j, 2 * j + 1, x2t_ref, x2_ref, 2 * j + 1)

    def horizontal(j):
        w_left, w_right = side_weights[j]
        left = kinds_of([reduce_minor(gram_ref[2 * j + 1, s], w_right) for s in range(2)])
        right = kinds_of([reduce_major(gram_ref[2 * j + 1, s], w_left) for s in range(2)])
        return left, right

    def last_gram(first, second, path):
        build_kron(kron_ref, final + 1, first, second)
        for s in range(2):
            y = dot(xq_ref[path, s], kron_ref[final + 1]).astype(BF16)
            gram_ref[final + 1, s] = dot(y, xq_ref[1 - path, s])

    @pl.when(far_up)
    def _():
        last_gram(cross_first, weights[-1][0], 1)
        for j in range(cols - 1):
            horizontal_gram(j)
        near = [down_legs(weights[j][0], j) for j in range(cols - 1)]
        near = majors(near + [cross_minor(final + 1, other_minor)])
        ship(send_v1, normalised([ordered(near, nothing, k) for k in range(2)]))
        (other,) = minors([cross_major(final + 1, weights[-1][1])])
        for k in range(2):
            other_ref[k] = other[k]

        @pl.when(has_down)
        def _():
            down_near.start()

    @pl.when(far_down)
    def _():
        last_gram(weights[-1][1], cross_second, 0)
        for j in range(cols - 1):
            horizontal_gram(j)
        near = [up_legs(weights[j][1], j) for j in range(cols - 1)]
        near = minors(near + [cross_major(final + 1, other_major)])
        ship(send_v1, normalised([ordered(nothing, near, k) for k in range(2)]))
        (other,) = majors([cross_minor(final + 1, weights[-1][0])])
        for k in range(2):
            other_ref[k] = other[k]

        @pl.when(has_up)
        def _():
            up_near.start()

    half = cols * D
    swapped = jnp.where(
        slot < cols, lane + half, jnp.where(slot < 2 * cols, lane - half, lane)
    )
    o_rows = [
        pick(send_f1[k * D : (k + 1) * D] + send_v1[k * D : (k + 1) * D], swapped)
        for k in range(2)
    ]
    others = [horizontal(j) for j in range(cols - 1)]
    lefts = majors([o[0] for o in others])
    rights = minors([o[1] for o in others])

    def own_sides(kind):
        return placed(
            [(order[j], lefts[j][kind]) for j in range(cols - 1)]
            + [(cols + order[j], rights[j][kind]) for j in range(cols - 1)]
            + [(other_slot, other_ref[kind])]
        )

    def other_sides(kind):
        entries = []
        for j in range(cols - 1):
            i = order[j]
            entries.append((jnp.where(i == 0, -1, cols + i - 1), lefts[j][kind]))
            entries.append((jnp.where(i == cols - 1, -1, i + 1), rights[j][kind]))
        entries.append((jnp.where(group == 0, cols + crossing - 1, 1), other_ref[kind]))
        return placed(entries)

    is_cross = (slot == cross_slot) | (slot == jnp.where(group == 0, 2 * cols + 1, 2 * cols))
    o_sides = [
        jnp.where(is_cross, send_s1[k * D : (k + 1) * D], value)
        for k, value in enumerate(normalised([own_sides(k) for k in range(2)]))
    ]
    n_sides = normalised([other_sides(k) for k in range(2)])
    state, rotated, trace = bond_open(*[o + n for o, n in zip(o_sides, n_sides)])
    for step in range(EARLY_STEPS):
        state, rotated = bond_step(state, rotated)
    for n, value in enumerate([state] + rotated + [trace]):
        inner_ref[n] = value
    zero = jnp.zeros((D, LANES), F32)
    sides_1.wait()
    n_sides = joined_sides(side_1, n_sides, [edge_sides, zero])
    rows_edges = jnp.concatenate([edge_rows, zero], axis=0)
    above_arrives(up_near, down_near, up_1, rows_edges)
    below_arrives(down_near, up_near, down_1, rows_edges)
    n_rows = joined_rows(up_1[...], down_1[...])
    for k in range(2):
        env_ref[k] = jnp.where(
            slot < 2 * cols, o_rows[k] + n_rows[k], o_sides[k] + n_sides[k]
        )
    mout_ref[0] = n_rows[0]
    mout_ref[1] = n_sides[0]


def gates_kernel(tiles, groups, cols, D, ax_ref, env_ref, inner_ref, in_ref, out_hbm, mout_hbm,
                 kron_ref, out_ref, mout_ref, store_sem):
    tile = lax.axis_index("tile")
    group = lax.axis_index("group")
    DD = D * D
    shift = D.bit_length() - 1
    halves = DD // LANES
    mixed = 2 * halves
    rows = DD // mixed
    lane = iota((D, LANES), 1)
    row = iota((D, LANES), 0)
    inner = lane & (D - 1)
    start = lane - inner
    slot = lane >> shift

    unit = jnp.where(inner == row, 1.0, 0.0).astype(F32)
    at_edge = (
        ((slot < cols) & (tile == 0))
        | ((slot >= cols) & (slot < 2 * cols) & (tile == tiles - 1))
        | ((slot == 2 * cols) & (group == 0))
        | ((slot == 2 * cols + 1) & (group == groups - 1))
    )
    state, rotated, trace = bond_open(env_ref[0], env_ref[1])
    begun, turning = inner_ref[0], [inner_ref[1], inner_ref[2]]
    early_left = NS_STEPS - 2 - EARLY_STEPS
    for step in range(NS_STEPS - 2):
        if step < early_left:
            begun, turning = bond_step(begun, turning)
        elif step == early_left:
            early = [
                w.astype(BF16).astype(F32) for w in bond_close(begun, turning, inner_ref[3])
            ]
        state, rotated = bond_step(state, rotated)
    late = [
        jnp.where(at_edge, unit, w).astype(BF16).astype(F32)
        for w in bond_close(state, rotated, trace)
    ]

    unfold_mask = slot == (row & (LANES // D - 1))
    flat_rows = []
    for m in range(4 * cols):
        at = m // 4 + (cols if m % 4 >= 2 else 0)
        tiled = jnp.where(unfold_mask, pick(in_ref[m % 2], inner + at * D), 0.0)
        step = D // halves
        flat_rows.append(
            jnp.concatenate(
                [
                    jnp.sum(tiled[h * step : (h + 1) * step], axis=0, keepdims=True)
                    for h in range(halves)
                ],
                axis=1,
            )
        )
    mout_ref[...] = jnp.concatenate(flat_rows, axis=0).reshape(cols, 4, DD)
    store_msg = pltpu.make_async_copy(mout_ref, mout_hbm, store_sem.at[cols])
    store_msg.start()

    def by_major(value, m):
        return jnp.concatenate(
            [pick(value, m * D + slot + h * (LANES // D)) for h in range(halves)], axis=1
        )

    def by_minor(value, m):
        part = pick(value, m * D + inner)
        return jnp.concatenate([part] * halves, axis=1)

    scatter = unmixing(D, mixed, 1)
    stores = [
        pltpu.make_async_copy(out_ref.at[i], out_hbm.at[i], store_sem.at[i]) for i in range(cols)
    ]

    for i in range(cols):
        for s in range(2):
            left = by_major(late[s], 2 * cols) if i == 0 else by_major(early[s], i)
            right = (
                by_minor(late[s], 2 * cols + 1) if i == cols - 1 else by_minor(early[s], i + 1)
            )
            at = (i * 2 + s) * 2
            down = math.cosh(FIELD) * by_major(late[s], cols + i)
            build_kron(kron_ref, at, down, right)
            build_kron(kron_ref, at + 1, left, by_minor(late[s], i))
    gated = [
        [dot_nt(ax_ref[i, s], kron_ref[(i * 2 + s) * 2]).astype(BF16) for s in range(2)]
        for i in range(cols)
    ]
    gated = [
        [dot(kron_ref[(i * 2 + s) * 2 + 1], gated[i][s]).astype(BF16) for s in range(2)]
        for i in range(cols)
    ]

    def emit(i, gated):
        for b in range(0, mixed, 2):
            block = jnp.concatenate(
                [
                    jnp.concatenate(
                        [
                            gated[g % 2][
                                (b + c) * rows : (b + c + 1) * rows,
                                (g // 2) * LANES : (g // 2 + 1) * LANES,
                            ]
                            for c in range(2)
                        ],
                        axis=1,
                    )
                    for g in range(mixed)
                ],
                axis=0,
            )
            done = dot(scatter, block).astype(BF16)
            for c in range(2):
                for u in range(D):
                    at = u * D * mixed + (b + c) * D
                    out_ref[i, at : at + D, :] = done[
                        u * D : (u + 1) * D, c * LANES : (c + 1) * LANES
                    ]
        stores[i].start()

    for i in range(cols):
        emit(i, gated[i])
    for store in stores + [store_msg]:
        store.wait()


def per_device(tiles, groups, site_tensors, msg_in):
    _, cols, _, size = site_tensors.shape
    DD = msg_in.shape[-1]
    D = math.isqrt(DD)
    chunks = size // LANES
    a = site_tensors.reshape(cols, 2, chunks, LANES).transpose(0, 2, 1, 3)
    a = a.reshape(cols, 2 * chunks, LANES)
    vmem = pl.BlockSpec(memory_space=pltpu.VMEM)
    hbm = pl.BlockSpec(memory_space=pltpu.HBM)
    gated, env, inner, stacked = pl.pallas_call(
        functools.partial(messages_kernel, tiles, groups, cols, D),
        out_shape=(
            jax.ShapeDtypeStruct((cols, 2, DD, DD), BF16),
            jax.ShapeDtypeStruct((2, D, LANES), F32),
            jax.ShapeDtypeStruct((4, D, LANES), F32),
            jax.ShapeDtypeStruct((2, D, LANES), F32),
        ),
        in_specs=[hbm, hbm],
        out_specs=(vmem, vmem, vmem, vmem),
        scratch_shapes=[
            pltpu.VMEM(a.shape, BF16),
            pltpu.VMEM((cols, 4, DD), F32),
            pltpu.VMEM((2, D, LANES), F32),
            pltpu.VMEM((cols, 2, DD, DD), BF16),
            pltpu.VMEM((cols, 2, DD, DD), BF16),
            pltpu.VMEM((2, 2, DD, DD), BF16),
            pltpu.VMEM((cols - 1, 2, DD, DD), BF16),
            pltpu.VMEM((cols - 1, 2, DD, DD), BF16),
            pltpu.VMEM((2 * cols, DD, DD), BF16),
            pltpu.VMEM((2 * cols, 2, DD, DD), F32),
        ]
        + [
            pltpu.VMEM(((1 + turn) * D, LANES), F32) for _ in range(6) for turn in range(ITERS)
        ]
        + [
            pltpu.SemaphoreType.DMA((ITERS, 3)),
            pltpu.SemaphoreType.DMA((ITERS, 3)),
            pltpu.SemaphoreType.DMA((cols + 1,)),
        ],
        compiler_params=pltpu.CompilerParams(
            collective_id=0, has_side_effects=True, vmem_limit_bytes=24 * 2**20
        ),
    )(
        pltpu.with_memory_space_constraint(a, pltpu.HBM),
        pltpu.with_memory_space_constraint(msg_in[0], pltpu.HBM),
    )
    out, messages = pl.pallas_call(
        functools.partial(gates_kernel, tiles, groups, cols, D),
        out_shape=(
            jax.ShapeDtypeStruct(a.shape, BF16),
            jax.ShapeDtypeStruct((cols, 4, DD), F32),
        ),
        in_specs=[vmem, vmem, vmem, vmem],
        out_specs=(hbm, hbm),
        scratch_shapes=[
            pltpu.VMEM((4 * cols, DD, DD), BF16),
            pltpu.VMEM(a.shape, BF16),
            pltpu.VMEM((cols, 4, DD), F32),
            pltpu.SemaphoreType.DMA((cols + 1,)),
        ],
        compiler_params=pltpu.CompilerParams(vmem_limit_bytes=24 * 2**20),
    )(gated, env, inner, stacked)
    out = out.reshape(cols, chunks, 2, LANES).transpose(0, 2, 1, 3)
    return out.reshape(1, cols, 2, size), messages[None]


def solution(mesh):
    spec = P("tile", "group", None, None)
    return jax.shard_map(
        functools.partial(per_device, mesh.shape["tile"], mesh.shape["group"]),
        mesh=mesh, in_specs=(spec, spec), out_specs=(spec, spec), check_vma=False,
    )
```

```python
import functools
import math

import jax
import jax.numpy as jnp
from jax import lax
from jax.experimental import pallas as pl
from jax.experimental.pallas import tpu as pltpu
from jax.sharding import PartitionSpec as P

ITERS = 2
NS_STEPS = 6
EARLY_STEPS = 3
LANES = 128
EPSILON = 1e-06
COUPLING = 0.5
FIELD = 0.3
F32 = jnp.float32
BF16 = jnp.bfloat16
MESH = pl.DeviceIdType.MESH


def iota(shape, axis):
    return lax.broadcasted_iota(jnp.int32, shape, axis)


def dot(a, b):
    return jnp.dot(a, b, preferred_element_type=F32)


def dot_nt(a, b):
    return lax.dot_general(a, b, (((1,), (1,)), ((), ())), preferred_element_type=F32)


def dot_tn(a, b):
    return lax.dot_general(a, b, (((0,), (0,)), ((), ())), preferred_element_type=F32)


def parts(value, count):
    out = []
    for _ in range(count):
        piece = value.astype(BF16)
        out.append(piece)
        value = value - piece.astype(F32)
    return out


def select_dot(value, selector, count):
    total = None
    for piece in parts(value, count):
        term = dot(piece, selector)
        total = term if total is None else total + term
    return total


def one_hot(mask):
    return jnp.where(mask, 1.0, 0.0).astype(BF16)


def build_kron(kron_ref, slot, first, second):
    D = first.shape[0]
    for d in range(D):
        kron_ref[slot, d * D : (d + 1) * D, :] = (first[d : d + 1, :] * second).astype(BF16)


def pick(value, index):
    return jnp.take_along_axis(value, index, axis=1, mode="promise_in_bounds")


def row_of(value, k):
    return jnp.broadcast_to(value[k : k + 1, :], value.shape)


def bond_open(msg_sum, twist_sum):
    D = msg_sum.shape[0]
    lane = iota((D, LANES), 1)
    row = iota((D, LANES), 0)
    inner = lane & (D - 1)
    turned = lane - inner + row
    g0, g1 = math.cosh(COUPLING), math.sinh(COUPLING)
    cross = math.sqrt(g0 * g1)
    root2 = math.sqrt(2.0)
    halves = [
        ((g0 * msg_sum + cross * twist_sum) / root2).astype(BF16).astype(F32),
        ((cross * twist_sum + g1 * msg_sum) / root2).astype(BF16).astype(F32),
    ]
    squares = halves[0] * halves[0] + halves[1] * halves[1]
    squares = jnp.broadcast_to(jnp.sum(squares, axis=0, keepdims=True), (D, LANES))
    trace = jnp.sum(pick(squares, turned), axis=0, keepdims=True) + EPSILON

    gram = None
    rotated = []
    for half in halves:
        transposed = None
        for k in range(D):
            own = row_of(half, k)
            column = pick(own, turned)
            term = column * own
            gram = term if gram is None else gram + term
            placed = jnp.where(inner == k, column, 0.0)
            transposed = placed if transposed is None else transposed + placed
        rotated.append(transposed)

    return gram / trace, rotated, jnp.broadcast_to(trace, (D, LANES))


def bond_tools(D):
    lane = iota((D, LANES), 1)
    row = iota((D, LANES), 0)
    inner = lane & (D - 1)
    turned = lane - inner + row
    unit = jnp.where(inner == row, 1.0, 0.0).astype(F32)

    def columns(value):
        return [pick(row_of(value, k), turned) for k in range(D)]

    def times(left, right):
        sums = [None] * 4
        for k in range(D):
            term = left[k] * row_of(right, k)
            sums[k % 4] = term if sums[k % 4] is None else sums[k % 4] + term
        return (sums[0] + sums[1]) + (sums[2] + sums[3])

    return unit, columns, times


def bond_step(state, rotated):
    unit, columns, times = bond_tools(state.shape[0])
    left = columns(state)
    square = times(left, state)
    rotated = [1.5 * v - 0.5 * times(left, v) for v in rotated]
    state = times(left, 2.25 * unit - 1.5 * state + 0.25 * square)
    return state, rotated


def bond_close(state, rotated, trace):
    _, columns, times = bond_tools(state.shape[0])
    left = columns(state)
    rotated = [1.5 * v - 0.5 * times(left, v) for v in rotated]
    again = rotated
    for _ in range(2):
        again = [1.5 * v - 0.5 * times(left, v) for v in again]
    rotated = [1.5 * v - 0.5 * times(left, w) for v, w in zip(rotated, again)]
    scale = 1.0 / jnp.sqrt(trace)
    first = math.sqrt(math.cosh(COUPLING)) * rotated[0] * scale
    second = math.sqrt(math.sinh(COUPLING)) * rotated[1] * scale
    return [first + second, first - second]


def unmixing(D, mixed, out_axis):
    DD = D * D
    sub = D // mixed
    p, k = iota((DD, DD), out_axis), iota((DD, DD), 1 - out_axis)
    low = p & (D - 1)
    mid = (p >> (D.bit_length() - 1)) & (sub - 1)
    top = p >> (D * sub).bit_length() - 1
    return one_hot(k == low * D + mid * mixed + top)


def messages_kernel(tiles, groups, cols, D, a_hbm, msg_hbm, ax_ref, env_ref, inner_ref, mout_ref,
           a_ref, msg_ref, other_ref, x_ref, xt_ref, xq_ref, x2_ref, x2t_ref, kron_ref, gram_ref,
           send_v0, send_v1, send_s0, send_s1, _, send_f1, up_0, up_1, down_0, down_1, side_0, side_1,
           send_sem, recv_sem, load_sem):
    loads = [pltpu.make_async_copy(msg_hbm, msg_ref, load_sem.at[cols])]
    loads += [
        pltpu.make_async_copy(a_hbm.at[i], a_ref.at[i], load_sem.at[i]) for i in range(cols)
    ]
    for load in loads:
        load.start()
    tile = lax.axis_index("tile")
    group = lax.axis_index("group")
    DD = D * D
    shift = D.bit_length() - 1
    halves = DD // LANES
    mixed = 2 * halves
    sub = D // mixed
    per = LANES // D
    legs = 4 * cols
    crossing = jnp.where(group == 0, cols - 1, 0)
    closed = jnp.where(group == 0, 0, cols - 1)
    order = list(range(1, cols - 1)) + [closed, crossing]
    has_up = tile > 0
    has_down = tile < tiles - 1
    far_path = lax.rem(tile, 2)
    far_up = far_path == 0
    far_down = jnp.logical_not(far_up)
    swap_sides = far_path == group
    cross_slot = jnp.where(group == 0, cols + crossing, crossing)
    other_slot = jnp.where(group == 0, crossing, cols + crossing)

    barrier = pltpu.get_barrier_semaphore()

    @pl.when(has_up)
    def _():
        pl.semaphore_signal(barrier, inc=1, device_id={"tile": tile - 1}, device_id_type=MESH)

    @pl.when(has_down)
    def _():
        pl.semaphore_signal(barrier, inc=1, device_id={"tile": tile + 1}, device_id_type=MESH)

    pl.semaphore_signal(barrier, inc=1, device_id={"group": 1 - group}, device_id_type=MESH)

    lane = iota((D, LANES), 1)
    row = iota((D, LANES), 0)
    within = lane & (D - 1)
    turned = lane - within + row
    slot = lane >> shift
    gather = unmixing(D, mixed, 0)
    fold_minor = one_hot((iota((LANES, LANES), 0) & (D - 1)) == (iota((LANES, LANES), 1) & (D - 1)))
    fold_major = one_hot((iota((DD, LANES), 0) >> shift) == (iota((DD, LANES), 1) & (D - 1)))

    def placed(entries):
        total = jnp.zeros((D, LANES), F32)
        for where, value in entries:
            total = jnp.where(slot == where, value, total)
        return total

    def by_major(value, m):
        return jnp.concatenate([pick(value, m * D + slot + h * per) for h in range(halves)], axis=1)

    def by_minor(value, m):
        return jnp.concatenate([pick(value, m * D + within)] * halves, axis=1)

    def rounded(value):
        return value.astype(BF16).astype(F32)

    def reduce_major(gram, weight):
        total = gram[:D] * weight[0:1, :]
        for d in range(1, D):
            total = total + gram[d * D : (d + 1) * D] * weight[d : d + 1, :]
        return total

    sublane = iota((8, DD), 0)

    def reduce_minor(gram, weight):
        blocks = []
        for d in range(D):
            block = gram[d * D : (d + 1) * D] * weight
            total = block[:8]
            for h in range(1, D // 8):
                total = total + block[h * 8 : (h + 1) * 8]
            blocks.append(total)
        out = []
        for base in range(0, D, 8):
            level = blocks[base : base + 8]
            step = 1
            while len(level) > 1:
                low = (sublane & step) == 0
                level = [
                    jnp.where(low, level[n], level[n + 1])
                    + pltpu.roll(jnp.where(low, level[n + 1], level[n]), step, 0)
                    for n in range(0, len(level), 2)
                ]
                step *= 2
            out.append(level[0])
        return jnp.concatenate(out, axis=0)

    def kinds_of(totals):
        if len(totals) == 1:
            return totals
        return [totals[0] + totals[1], totals[0] - totals[1]]

    def folded(totals, selector):
        pieces = []
        for total in totals:
            if selector is fold_minor:
                joined = total[:, :LANES]
                for h in range(1, halves):
                    joined = joined + total[:, h * LANES : (h + 1) * LANES]
                total = joined
            pieces += parts(total, 2)
        out = dot(jnp.concatenate(pieces, axis=0), selector)
        return [
            out[2 * n * D : (2 * n + 1) * D] + out[(2 * n + 1) * D : (2 * n + 2) * D]
            for n in range(len(totals))
        ]

    def minors(totals):
        count = len(totals[0])
        flat = folded([v for t in totals for v in t], fold_minor)
        return [flat[n * count : (n + 1) * count] for n in range(len(totals))]

    def majors(totals):
        count = len(totals[0])
        flat = folded([v for t in totals for v in t], fold_major)
        return [flat[n * count : (n + 1) * count] for n in range(len(totals))]

    def normalised(values):
        power = jnp.sum(values[0] * values[0], axis=0, keepdims=True)
        power = pick(jnp.broadcast_to(power, (D, LANES)), turned)
        power = jnp.sum(power, axis=0, keepdims=True) / DD
        scale = 1.0 / jnp.sqrt(power + EPSILON)
        return [v * scale for v in values]

    def upright(ups, downs, kind):
        return placed(
            [(i, ups[i][kind]) for i in range(cols)]
            + [(cols + i, downs[i][kind]) for i in range(cols)]
        )

    def copy(src, dst, turn, k, device):
        return pltpu.make_async_remote_copy(
            src_ref=src, dst_ref=dst, send_sem=send_sem.at[turn, k],
            recv_sem=recv_sem.at[turn, k], device_id=device, device_id_type=MESH,
        )

    def above_arrives(sent, arriving, dst, edges):
        @pl.when(has_up)
        def _():
            sent.wait_send()
            arriving.wait_recv()

        @pl.when(jnp.logical_not(has_up))
        def _():
            dst[...] = edges

    def below_arrives(sent, arriving, dst, edges):
        @pl.when(has_down)
        def _():
            sent.wait_send()
            arriving.wait_recv()

        @pl.when(jnp.logical_not(has_down))
        def _():
            dst[...] = edges

    def joined_rows(above, below):
        return [
            jnp.where(slot < cols, above[k * D : (k + 1) * D], below[k * D : (k + 1) * D])
            for k in range(above.shape[0] // D)
        ]

    from_left = (slot == 0) | (slot == 2 * cols)
    from_right = (slot == 2 * cols - 1) | (slot == 2 * cols + 1)

    def joined_sides(dst, local, edges):
        got = dst[...]
        out = []
        for k, (value, edge) in enumerate(zip(local, edges)):
            other = got[k * D : (k + 1) * D]
            value = jnp.where(from_left, jnp.where(group == 0, edge, other), value)
            out.append(
                jnp.where(from_right, jnp.where(group == groups - 1, edge, other), value)
            )
        return out

    loads[0].wait()
    spot = (row & (per - 1)) * D + within
    flat = msg_ref[...].reshape(legs, DD)

    def unfolded(m):
        source = jnp.concatenate(
            [
                jnp.broadcast_to(flat[m : m + 1, h * LANES : (h + 1) * LANES], (per, LANES))
                for h in range(halves)
            ],
            axis=0,
        )
        return pick(source, spot)

    singles = [unfolded(m) for m in range(legs)]
    edge_rows = placed(
        [(i, singles[4 * i]) for i in range(cols)]
        + [(cols + i, singles[4 * i + 2]) for i in range(cols)]
    )
    edge_sides = placed(
        [(i, singles[4 * i + 1]) for i in range(cols)]
        + [(cols + i, singles[4 * i + 3]) for i in range(cols)]
    )

    def unmix(i):
        for b in range(0, mixed, 2):
            pair = jnp.concatenate(
                [
                    jnp.concatenate(
                        [
                            a_ref[i, u * D * mixed + (b + c) * D : u * D * mixed + (b + c + 1) * D]
                            for u in range(D)
                        ],
                        axis=0,
                    )
                    for c in range(2)
                ],
                axis=1,
            )
            block = dot(gather, pair).astype(BF16)
            span = sub * D
            for c in range(2):
                for g in range(mixed):
                    x_ref[
                        i,
                        g % 2,
                        (b + c) * span : (b + c + 1) * span,
                        (g // 2) * LANES : (g // 2 + 1) * LANES,
                    ] = block[g * span : (g + 1) * span, c * LANES : (c + 1) * LANES]

    def exchanged(groups_of, masks, unit_lanes):
        step = 1
        for high in masks:
            following = []
            for values in groups_of:
                out = list(values)
                for a in range(len(values)):
                    if a & step:
                        continue
                    b = a | step
                    low_up = pltpu.roll(values[b], unit_lanes * step, 1)
                    high_down = pltpu.roll(values[a], LANES - unit_lanes * step, 1)
                    out[a] = jnp.where(high[0], low_up, values[a])
                    out[b] = jnp.where(high[1], values[b], high_down)
                following.append(out)
            groups_of = following
            step *= 2
        return groups_of

    def relayout(j, s):
        bits = per.bit_length() - 1
        masks = [((slot & (1 << n)) != 0,) * 2 for n in range(bits)]
        blocks = [(h, lh) for h in range(halves) for lh in range(halves)]
        groups_of = [
            [
                x_ref[
                    order[j], s, (lh * per + k) * D : (lh * per + k + 1) * D,
                    h * LANES : (h + 1) * LANES,
                ]
                for k in range(per)
            ]
            for h, lh in blocks
        ]
        for (h, lh), values in zip(blocks, exchanged(groups_of, masks, D)):
            for d in range(per):
                x2_ref[
                    j, s, (h * per + d) * D : (h * per + d + 1) * D,
                    lh * LANES : (lh + 1) * LANES,
                ] = values[d]
        x2t_ref[j, s] = x2_ref[j, s].T

    def cross_layout(s):
        shut = jnp.where(swap_sides, 0, 1)
        masks = []
        for n in range(shift):
            bit = (lane >> n) & 1
            masks.append(((bit & (1 - shut)) != 0, (bit | shut) != 0))
        groups_of = [
            [
                x_ref[crossing, s, k * D : (k + 1) * D, h * LANES : (h + 1) * LANES]
                for k in range(D)
            ]
            for h in range(halves)
        ]
        for h, values in enumerate(exchanged(groups_of, masks, 1)):
            for k in range(D):
                xq_ref[0, s, k * D : (k + 1) * D, h * LANES : (h + 1) * LANES] = values[k]
        xq_ref[1, s] = xq_ref[0, s].T

    v_rows, v_sides = rounded(edge_rows), rounded(edge_sides)
    weights = []
    for i in range(cols):
        w_up, w_down = by_minor(v_rows, i), by_major(v_rows, cols + i)
        w_left, w_right = by_major(v_sides, i), by_minor(v_sides, cols + i)
        weights.append((w_up, w_down, w_left, w_right))
        build_kron(kron_ref, 2 * i, w_down, w_right)
        build_kron(kron_ref, 2 * i + 1, w_left, w_up)
    for load in loads[1:]:
        load.wait()
    for i in range(cols):
        unmix(i)
    for i in range(cols):
        for s in range(2):
            xt_ref[i, s] = x_ref[i, s].T
    sides_of = ((x_ref, xt_ref), (xt_ref, x_ref))

    def first_gram(path, i):
        left, right = sides_of[path]
        y = [dot(left[i, s], kron_ref[2 * i + path]).astype(BF16) for s in range(2)]
        gram_ref[2 * i + path, 0] = dot(
            jnp.concatenate(y, axis=1), right[i].reshape(2 * DD, DD)
        )

    def outer(i, leg):
        w_up, w_down, w_left, w_right = weights[i]
        if leg == 0:
            return [reduce_major(gram_ref[2 * i, 0], w_left)]
        if leg == 1:
            return [reduce_minor(gram_ref[2 * i, 0], w_up)]
        if leg == 2:
            return [reduce_minor(gram_ref[2 * i + 1, 0], w_right)]
        return [reduce_major(gram_ref[2 * i + 1, 0], w_down)]

    first_gram(0, 0)
    first_gram(1, cols - 1)
    for i in range(1, cols):
        first_gram(0, i)
    for i in range(cols - 1):
        first_gram(1, i)
    (left_first,), (right_last,) = majors([outer(0, 1)]), minors([outer(cols - 1, 3)])
    send_s0[...] = normalised([jnp.where(from_left, right_last[0], left_first[0])])[0]
    ups = [outer(i, 0) for i in range(cols)]

    mix = jnp.full((D, DD), math.tanh(FIELD), BF16)
    for i in range(cols):
        for d in range(0, DD, D):
            a0, a1 = (x_ref[i, s, d : d + D] for s in range(2))
            ax_ref[i, 0, d : d + D] = a0 + mix * a1
            ax_ref[i, 1, d : d + D] = a1 + mix * a0

    inside = jnp.logical_and(has_up, has_down)

    @pl.when(inside)
    def _():
        pl.semaphore_wait(barrier, 3)

    @pl.when(jnp.logical_not(inside))
    def _():
        pl.semaphore_wait(barrier, 2)

    sides_0 = copy(send_s0, side_0, 0, 2, {"group": 1 - group})
    sides_0.start()
    downs = majors([outer(i, 2) for i in range(cols)])
    ups = minors(ups)
    send_v0[...] = normalised([upright(downs, ups, 0)])[0]
    to_up = copy(send_v0, down_0, 0, 0, {"tile": tile - 1})
    to_down = copy(send_v0, up_0, 0, 1, {"tile": tile + 1})

    @pl.when(has_up)
    def _():
        to_up.start()

    @pl.when(has_down)
    def _():
        to_down.start()

    for s in range(2):
        cross_layout(s)
    for j in range(cols - 1):
        for s in range(2):
            relayout(j, s)

    lefts = [left_first] + majors([outer(i, 1) for i in range(1, cols)])
    rights = minors([outer(i, 3) for i in range(cols - 1)]) + [right_last]

    def inner_view(lefts, rights, kind):
        return placed(
            [(i, rights[i - 1][kind]) for i in range(1, cols)]
            + [(cols + i, lefts[i + 1][kind]) for i in range(cols - 1)]
        )

    n_sides = normalised([inner_view(lefts, rights, 0)])

    def above_0():
        above_arrives(to_up, to_down, up_0, edge_rows)

    def below_0():
        below_arrives(to_down, to_up, down_0, edge_rows)

    side_weights = []

    def paired(j, kron, left, right, at):
        for s in range(2):
            y = dot(left[j, s], kron_ref[kron]).astype(BF16)
            gram_ref[at, s] = dot_nt(y, x2_ref[j, s]) if right is x2t_ref else dot(y, right[j, s])

    v_sides = rounded(jnp.where(from_left | from_right, edge_sides, n_sides[0]))
    for j in range(cols - 1):
        i = order[j]
        w_left, w_right = by_major(v_sides, i), by_minor(v_sides, cols + i)
        side_weights.append((w_left, w_right))
        build_kron(kron_ref, 2 * j, w_left, w_right)
        paired(j, 2 * j, x2_ref, x2t_ref, 2 * j)
    other_major, other_minor = by_major(v_sides, other_slot), by_minor(v_sides, other_slot)

    final = 2 * (cols - 1)

    def crossing_gram(first, second, path):
        build_kron(kron_ref, final, first, second)
        for s in range(2):
            y = dot(xq_ref[path, s], kron_ref[final]).astype(BF16)
            gram_ref[final, s] = dot_nt(y, xq_ref[path, s])

    def all_sides():
        return rounded(joined_sides(side_0, n_sides, [edge_sides])[0])

    def up_legs(weight, j):
        return kinds_of([reduce_major(gram_ref[2 * j, s], weight) for s in range(2)])

    def down_legs(weight, j):
        return kinds_of([reduce_minor(gram_ref[2 * j, s], weight) for s in range(2)])

    def ship(buffer, values):
        for k in range(2):
            buffer[k * D : (k + 1) * D] = values[k]

    def ordered(above, below, kind):
        return placed(
            [(order[j], above[j][kind]) for j in range(cols)]
            + [(cols + order[j], below[j][kind]) for j in range(cols)]
        )

    nothing = [[jnp.zeros((D, LANES), F32)] * 2] * cols
    up_far = copy(send_f1, down_1, 1, 0, {"tile": tile - 1})
    up_near = copy(send_v1, down_1, 1, 0, {"tile": tile - 1})
    down_far = copy(send_f1, up_1, 1, 1, {"tile": tile + 1})
    down_near = copy(send_v1, up_1, 1, 1, {"tile": tile + 1})

    sides_1 = copy(send_s1, side_1, 1, 2, {"group": 1 - group})

    def cross_major(at, weight):
        return kinds_of([reduce_major(gram_ref[at, s], weight) for s in range(2)])

    def cross_minor(at, weight):
        return kinds_of([reduce_minor(gram_ref[at, s], weight) for s in range(2)])

    @pl.when(far_up)
    def _():
        below_0()
        near = rounded(down_0[...])
        crossing_gram(by_major(near, cols + crossing), other_minor, 0)
        early = [up_legs(by_major(near, cols + order[j]), j) for j in range(cols - 1)]
        early = minors(early)
        sides_0.wait()
        weight = by_major(all_sides(), cross_slot)
        legs_up = early + minors([cross_major(final, weight)])
        ship(send_f1, normalised([ordered(nothing, legs_up, k) for k in range(2)]))

        @pl.when(has_up)
        def _():
            up_far.start()

        above_0()
        weight = by_minor(rounded(up_0[...]), crossing)
        (cross,) = majors([cross_minor(final, weight)])
        ship(send_s1, normalised(cross))
        sides_1.start()

    @pl.when(far_down)
    def _():
        above_0()
        near = rounded(up_0[...])
        crossing_gram(other_major, by_minor(near, crossing), 1)
        early = [down_legs(by_minor(near, order[j]), j) for j in range(cols - 1)]
        early = majors(early)
        sides_0.wait()
        weight = by_minor(all_sides(), cross_slot)
        legs_down = early + majors([cross_minor(final, weight)])
        ship(send_f1, normalised([ordered(legs_down, nothing, k) for k in range(2)]))

        @pl.when(has_down)
        def _():
            down_far.start()

        below_0()
        weight = by_major(rounded(down_0[...]), cols + crossing)
        (cross,) = minors([cross_major(final, weight)])
        ship(send_s1, normalised(cross))
        sides_1.start()

    v_rows = rounded(joined_rows(up_0[...], down_0[...])[0])
    weights = []
    for j in range(cols):
        i = order[j]
        weights.append((by_minor(v_rows, i), by_major(v_rows, cols + i)))
    v_sides = all_sides()
    cross_first, cross_second = by_major(v_sides, cross_slot), by_minor(v_sides, cross_slot)

    def horizontal_gram(j):
        build_kron(kron_ref, 2 * j + 1, weights[j][1], weights[j][0])
        paired(j, 2 * j + 1, x2t_ref, x2_ref, 2 * j + 1)

    def horizontal(j):
        w_left, w_right = side_weights[j]
        left = kinds_of([reduce_minor(gram_ref[2 * j + 1, s], w_right) for s in range(2)])
        right = kinds_of([reduce_major(gram_ref[2 * j + 1, s], w_left) for s in range(2)])
        return left, right

    def last_gram(first, second, path):
        build_kron(kron_ref, final + 1, first, second)
        for s in range(2):
            y = dot(xq_ref[path, s], kron_ref[final + 1]).astype(BF16)
            gram_ref[final + 1, s] = dot(y, xq_ref[1 - path, s])

    @pl.when(far_up)
    def _():
        last_gram(cross_first, weights[-1][0], 1)
        for j in range(cols - 1):
            horizontal_gram(j)
        near = [down_legs(weights[j][0], j) for j in range(cols - 1)]
        near = majors(near + [cross_minor(final + 1, other_minor)])
        ship(send_v1, normalised([ordered(near, nothing, k) for k in range(2)]))
        (other,) = minors([cross_major(final + 1, weights[-1][1])])
        for k in range(2):
            other_ref[k] = other[k]

        @pl.when(has_down)
        def _():
            down_near.start()

    @pl.when(far_down)
    def _():
        last_gram(weights[-1][1], cross_second, 0)
        for j in range(cols - 1):
            horizontal_gram(j)
        near = [up_legs(weights[j][1], j) for j in range(cols - 1)]
        near = minors(near + [cross_major(final + 1, other_major)])
        ship(send_v1, normalised([ordered(nothing, near, k) for k in range(2)]))
        (other,) = majors([cross_minor(final + 1, weights[-1][0])])
        for k in range(2):
            other_ref[k] = other[k]

        @pl.when(has_up)
        def _():
            up_near.start()

    half = cols * D
    swapped = jnp.where(
        slot < cols, lane + half, jnp.where(slot < 2 * cols, lane - half, lane)
    )
    o_rows = [
        pick(send_f1[k * D : (k + 1) * D] + send_v1[k * D : (k + 1) * D], swapped)
        for k in range(2)
    ]
    others = [horizontal(j) for j in range(cols - 1)]
    lefts = majors([o[0] for o in others])
    rights = minors([o[1] for o in others])

    def own_sides(kind):
        return placed(
            [(order[j], lefts[j][kind]) for j in range(cols - 1)]
            + [(cols + order[j], rights[j][kind]) for j in range(cols - 1)]
            + [(other_slot, other_ref[kind])]
        )

    def other_sides(kind):
        entries = []
        for j in range(cols - 1):
            i = order[j]
            entries.append((jnp.where(i == 0, -1, cols + i - 1), lefts[j][kind]))
            entries.append((jnp.where(i == cols - 1, -1, i + 1), rights[j][kind]))
        entries.append((jnp.where(group == 0, cols + crossing - 1, 1), other_ref[kind]))
        return placed(entries)

    is_cross = (slot == cross_slot) | (slot == jnp.where(group == 0, 2 * cols + 1, 2 * cols))
    o_sides = [
        jnp.where(is_cross, send_s1[k * D : (k + 1) * D], value)
        for k, value in enumerate(normalised([own_sides(k) for k in range(2)]))
    ]
    n_sides = normalised([other_sides(k) for k in range(2)])
    state, rotated, trace = bond_open(*[o + n for o, n in zip(o_sides, n_sides)])
    for step in range(EARLY_STEPS):
        state, rotated = bond_step(state, rotated)
    for n, value in enumerate([state] + rotated + [trace]):
        inner_ref[n] = value
    zero = jnp.zeros((D, LANES), F32)
    sides_1.wait()
    n_sides = joined_sides(side_1, n_sides, [edge_sides, zero])
    rows_edges = jnp.concatenate([edge_rows, zero], axis=0)
    above_arrives(up_near, down_near, up_1, rows_edges)
    below_arrives(down_near, up_near, down_1, rows_edges)
    n_rows = joined_rows(up_1[...], down_1[...])
    for k in range(2):
        env_ref[k] = jnp.where(
            slot < 2 * cols, o_rows[k] + n_rows[k], o_sides[k] + n_sides[k]
        )
    mout_ref[0] = n_rows[0]
    mout_ref[1] = n_sides[0]


def gates_kernel(tiles, groups, cols, D, ax_ref, env_ref, inner_ref, in_ref, out_hbm, mout_hbm,
                 kron_ref, out_ref, mout_ref, store_sem):
    tile = lax.axis_index("tile")
    group = lax.axis_index("group")
    DD = D * D
    shift = D.bit_length() - 1
    halves = DD // LANES
    mixed = 2 * halves
    rows = DD // mixed
    lane = iota((D, LANES), 1)
    row = iota((D, LANES), 0)
    inner = lane & (D - 1)
    start = lane - inner
    slot = lane >> shift

    unit = jnp.where(inner == row, 1.0, 0.0).astype(F32)
    at_edge = (
        ((slot < cols) & (tile == 0))
        | ((slot >= cols) & (slot < 2 * cols) & (tile == tiles - 1))
        | ((slot == 2 * cols) & (group == 0))
        | ((slot == 2 * cols + 1) & (group == groups - 1))
    )
    state, rotated, trace = bond_open(env_ref[0], env_ref[1])
    begun, turning = inner_ref[0], [inner_ref[1], inner_ref[2]]
    early_left = NS_STEPS - 2 - EARLY_STEPS
    for step in range(NS_STEPS - 2):
        if step < early_left:
            begun, turning = bond_step(begun, turning)
        elif step == early_left:
            early = [
                w.astype(BF16).astype(F32) for w in bond_close(begun, turning, inner_ref[3])
            ]
        state, rotated = bond_step(state, rotated)
    late = [
        jnp.where(at_edge, unit, w).astype(BF16).astype(F32)
        for w in bond_close(state, rotated, trace)
    ]

    unfold_mask = slot == (row & (LANES // D - 1))
    flat_rows = []
    for m in range(4 * cols):
        at = m // 4 + (cols if m % 4 >= 2 else 0)
        tiled = jnp.where(unfold_mask, pick(in_ref[m % 2], inner + at * D), 0.0)
        step = D // halves
        flat_rows.append(
            jnp.concatenate(
                [
                    jnp.sum(tiled[h * step : (h + 1) * step], axis=0, keepdims=True)
                    for h in range(halves)
                ],
                axis=1,
            )
        )
    mout_ref[...] = jnp.concatenate(flat_rows, axis=0).reshape(cols, 4, DD)
    store_msg = pltpu.make_async_copy(mout_ref, mout_hbm, store_sem.at[cols])
    store_msg.start()

    def by_major(value, m):
        return jnp.concatenate(
            [pick(value, m * D + slot + h * (LANES // D)) for h in range(halves)], axis=1
        )

    def by_minor(value, m):
        part = pick(value, m * D + inner)
        return jnp.concatenate([part] * halves, axis=1)

    scatter = unmixing(D, mixed, 1)
    stores = [
        pltpu.make_async_copy(out_ref.at[i], out_hbm.at[i], store_sem.at[i]) for i in range(cols)
    ]

    for i in range(cols):
        for s in range(2):
            left = by_major(late[s], 2 * cols) if i == 0 else by_major(early[s], i)
            right = (
                by_minor(late[s], 2 * cols + 1) if i == cols - 1 else by_minor(early[s], i + 1)
            )
            at = (i * 2 + s) * 2
            down = math.cosh(FIELD) * by_major(late[s], cols + i)
            build_kron(kron_ref, at, down, right)
            build_kron(kron_ref, at + 1, left, by_minor(late[s], i))
    gated = [
        [dot_nt(ax_ref[i, s], kron_ref[(i * 2 + s) * 2]).astype(BF16) for s in range(2)]
        for i in range(cols)
    ]
    gated = [
        [dot(kron_ref[(i * 2 + s) * 2 + 1], gated[i][s]).astype(BF16) for s in range(2)]
        for i in range(cols)
    ]

    def emit(i, gated):
        for b in range(0, mixed, 2):
            block = jnp.concatenate(
                [
                    jnp.concatenate(
                        [
                            gated[g % 2][
                                (b + c) * rows : (b + c + 1) * rows,
                                (g // 2) * LANES : (g // 2 + 1) * LANES,
                            ]
                            for c in range(2)
                        ],
                        axis=1,
                    )
                    for g in range(mixed)
                ],
                axis=0,
            )
            done = dot(scatter, block).astype(BF16)
            for c in range(2):
                for u in range(D):
                    at = u * D * mixed + (b + c) * D
                    out_ref[i, at : at + D, :] = done[
                        u * D : (u + 1) * D, c * LANES : (c + 1) * LANES
                    ]
        stores[i].start()

    for i in range(cols):
        emit(i, gated[i])
    for store in stores + [store_msg]:
        store.wait()


def per_device(tiles, groups, site_tensors, msg_in):
    _, cols, _, size = site_tensors.shape
    DD = msg_in.shape[-1]
    D = math.isqrt(DD)
    chunks = size // LANES
    a = site_tensors.reshape(cols, 2, chunks, LANES).transpose(0, 2, 1, 3)
    a = a.reshape(cols, 2 * chunks, LANES)
    vmem = pl.BlockSpec(memory_space=pltpu.VMEM)
    hbm = pl.BlockSpec(memory_space=pltpu.HBM)
    gated, env, inner, stacked = pl.pallas_call(
        functools.partial(messages_kernel, tiles, groups, cols, D),
        out_shape=(
            jax.ShapeDtypeStruct((cols, 2, DD, DD), BF16),
            jax.ShapeDtypeStruct((2, D, LANES), F32),
            jax.ShapeDtypeStruct((4, D, LANES), F32),
            jax.ShapeDtypeStruct((2, D, LANES), F32),
        ),
        in_specs=[hbm, hbm],
        out_specs=(vmem, vmem, vmem, vmem),
        scratch_shapes=[
            pltpu.VMEM(a.shape, BF16),
            pltpu.VMEM((cols, 4, DD), F32),
            pltpu.VMEM((2, D, LANES), F32),
            pltpu.VMEM((cols, 2, DD, DD), BF16),
            pltpu.VMEM((cols, 2, DD, DD), BF16),
            pltpu.VMEM((2, 2, DD, DD), BF16),
            pltpu.VMEM((cols - 1, 2, DD, DD), BF16),
            pltpu.VMEM((cols - 1, 2, DD, DD), BF16),
            pltpu.VMEM((2 * cols, DD, DD), BF16),
            pltpu.VMEM((2 * cols, 2, DD, DD), F32),
        ]
        + [
            pltpu.VMEM(((1 + turn) * D, LANES), F32) for _ in range(6) for turn in range(ITERS)
        ]
        + [
            pltpu.SemaphoreType.DMA((ITERS, 3)),
            pltpu.SemaphoreType.DMA((ITERS, 3)),
            pltpu.SemaphoreType.DMA((cols + 1,)),
        ],
        compiler_params=pltpu.CompilerParams(
            collective_id=0, has_side_effects=True, vmem_limit_bytes=24 * 2**20
        ),
    )(
        pltpu.with_memory_space_constraint(a, pltpu.HBM),
        pltpu.with_memory_space_constraint(msg_in[0], pltpu.HBM),
    )
    out, messages = pl.pallas_call(
        functools.partial(gates_kernel, tiles, groups, cols, D),
        out_shape=(
            jax.ShapeDtypeStruct(a.shape, BF16),
            jax.ShapeDtypeStruct((cols, 4, DD), F32),
        ),
        in_specs=[vmem, vmem, vmem, vmem],
        out_specs=(hbm, hbm),
        scratch_shapes=[
            pltpu.VMEM((4 * cols, DD, DD), BF16),
            pltpu.VMEM(a.shape, BF16),
            pltpu.VMEM((cols, 4, DD), F32),
            pltpu.SemaphoreType.DMA((cols + 1,)),
        ],
        compiler_params=pltpu.CompilerParams(vmem_limit_bytes=24 * 2**20),
    )(gated, env, inner, stacked)
    out = out.reshape(cols, chunks, 2, LANES).transpose(0, 2, 1, 3)
    return out.reshape(1, cols, 2, size), messages[None]


def solution(mesh):
    spec = P("tile", "group", None, None)
    return jax.shard_map(
        functools.partial(per_device, mesh.shape["tile"], mesh.shape["group"]),
        mesh=mesh, in_specs=(spec, spec), out_specs=(spec, spec), check_vma=False,
    )
```

```python
import functools
import math

import jax
import jax.numpy as jnp
from jax import lax
from jax.experimental import pallas as pl
from jax.experimental.pallas import tpu as pltpu
from jax.sharding import PartitionSpec as P

ITERS = 2
NS_STEPS = 6
EARLY_STEPS = 2
FENCE_STEP = 2
LANES = 128
EPSILON = 1e-06
COUPLING = 0.5
FIELD = 0.3
F32 = jnp.float32
BF16 = jnp.bfloat16
MESH = pl.DeviceIdType.MESH


def iota(shape, axis):
    return lax.broadcasted_iota(jnp.int32, shape, axis)


def dot(a, b):
    return jnp.dot(a, b, preferred_element_type=F32)


def dot_nt(a, b):
    return lax.dot_general(a, b, (((1,), (1,)), ((), ())), preferred_element_type=F32)


def dot_tn(a, b):
    return lax.dot_general(a, b, (((0,), (0,)), ((), ())), preferred_element_type=F32)


def parts(value, count):
    out = []
    for _ in range(count):
        piece = value.astype(BF16)
        out.append(piece)
        value = value - piece.astype(F32)
    return out


def select_dot(value, selector, count):
    total = None
    for piece in parts(value, count):
        term = dot(piece, selector)
        total = term if total is None else total + term
    return total


def one_hot(mask):
    return jnp.where(mask, 1.0, 0.0).astype(BF16)


def build_kron(kron_ref, slot, first, second):
    D = first.shape[0]
    for d in range(D):
        kron_ref[slot, d * D : (d + 1) * D, :] = (first[d : d + 1, :] * second).astype(BF16)


def pick(value, index):
    return jnp.take_along_axis(value, index, axis=1, mode="promise_in_bounds")


def row_of(value, k):
    return jnp.broadcast_to(value[k : k + 1, :], value.shape)


def bond_open(msg_sum, twist_sum):
    D = msg_sum.shape[0]
    lane = iota((D, LANES), 1)
    row = iota((D, LANES), 0)
    inner = lane & (D - 1)
    turned = lane - inner + row
    g0, g1 = math.cosh(COUPLING), math.sinh(COUPLING)
    cross = math.sqrt(g0 * g1)
    root2 = math.sqrt(2.0)
    halves = [
        ((g0 * msg_sum + cross * twist_sum) / root2).astype(BF16).astype(F32),
        ((cross * twist_sum + g1 * msg_sum) / root2).astype(BF16).astype(F32),
    ]
    squares = halves[0] * halves[0] + halves[1] * halves[1]
    squares = jnp.broadcast_to(jnp.sum(squares, axis=0, keepdims=True), (D, LANES))
    trace = jnp.sum(pick(squares, turned), axis=0, keepdims=True) + EPSILON

    gram = None
    rotated = []
    for half in halves:
        transposed = None
        for k in range(D):
            own = row_of(half, k)
            column = pick(own, turned)
            term = column * own
            gram = term if gram is None else gram + term
            placed = jnp.where(inner == k, column, 0.0)
            transposed = placed if transposed is None else transposed + placed
        rotated.append(transposed)

    return gram / trace, rotated, jnp.broadcast_to(trace, (D, LANES))


def bond_tools(D):
    lane = iota((D, LANES), 1)
    row = iota((D, LANES), 0)
    inner = lane & (D - 1)
    turned = lane - inner + row
    unit = jnp.where(inner == row, 1.0, 0.0).astype(F32)

    def columns(value):
        return [pick(row_of(value, k), turned) for k in range(D)]

    def times(left, right):
        sums = [None] * 4
        for k in range(D):
            term = left[k] * row_of(right, k)
            sums[k % 4] = term if sums[k % 4] is None else sums[k % 4] + term
        return (sums[0] + sums[1]) + (sums[2] + sums[3])

    return unit, columns, times


def bond_step(state, rotated):
    unit, columns, times = bond_tools(state.shape[0])
    left = columns(state)
    square = times(left, state)
    rotated = [1.5 * v - 0.5 * times(left, v) for v in rotated]
    state = times(left, 2.25 * unit - 1.5 * state + 0.25 * square)
    return state, rotated


def bond_close(state, rotated, trace):
    _, columns, times = bond_tools(state.shape[0])
    left = columns(state)
    rotated = [1.5 * v - 0.5 * times(left, v) for v in rotated]
    again = rotated
    for _ in range(2):
        again = [1.5 * v - 0.5 * times(left, v) for v in again]
    rotated = [1.5 * v - 0.5 * times(left, w) for v, w in zip(rotated, again)]
    scale = 1.0 / jnp.sqrt(trace)
    first = math.sqrt(math.cosh(COUPLING)) * rotated[0] * scale
    second = math.sqrt(math.sinh(COUPLING)) * rotated[1] * scale
    return [first + second, first - second]


def unmixing(D, mixed, out_axis):
    DD = D * D
    sub = D // mixed
    p, k = iota((DD, DD), out_axis), iota((DD, DD), 1 - out_axis)
    low = p & (D - 1)
    mid = (p >> (D.bit_length() - 1)) & (sub - 1)
    top = p >> (D * sub).bit_length() - 1
    return one_hot(k == low * D + mid * mixed + top)


def messages_kernel(tiles, groups, cols, D, a_hbm, msg_hbm, ax_ref, env_ref, inner_ref, mout_ref,
           a_ref, msg_ref, other_ref, x_ref, xt_ref, xq_ref, x2_ref, x2t_ref, kron_ref, gram_ref,
           send_v0, send_v1, send_s0, send_s1, _, send_f1, up_0, up_1, down_0, down_1, side_0, side_1,
           send_sem, recv_sem, load_sem):
    loads = [pltpu.make_async_copy(msg_hbm, msg_ref, load_sem.at[cols])]
    loads += [
        pltpu.make_async_copy(a_hbm.at[i], a_ref.at[i], load_sem.at[i]) for i in range(cols)
    ]
    for load in loads:
        load.start()
    tile = lax.axis_index("tile")
    group = lax.axis_index("group")
    DD = D * D
    shift = D.bit_length() - 1
    halves = DD // LANES
    mixed = 2 * halves
    sub = D // mixed
    per = LANES // D
    legs = 4 * cols
    crossing = jnp.where(group == 0, cols - 1, 0)
    closed = jnp.where(group == 0, 0, cols - 1)
    order = list(range(1, cols - 1)) + [closed, crossing]
    has_up = tile > 0
    has_down = tile < tiles - 1
    far_path = lax.rem(tile, 2)
    far_up = far_path == 0
    far_down = jnp.logical_not(far_up)
    swap_sides = far_path == group
    cross_slot = jnp.where(group == 0, cols + crossing, crossing)
    other_slot = jnp.where(group == 0, crossing, cols + crossing)

    barrier = pltpu.get_barrier_semaphore()

    @pl.when(has_up)
    def _():
        pl.semaphore_signal(barrier, inc=1, device_id={"tile": tile - 1}, device_id_type=MESH)

    @pl.when(has_down)
    def _():
        pl.semaphore_signal(barrier, inc=1, device_id={"tile": tile + 1}, device_id_type=MESH)

    pl.semaphore_signal(barrier, inc=1, device_id={"group": 1 - group}, device_id_type=MESH)

    lane = iota((D, LANES), 1)
    row = iota((D, LANES), 0)
    within = lane & (D - 1)
    turned = lane - within + row
    slot = lane >> shift
    gather = unmixing(D, mixed, 0)
    fold_minor = one_hot((iota((LANES, LANES), 0) & (D - 1)) == (iota((LANES, LANES), 1) & (D - 1)))
    fold_major = one_hot((iota((DD, LANES), 0) >> shift) == (iota((DD, LANES), 1) & (D - 1)))

    def placed(entries):
        total = jnp.zeros((D, LANES), F32)
        for where, value in entries:
            total = jnp.where(slot == where, value, total)
        return total

    def by_major(value, m):
        return jnp.concatenate([pick(value, m * D + slot + h * per) for h in range(halves)], axis=1)

    def by_minor(value, m):
        return jnp.concatenate([pick(value, m * D + within)] * halves, axis=1)

    def rounded(value):
        return value.astype(BF16).astype(F32)

    def reduce_major(gram, weight):
        total = gram[:D] * weight[0:1, :]
        for d in range(1, D):
            total = total + gram[d * D : (d + 1) * D] * weight[d : d + 1, :]
        return total

    sublane = iota((8, DD), 0)

    def reduce_minor(gram, weight):
        blocks = []
        for d in range(D):
            block = gram[d * D : (d + 1) * D] * weight
            total = block[:8]
            for h in range(1, D // 8):
                total = total + block[h * 8 : (h + 1) * 8]
            blocks.append(total)
        out = []
        for base in range(0, D, 8):
            level = blocks[base : base + 8]
            step = 1
            while len(level) > 1:
                low = (sublane & step) == 0
                level = [
                    jnp.where(low, level[n], level[n + 1])
                    + pltpu.roll(jnp.where(low, level[n + 1], level[n]), step, 0)
                    for n in range(0, len(level), 2)
                ]
                step *= 2
            out.append(level[0])
        return jnp.concatenate(out, axis=0)

    def kinds_of(totals):
        if len(totals) == 1:
            return totals
        return [totals[0] + totals[1], totals[0] - totals[1]]

    def folded(totals, selector):
        pieces = []
        for total in totals:
            if selector is fold_minor:
                joined = total[:, :LANES]
                for h in range(1, halves):
                    joined = joined + total[:, h * LANES : (h + 1) * LANES]
                total = joined
            pieces += parts(total, 2)
        out = dot(jnp.concatenate(pieces, axis=0), selector)
        return [
            out[2 * n * D : (2 * n + 1) * D] + out[(2 * n + 1) * D : (2 * n + 2) * D]
            for n in range(len(totals))
        ]

    def minors(totals):
        count = len(totals[0])
        flat = folded([v for t in totals for v in t], fold_minor)
        return [flat[n * count : (n + 1) * count] for n in range(len(totals))]

    def majors(totals):
        count = len(totals[0])
        flat = folded([v for t in totals for v in t], fold_major)
        return [flat[n * count : (n + 1) * count] for n in range(len(totals))]

    def normalised(values):
        power = jnp.sum(values[0] * values[0], axis=0, keepdims=True)
        power = pick(jnp.broadcast_to(power, (D, LANES)), turned)
        power = jnp.sum(power, axis=0, keepdims=True) / DD
        scale = 1.0 / jnp.sqrt(power + EPSILON)
        return [v * scale for v in values]

    def upright(ups, downs, kind):
        return placed(
            [(i, ups[i][kind]) for i in range(cols)]
            + [(cols + i, downs[i][kind]) for i in range(cols)]
        )

    def copy(src, dst, turn, k, device):
        return pltpu.make_async_remote_copy(
            src_ref=src, dst_ref=dst, send_sem=send_sem.at[turn, k],
            recv_sem=recv_sem.at[turn, k], device_id=device, device_id_type=MESH,
        )

    def above_arrives(sent, arriving, dst, edges):
        @pl.when(has_up)
        def _():
            sent.wait_send()
            arriving.wait_recv()

        @pl.when(jnp.logical_not(has_up))
        def _():
            dst[...] = edges

    def below_arrives(sent, arriving, dst, edges):
        @pl.when(has_down)
        def _():
            sent.wait_send()
            arriving.wait_recv()

        @pl.when(jnp.logical_not(has_down))
        def _():
            dst[...] = edges

    def joined_rows(above, below):
        return [
            jnp.where(slot < cols, above[k * D : (k + 1) * D], below[k * D : (k + 1) * D])
            for k in range(above.shape[0] // D)
        ]

    from_left = (slot == 0) | (slot == 2 * cols)
    from_right = (slot == 2 * cols - 1) | (slot == 2 * cols + 1)

    def joined_sides(dst, local, edges):
        got = dst[...]
        out = []
        for k, (value, edge) in enumerate(zip(local, edges)):
            other = got[k * D : (k + 1) * D]
            value = jnp.where(from_left, jnp.where(group == 0, edge, other), value)
            out.append(
                jnp.where(from_right, jnp.where(group == groups - 1, edge, other), value)
            )
        return out

    loads[0].wait()
    spot = (row & (per - 1)) * D + within
    flat = msg_ref[...].reshape(legs, DD)

    def unfolded(m):
        source = jnp.concatenate(
            [
                jnp.broadcast_to(flat[m : m + 1, h * LANES : (h + 1) * LANES], (per, LANES))
                for h in range(halves)
            ],
            axis=0,
        )
        return pick(source, spot)

    singles = [unfolded(m) for m in range(legs)]
    edge_rows = placed(
        [(i, singles[4 * i]) for i in range(cols)]
        + [(cols + i, singles[4 * i + 2]) for i in range(cols)]
    )
    edge_sides = placed(
        [(i, singles[4 * i + 1]) for i in range(cols)]
        + [(cols + i, singles[4 * i + 3]) for i in range(cols)]
    )

    def unmix(i):
        for b in range(0, mixed, 2):
            pair = jnp.concatenate(
                [
                    jnp.concatenate(
                        [
                            a_ref[i, u * D * mixed + (b + c) * D : u * D * mixed + (b + c + 1) * D]
                            for u in range(D)
                        ],
                        axis=0,
                    )
                    for c in range(2)
                ],
                axis=1,
            )
            block = dot(gather, pair).astype(BF16)
            span = sub * D
            for c in range(2):
                for g in range(mixed):
                    x_ref[
                        i,
                        g % 2,
                        (b + c) * span : (b + c + 1) * span,
                        (g // 2) * LANES : (g // 2 + 1) * LANES,
                    ] = block[g * span : (g + 1) * span, c * LANES : (c + 1) * LANES]

    def exchanged(groups_of, masks, unit_lanes):
        step = 1
        for high in masks:
            following = []
            for values in groups_of:
                out = list(values)
                for a in range(len(values)):
                    if a & step:
                        continue
                    b = a | step
                    low_up = pltpu.roll(values[b], unit_lanes * step, 1)
                    high_down = pltpu.roll(values[a], LANES - unit_lanes * step, 1)
                    out[a] = jnp.where(high[0], low_up, values[a])
                    out[b] = jnp.where(high[1], values[b], high_down)
                following.append(out)
            groups_of = following
            step *= 2
        return groups_of

    def relayout(j, s):
        bits = per.bit_length() - 1
        masks = [((slot & (1 << n)) != 0,) * 2 for n in range(bits)]
        blocks = [(h, lh) for h in range(halves) for lh in range(halves)]
        groups_of = [
            [
                x_ref[
                    order[j], s, (lh * per + k) * D : (lh * per + k + 1) * D,
                    h * LANES : (h + 1) * LANES,
                ]
                for k in range(per)
            ]
            for h, lh in blocks
        ]
        for (h, lh), values in zip(blocks, exchanged(groups_of, masks, D)):
            for d in range(per):
                x2_ref[
                    j, s, (h * per + d) * D : (h * per + d + 1) * D,
                    lh * LANES : (lh + 1) * LANES,
                ] = values[d]
        x2t_ref[j, s] = x2_ref[j, s].T

    def cross_layout(s):
        shut = jnp.where(swap_sides, 0, 1)
        masks = []
        for n in range(shift):
            bit = (lane >> n) & 1
            masks.append(((bit & (1 - shut)) != 0, (bit | shut) != 0))
        groups_of = [
            [
                x_ref[crossing, s, k * D : (k + 1) * D, h * LANES : (h + 1) * LANES]
                for k in range(D)
            ]
            for h in range(halves)
        ]
        for h, values in enumerate(exchanged(groups_of, masks, 1)):
            for k in range(D):
                xq_ref[0, s, k * D : (k + 1) * D, h * LANES : (h + 1) * LANES] = values[k]
        xq_ref[1, s] = xq_ref[0, s].T

    v_rows, v_sides = rounded(edge_rows), rounded(edge_sides)
    weights = []
    for i in range(cols):
        w_up, w_down = by_minor(v_rows, i), by_major(v_rows, cols + i)
        w_left, w_right = by_major(v_sides, i), by_minor(v_sides, cols + i)
        weights.append((w_up, w_down, w_left, w_right))
        build_kron(kron_ref, 2 * i, w_down, w_right)
        build_kron(kron_ref, 2 * i + 1, w_left, w_up)
    for load in loads[1:]:
        load.wait()
    for i in range(cols):
        unmix(i)
    for i in range(cols):
        for s in range(2):
            xt_ref[i, s] = x_ref[i, s].T
    sides_of = ((x_ref, xt_ref), (xt_ref, x_ref))

    def first_gram(path, i):
        left, right = sides_of[path]
        y = [dot(left[i, s], kron_ref[2 * i + path]).astype(BF16) for s in range(2)]
        gram_ref[2 * i + path, 0] = dot(
            jnp.concatenate(y, axis=1), right[i].reshape(2 * DD, DD)
        )

    def outer(i, leg):
        w_up, w_down, w_left, w_right = weights[i]
        if leg == 0:
            return [reduce_major(gram_ref[2 * i, 0], w_left)]
        if leg == 1:
            return [reduce_minor(gram_ref[2 * i, 0], w_up)]
        if leg == 2:
            return [reduce_minor(gram_ref[2 * i + 1, 0], w_right)]
        return [reduce_major(gram_ref[2 * i + 1, 0], w_down)]

    first_gram(0, 0)
    first_gram(1, cols - 1)
    for i in range(1, cols):
        first_gram(0, i)
    for i in range(cols - 1):
        first_gram(1, i)
    (left_first,), (right_last,) = majors([outer(0, 1)]), minors([outer(cols - 1, 3)])
    send_s0[...] = normalised([jnp.where(from_left, right_last[0], left_first[0])])[0]
    ups = [outer(i, 0) for i in range(cols)]

    mix = jnp.full((D, DD), math.tanh(FIELD), BF16)
    for i in range(cols):
        for d in range(0, DD, D):
            a0, a1 = (x_ref[i, s, d : d + D] for s in range(2))
            ax_ref[i, 0, d : d + D] = a0 + mix * a1
            ax_ref[i, 1, d : d + D] = a1 + mix * a0

    inside = jnp.logical_and(has_up, has_down)

    @pl.when(inside)
    def _():
        pl.semaphore_wait(barrier, 3)

    @pl.when(jnp.logical_not(inside))
    def _():
        pl.semaphore_wait(barrier, 2)

    sides_0 = copy(send_s0, side_0, 0, 2, {"group": 1 - group})
    sides_0.start()
    downs = majors([outer(i, 2) for i in range(cols)])
    ups = minors(ups)
    send_v0[...] = normalised([upright(downs, ups, 0)])[0]
    to_up = copy(send_v0, down_0, 0, 0, {"tile": tile - 1})
    to_down = copy(send_v0, up_0, 0, 1, {"tile": tile + 1})

    @pl.when(has_up)
    def _():
        to_up.start()

    @pl.when(has_down)
    def _():
        to_down.start()

    for s in range(2):
        cross_layout(s)
    for j in range(cols - 1):
        for s in range(2):
            relayout(j, s)

    lefts = [left_first] + majors([outer(i, 1) for i in range(1, cols)])
    rights = minors([outer(i, 3) for i in range(cols - 1)]) + [right_last]

    def inner_view(lefts, rights, kind):
        return placed(
            [(i, rights[i - 1][kind]) for i in range(1, cols)]
            + [(cols + i, lefts[i + 1][kind]) for i in range(cols - 1)]
        )

    n_sides = normalised([inner_view(lefts, rights, 0)])

    def above_0():
        above_arrives(to_up, to_down, up_0, edge_rows)

    def below_0():
        below_arrives(to_down, to_up, down_0, edge_rows)

    side_weights = []

    def paired(j, kron, left, right, at):
        for s in range(2):
            y = dot(left[j, s], kron_ref[kron]).astype(BF16)
            gram_ref[at, s] = dot_nt(y, x2_ref[j, s]) if right is x2t_ref else dot(y, right[j, s])

    v_sides = rounded(jnp.where(from_left | from_right, edge_sides, n_sides[0]))
    for j in range(cols - 1):
        i = order[j]
        w_left, w_right = by_major(v_sides, i), by_minor(v_sides, cols + i)
        side_weights.append((w_left, w_right))
        build_kron(kron_ref, 2 * j, w_left, w_right)
        paired(j, 2 * j, x2_ref, x2t_ref, 2 * j)
    other_major, other_minor = by_major(v_sides, other_slot), by_minor(v_sides, other_slot)

    final = 2 * (cols - 1)

    def crossing_gram(first, second, path):
        build_kron(kron_ref, final, first, second)
        for s in range(2):
            y = dot(xq_ref[path, s], kron_ref[final]).astype(BF16)
            gram_ref[final, s] = dot_nt(y, xq_ref[path, s])

    def all_sides():
        return rounded(joined_sides(side_0, n_sides, [edge_sides])[0])

    def up_legs(weight, j):
        return kinds_of([reduce_major(gram_ref[2 * j, s], weight) for s in range(2)])

    def down_legs(weight, j):
        return kinds_of([reduce_minor(gram_ref[2 * j, s], weight) for s in range(2)])

    def ship(buffer, values):
        for k in range(2):
            buffer[k * D : (k + 1) * D] = values[k]

    def ordered(above, below, kind):
        return placed(
            [(order[j], above[j][kind]) for j in range(cols)]
            + [(cols + order[j], below[j][kind]) for j in range(cols)]
        )

    nothing = [[jnp.zeros((D, LANES), F32)] * 2] * cols
    up_far = copy(send_f1, down_1, 1, 0, {"tile": tile - 1})
    up_near = copy(send_v1, down_1, 1, 0, {"tile": tile - 1})
    down_far = copy(send_f1, up_1, 1, 1, {"tile": tile + 1})
    down_near = copy(send_v1, up_1, 1, 1, {"tile": tile + 1})

    sides_1 = copy(send_s1, side_1, 1, 2, {"group": 1 - group})

    def cross_major(at, weight):
        return kinds_of([reduce_major(gram_ref[at, s], weight) for s in range(2)])

    def cross_minor(at, weight):
        return kinds_of([reduce_minor(gram_ref[at, s], weight) for s in range(2)])

    @pl.when(far_up)
    def _():
        below_0()
        near = rounded(down_0[...])
        crossing_gram(by_major(near, cols + crossing), other_minor, 0)
        early = [up_legs(by_major(near, cols + order[j]), j) for j in range(cols - 1)]
        early = minors(early)
        sides_0.wait()
        weight = by_major(all_sides(), cross_slot)
        legs_up = early + minors([cross_major(final, weight)])
        ship(send_f1, normalised([ordered(nothing, legs_up, k) for k in range(2)]))

        @pl.when(has_up)
        def _():
            up_far.start()

        above_0()
        weight = by_minor(rounded(up_0[...]), crossing)
        (cross,) = majors([cross_minor(final, weight)])
        ship(send_s1, normalised(cross))
        sides_1.start()

    @pl.when(far_down)
    def _():
        above_0()
        near = rounded(up_0[...])
        crossing_gram(other_major, by_minor(near, crossing), 1)
        early = [down_legs(by_minor(near, order[j]), j) for j in range(cols - 1)]
        early = majors(early)
        sides_0.wait()
        weight = by_minor(all_sides(), cross_slot)
        legs_down = early + majors([cross_minor(final, weight)])
        ship(send_f1, normalised([ordered(legs_down, nothing, k) for k in range(2)]))

        @pl.when(has_down)
        def _():
            down_far.start()

        below_0()
        weight = by_major(rounded(down_0[...]), cols + crossing)
        (cross,) = minors([cross_major(final, weight)])
        ship(send_s1, normalised(cross))
        sides_1.start()

    v_rows = rounded(joined_rows(up_0[...], down_0[...])[0])
    weights = []
    for j in range(cols):
        i = order[j]
        weights.append((by_minor(v_rows, i), by_major(v_rows, cols + i)))
    v_sides = all_sides()
    cross_first, cross_second = by_major(v_sides, cross_slot), by_minor(v_sides, cross_slot)

    def horizontal_gram(j):
        build_kron(kron_ref, 2 * j + 1, weights[j][1], weights[j][0])
        paired(j, 2 * j + 1, x2t_ref, x2_ref, 2 * j + 1)

    def horizontal(j):
        w_left, w_right = side_weights[j]
        left = kinds_of([reduce_minor(gram_ref[2 * j + 1, s], w_right) for s in range(2)])
        right = kinds_of([reduce_major(gram_ref[2 * j + 1, s], w_left) for s in range(2)])
        return left, right

    def last_gram(first, second, path):
        build_kron(kron_ref, final + 1, first, second)
        for s in range(2):
            y = dot(xq_ref[path, s], kron_ref[final + 1]).astype(BF16)
            gram_ref[final + 1, s] = dot(y, xq_ref[1 - path, s])

    @pl.when(far_up)
    def _():
        last_gram(cross_first, weights[-1][0], 1)
        for j in range(cols - 1):
            horizontal_gram(j)
        near = [down_legs(weights[j][0], j) for j in range(cols - 1)]
        near = majors(near + [cross_minor(final + 1, other_minor)])
        ship(send_v1, normalised([ordered(near, nothing, k) for k in range(2)]))
        (other,) = minors([cross_major(final + 1, weights[-1][1])])
        for k in range(2):
            other_ref[k] = other[k]

        @pl.when(has_down)
        def _():
            down_near.start()

    @pl.when(far_down)
    def _():
        last_gram(weights[-1][1], cross_second, 0)
        for j in range(cols - 1):
            horizontal_gram(j)
        near = [up_legs(weights[j][1], j) for j in range(cols - 1)]
        near = minors(near + [cross_major(final + 1, other_major)])
        ship(send_v1, normalised([ordered(nothing, near, k) for k in range(2)]))
        (other,) = majors([cross_minor(final + 1, weights[-1][0])])
        for k in range(2):
            other_ref[k] = other[k]

        @pl.when(has_up)
        def _():
            up_near.start()

    half = cols * D
    swapped = jnp.where(
        slot < cols, lane + half, jnp.where(slot < 2 * cols, lane - half, lane)
    )
    o_rows = [
        pick(send_f1[k * D : (k + 1) * D] + send_v1[k * D : (k + 1) * D], swapped)
        for k in range(2)
    ]
    others = [horizontal(j) for j in range(cols - 1)]
    lefts = majors([o[0] for o in others])
    rights = minors([o[1] for o in others])

    def own_sides(kind):
        return placed(
            [(order[j], lefts[j][kind]) for j in range(cols - 1)]
            + [(cols + order[j], rights[j][kind]) for j in range(cols - 1)]
            + [(other_slot, other_ref[kind])]
        )

    def other_sides(kind):
        entries = []
        for j in range(cols - 1):
            i = order[j]
            entries.append((jnp.where(i == 0, -1, cols + i - 1), lefts[j][kind]))
            entries.append((jnp.where(i == cols - 1, -1, i + 1), rights[j][kind]))
        entries.append((jnp.where(group == 0, cols + crossing - 1, 1), other_ref[kind]))
        return placed(entries)

    is_cross = (slot == cross_slot) | (slot == jnp.where(group == 0, 2 * cols + 1, 2 * cols))
    o_sides = [
        jnp.where(is_cross, send_s1[k * D : (k + 1) * D], value)
        for k, value in enumerate(normalised([own_sides(k) for k in range(2)]))
    ]
    n_sides = normalised([other_sides(k) for k in range(2)])
    state, rotated, trace = bond_open(*[o + n for o, n in zip(o_sides, n_sides)])
    for step in range(EARLY_STEPS):
        state, rotated = bond_step(state, rotated)
    for n, value in enumerate([state] + rotated + [trace]):
        inner_ref[n] = value
    zero = jnp.zeros((D, LANES), F32)
    sides_1.wait()
    n_sides = joined_sides(side_1, n_sides, [edge_sides, zero])
    rows_edges = jnp.concatenate([edge_rows, zero], axis=0)
    above_arrives(up_near, down_near, up_1, rows_edges)
    below_arrives(down_near, up_near, down_1, rows_edges)
    n_rows = joined_rows(up_1[...], down_1[...])
    for k in range(2):
        env_ref[k] = jnp.where(
            slot < 2 * cols, o_rows[k] + n_rows[k], o_sides[k] + n_sides[k]
        )
    mout_ref[0] = n_rows[0]
    mout_ref[1] = n_sides[0]


def gates_kernel(tiles, groups, cols, D, ax_ref, env_ref, inner_ref, in_ref, out_hbm, mout_hbm,
                 kron_ref, out_ref, mout_ref, early_ref, fence_ref, store_sem):
    tile = lax.axis_index("tile")
    group = lax.axis_index("group")
    DD = D * D
    shift = D.bit_length() - 1
    halves = DD // LANES
    mixed = 2 * halves
    rows = DD // mixed
    lane = iota((D, LANES), 1)
    row = iota((D, LANES), 0)
    inner = lane & (D - 1)
    start = lane - inner
    slot = lane >> shift

    unit = jnp.where(inner == row, 1.0, 0.0).astype(F32)
    at_edge = (
        ((slot < cols) & (tile == 0))
        | ((slot >= cols) & (slot < 2 * cols) & (tile == tiles - 1))
        | ((slot == 2 * cols) & (group == 0))
        | ((slot == 2 * cols + 1) & (group == groups - 1))
    )
    fence = pltpu.make_async_copy(env_ref.at[0], fence_ref, store_sem.at[cols + 1])
    fence.start()
    state, rotated, trace = bond_open(env_ref[0], env_ref[1])
    begun, turning = inner_ref[0], [inner_ref[1], inner_ref[2]]
    early_left = NS_STEPS - 2 - EARLY_STEPS
    for step in range(NS_STEPS - 2):
        if step < early_left:
            begun, turning = bond_step(begun, turning)
        elif step == early_left:
            for s, weight in enumerate(bond_close(begun, turning, inner_ref[3])):
                early_ref[s] = weight.astype(BF16).astype(F32)
        state, rotated = bond_step(state, rotated)
        if step == FENCE_STEP:
            fence.wait()
    early = [early_ref[s] for s in range(2)]
    late = [
        jnp.where(at_edge, unit, w).astype(BF16).astype(F32)
        for w in bond_close(state, rotated, trace)
    ]

    unfold_mask = slot == (row & (LANES // D - 1))
    flat_rows = []
    for m in range(4 * cols):
        at = m // 4 + (cols if m % 4 >= 2 else 0)
        tiled = jnp.where(unfold_mask, pick(in_ref[m % 2], inner + at * D), 0.0)
        step = D // halves
        flat_rows.append(
            jnp.concatenate(
                [
                    jnp.sum(tiled[h * step : (h + 1) * step], axis=0, keepdims=True)
                    for h in range(halves)
                ],
                axis=1,
            )
        )
    mout_ref[...] = jnp.concatenate(flat_rows, axis=0).reshape(cols, 4, DD)
    store_msg = pltpu.make_async_copy(mout_ref, mout_hbm, store_sem.at[cols])
    store_msg.start()

    def by_major(value, m):
        return jnp.concatenate(
            [pick(value, m * D + slot + h * (LANES // D)) for h in range(halves)], axis=1
        )

    def by_minor(value, m):
        part = pick(value, m * D + inner)
        return jnp.concatenate([part] * halves, axis=1)

    scatter = unmixing(D, mixed, 1)
    stores = [
        pltpu.make_async_copy(out_ref.at[i], out_hbm.at[i], store_sem.at[i]) for i in range(cols)
    ]

    for i in range(cols):
        for s in range(2):
            left = by_major(late[s], 2 * cols) if i == 0 else by_major(early[s], i)
            right = (
                by_minor(late[s], 2 * cols + 1) if i == cols - 1 else by_minor(early[s], i + 1)
            )
            at = (i * 2 + s) * 2
            down = math.cosh(FIELD) * by_major(late[s], cols + i)
            build_kron(kron_ref, at, down, right)
            build_kron(kron_ref, at + 1, left, by_minor(late[s], i))
    gated = [
        [dot_nt(ax_ref[i, s], kron_ref[(i * 2 + s) * 2]).astype(BF16) for s in range(2)]
        for i in range(cols)
    ]
    gated = [
        [dot(kron_ref[(i * 2 + s) * 2 + 1], gated[i][s]).astype(BF16) for s in range(2)]
        for i in range(cols)
    ]

    def emit(i, gated):
        for b in range(0, mixed, 2):
            block = jnp.concatenate(
                [
                    jnp.concatenate(
                        [
                            gated[g % 2][
                                (b + c) * rows : (b + c + 1) * rows,
                                (g // 2) * LANES : (g // 2 + 1) * LANES,
                            ]
                            for c in range(2)
                        ],
                        axis=1,
                    )
                    for g in range(mixed)
                ],
                axis=0,
            )
            done = dot(scatter, block).astype(BF16)
            for c in range(2):
                for u in range(D):
                    at = u * D * mixed + (b + c) * D
                    out_ref[i, at : at + D, :] = done[
                        u * D : (u + 1) * D, c * LANES : (c + 1) * LANES
                    ]
        stores[i].start()

    for i in range(cols):
        emit(i, gated[i])
    for store in stores + [store_msg]:
        store.wait()


def per_device(tiles, groups, site_tensors, msg_in):
    _, cols, _, size = site_tensors.shape
    DD = msg_in.shape[-1]
    D = math.isqrt(DD)
    chunks = size // LANES
    a = site_tensors.reshape(cols, 2, chunks, LANES).transpose(0, 2, 1, 3)
    a = a.reshape(cols, 2 * chunks, LANES)
    vmem = pl.BlockSpec(memory_space=pltpu.VMEM)
    hbm = pl.BlockSpec(memory_space=pltpu.HBM)
    gated, env, inner, stacked = pl.pallas_call(
        functools.partial(messages_kernel, tiles, groups, cols, D),
        out_shape=(
            jax.ShapeDtypeStruct((cols, 2, DD, DD), BF16),
            jax.ShapeDtypeStruct((2, D, LANES), F32),
            jax.ShapeDtypeStruct((4, D, LANES), F32),
            jax.ShapeDtypeStruct((2, D, LANES), F32),
        ),
        in_specs=[hbm, hbm],
        out_specs=(vmem, vmem, vmem, vmem),
        scratch_shapes=[
            pltpu.VMEM(a.shape, BF16),
            pltpu.VMEM((cols, 4, DD), F32),
            pltpu.VMEM((2, D, LANES), F32),
            pltpu.VMEM((cols, 2, DD, DD), BF16),
            pltpu.VMEM((cols, 2, DD, DD), BF16),
            pltpu.VMEM((2, 2, DD, DD), BF16),
            pltpu.VMEM((cols - 1, 2, DD, DD), BF16),
            pltpu.VMEM((cols - 1, 2, DD, DD), BF16),
            pltpu.VMEM((2 * cols, DD, DD), BF16),
            pltpu.VMEM((2 * cols, 2, DD, DD), F32),
        ]
        + [
            pltpu.VMEM(((1 + turn) * D, LANES), F32) for _ in range(6) for turn in range(ITERS)
        ]
        + [
            pltpu.SemaphoreType.DMA((ITERS, 3)),
            pltpu.SemaphoreType.DMA((ITERS, 3)),
            pltpu.SemaphoreType.DMA((cols + 1,)),
        ],
        compiler_params=pltpu.CompilerParams(
            collective_id=0, has_side_effects=True, vmem_limit_bytes=24 * 2**20
        ),
    )(
        pltpu.with_memory_space_constraint(a, pltpu.HBM),
        pltpu.with_memory_space_constraint(msg_in[0], pltpu.HBM),
    )
    out, messages = pl.pallas_call(
        functools.partial(gates_kernel, tiles, groups, cols, D),
        out_shape=(
            jax.ShapeDtypeStruct(a.shape, BF16),
            jax.ShapeDtypeStruct((cols, 4, DD), F32),
        ),
        in_specs=[vmem, vmem, vmem, vmem],
        out_specs=(hbm, hbm),
        scratch_shapes=[
            pltpu.VMEM((4 * cols, DD, DD), BF16),
            pltpu.VMEM(a.shape, BF16),
            pltpu.VMEM((cols, 4, DD), F32),
            pltpu.VMEM((2, D, LANES), F32),
            pltpu.VMEM((D, LANES), F32),
            pltpu.SemaphoreType.DMA((cols + 2,)),
        ],
        compiler_params=pltpu.CompilerParams(vmem_limit_bytes=24 * 2**20),
    )(gated, env, inner, stacked)
    out = out.reshape(cols, chunks, 2, LANES).transpose(0, 2, 1, 3)
    return out.reshape(1, cols, 2, size), messages[None]


def solution(mesh):
    spec = P("tile", "group", None, None)
    return jax.shard_map(
        functools.partial(per_device, mesh.shape["tile"], mesh.shape["group"]),
        mesh=mesh, in_specs=(spec, spec), out_specs=(spec, spec), check_vma=False,
    )
```

```python
import functools
import math

import jax
import jax.numpy as jnp
from jax import lax
from jax.experimental import pallas as pl
from jax.experimental.pallas import tpu as pltpu
from jax.sharding import PartitionSpec as P

ITERS = 2
NS_STEPS = 6
EARLY_STEPS = 2
FENCE_STEP = 2
LANES = 128
EPSILON = 1e-06
COUPLING = 0.5
FIELD = 0.3
F32 = jnp.float32
BF16 = jnp.bfloat16
MESH = pl.DeviceIdType.MESH


def iota(shape, axis):
    return lax.broadcasted_iota(jnp.int32, shape, axis)


def dot(a, b):
    return jnp.dot(a, b, preferred_element_type=F32)


def dot_nt(a, b):
    return lax.dot_general(a, b, (((1,), (1,)), ((), ())), preferred_element_type=F32)


def dot_tn(a, b):
    return lax.dot_general(a, b, (((0,), (0,)), ((), ())), preferred_element_type=F32)


def parts(value, count):
    out = []
    for _ in range(count):
        piece = value.astype(BF16)
        out.append(piece)
        value = value - piece.astype(F32)
    return out


def select_dot(value, selector, count):
    total = None
    for piece in parts(value, count):
        term = dot(piece, selector)
        total = term if total is None else total + term
    return total


def one_hot(mask):
    return jnp.where(mask, 1.0, 0.0).astype(BF16)


def build_kron(kron_ref, slot, first, second):
    D = first.shape[0]
    for d in range(D):
        kron_ref[slot, d * D : (d + 1) * D, :] = (first[d : d + 1, :] * second).astype(BF16)


def pick(value, index):
    return jnp.take_along_axis(value, index, axis=1, mode="promise_in_bounds")


def row_of(value, k):
    return jnp.broadcast_to(value[k : k + 1, :], value.shape)


def bond_open(msg_sum, twist_sum):
    D = msg_sum.shape[0]
    lane = iota((D, LANES), 1)
    row = iota((D, LANES), 0)
    inner = lane & (D - 1)
    turned = lane - inner + row
    g0, g1 = math.cosh(COUPLING), math.sinh(COUPLING)
    cross = math.sqrt(g0 * g1)
    root2 = math.sqrt(2.0)
    halves = [
        ((g0 * msg_sum + cross * twist_sum) / root2).astype(BF16).astype(F32),
        ((cross * twist_sum + g1 * msg_sum) / root2).astype(BF16).astype(F32),
    ]
    squares = halves[0] * halves[0] + halves[1] * halves[1]
    squares = jnp.broadcast_to(jnp.sum(squares, axis=0, keepdims=True), (D, LANES))
    trace = jnp.sum(pick(squares, turned), axis=0, keepdims=True) + EPSILON

    gram = None
    rotated = []
    for half in halves:
        transposed = None
        for k in range(D):
            own = row_of(half, k)
            column = pick(own, turned)
            term = column * own
            gram = term if gram is None else gram + term
            placed = jnp.where(inner == k, column, 0.0)
            transposed = placed if transposed is None else transposed + placed
        rotated.append(transposed)

    return gram / trace, rotated, jnp.broadcast_to(trace, (D, LANES))


def bond_tools(D):
    lane = iota((D, LANES), 1)
    row = iota((D, LANES), 0)
    inner = lane & (D - 1)
    turned = lane - inner + row
    unit = jnp.where(inner == row, 1.0, 0.0).astype(F32)

    def columns(value):
        return [pick(row_of(value, k), turned) for k in range(D)]

    def times(left, right):
        sums = [None] * 4
        for k in range(D):
            term = left[k] * row_of(right, k)
            sums[k % 4] = term if sums[k % 4] is None else sums[k % 4] + term
        return (sums[0] + sums[1]) + (sums[2] + sums[3])

    return unit, columns, times


def bond_step(state, rotated):
    unit, columns, times = bond_tools(state.shape[0])
    left = columns(state)
    square = times(left, state)
    rotated = [1.5 * v - 0.5 * times(left, v) for v in rotated]
    state = times(left, 2.25 * unit - 1.5 * state + 0.25 * square)
    return state, rotated


def bond_close(state, rotated, trace):
    _, columns, times = bond_tools(state.shape[0])
    left = columns(state)
    rotated = [1.5 * v - 0.5 * times(left, v) for v in rotated]
    again = rotated
    for _ in range(2):
        again = [1.5 * v - 0.5 * times(left, v) for v in again]
    rotated = [1.5 * v - 0.5 * times(left, w) for v, w in zip(rotated, again)]
    scale = 1.0 / jnp.sqrt(trace)
    first = math.sqrt(math.cosh(COUPLING)) * rotated[0] * scale
    second = math.sqrt(math.sinh(COUPLING)) * rotated[1] * scale
    return [first + second, first - second]


def unmixing(D, mixed, out_axis):
    DD = D * D
    sub = D // mixed
    p, k = iota((DD, DD), out_axis), iota((DD, DD), 1 - out_axis)
    low = p & (D - 1)
    mid = (p >> (D.bit_length() - 1)) & (sub - 1)
    top = p >> (D * sub).bit_length() - 1
    return one_hot(k == low * D + mid * mixed + top)


def messages_kernel(tiles, groups, cols, D, a_hbm, msg_hbm, ax_ref, env_ref, inner_ref, mout_ref,
           a_ref, msg_ref, other_ref, x_ref, xt_ref, xq_ref, x2_ref, x2t_ref, kron_ref, gram_ref,
           send_v0, send_v1, send_s0, send_s1, _, send_f1, up_0, up_1, down_0, down_1, side_0, side_1,
           send_sem, recv_sem, load_sem):
    loads = [pltpu.make_async_copy(msg_hbm, msg_ref, load_sem.at[cols])]
    loads += [
        pltpu.make_async_copy(a_hbm.at[i], a_ref.at[i], load_sem.at[i]) for i in range(cols)
    ]
    for load in loads:
        load.start()
    tile = lax.axis_index("tile")
    group = lax.axis_index("group")
    DD = D * D
    shift = D.bit_length() - 1
    halves = DD // LANES
    mixed = 2 * halves
    sub = D // mixed
    per = LANES // D
    legs = 4 * cols
    crossing = jnp.where(group == 0, cols - 1, 0)
    closed = jnp.where(group == 0, 0, cols - 1)
    order = list(range(1, cols - 1)) + [closed, crossing]
    has_up = tile > 0
    has_down = tile < tiles - 1
    far_path = lax.rem(tile, 2)
    far_up = far_path == 0
    far_down = jnp.logical_not(far_up)
    swap_sides = far_path == group
    cross_slot = jnp.where(group == 0, cols + crossing, crossing)
    other_slot = jnp.where(group == 0, crossing, cols + crossing)

    barrier = pltpu.get_barrier_semaphore()

    @pl.when(has_up)
    def _():
        pl.semaphore_signal(barrier, inc=1, device_id={"tile": tile - 1}, device_id_type=MESH)

    @pl.when(has_down)
    def _():
        pl.semaphore_signal(barrier, inc=1, device_id={"tile": tile + 1}, device_id_type=MESH)

    pl.semaphore_signal(barrier, inc=1, device_id={"group": 1 - group}, device_id_type=MESH)

    lane = iota((D, LANES), 1)
    row = iota((D, LANES), 0)
    within = lane & (D - 1)
    turned = lane - within + row
    slot = lane >> shift
    gather = unmixing(D, mixed, 0)
    fold_minor = one_hot((iota((LANES, LANES), 0) & (D - 1)) == (iota((LANES, LANES), 1) & (D - 1)))
    fold_major = one_hot((iota((DD, LANES), 0) >> shift) == (iota((DD, LANES), 1) & (D - 1)))

    def placed(entries):
        total = jnp.zeros((D, LANES), F32)
        for where, value in entries:
            total = jnp.where(slot == where, value, total)
        return total

    def by_major(value, m):
        return jnp.concatenate([pick(value, m * D + slot + h * per) for h in range(halves)], axis=1)

    def by_minor(value, m):
        return jnp.concatenate([pick(value, m * D + within)] * halves, axis=1)

    def rounded(value):
        return value.astype(BF16).astype(F32)

    def reduce_major(gram, weight):
        total = gram[:D] * weight[0:1, :]
        for d in range(1, D):
            total = total + gram[d * D : (d + 1) * D] * weight[d : d + 1, :]
        return total

    sublane = iota((8, DD), 0)

    def reduce_minor(gram, weight):
        blocks = []
        for d in range(D):
            block = gram[d * D : (d + 1) * D] * weight
            total = block[:8]
            for h in range(1, D // 8):
                total = total + block[h * 8 : (h + 1) * 8]
            blocks.append(total)
        out = []
        for base in range(0, D, 8):
            level = blocks[base : base + 8]
            step = 1
            while len(level) > 1:
                low = (sublane & step) == 0
                level = [
                    jnp.where(low, level[n], level[n + 1])
                    + pltpu.roll(jnp.where(low, level[n + 1], level[n]), step, 0)
                    for n in range(0, len(level), 2)
                ]
                step *= 2
            out.append(level[0])
        return jnp.concatenate(out, axis=0)

    def kinds_of(totals):
        if len(totals) == 1:
            return totals
        return [totals[0] + totals[1], totals[0] - totals[1]]

    def folded(totals, selector):
        pieces = []
        for total in totals:
            if selector is fold_minor:
                joined = total[:, :LANES]
                for h in range(1, halves):
                    joined = joined + total[:, h * LANES : (h + 1) * LANES]
                total = joined
            pieces += parts(total, 2)
        out = dot(jnp.concatenate(pieces, axis=0), selector)
        return [
            out[2 * n * D : (2 * n + 1) * D] + out[(2 * n + 1) * D : (2 * n + 2) * D]
            for n in range(len(totals))
        ]

    def minors(totals):
        count = len(totals[0])
        flat = folded([v for t in totals for v in t], fold_minor)
        return [flat[n * count : (n + 1) * count] for n in range(len(totals))]

    def majors(totals):
        count = len(totals[0])
        flat = folded([v for t in totals for v in t], fold_major)
        return [flat[n * count : (n + 1) * count] for n in range(len(totals))]

    def normalised(values):
        power = jnp.sum(values[0] * values[0], axis=0, keepdims=True)
        power = pick(jnp.broadcast_to(power, (D, LANES)), turned)
        power = jnp.sum(power, axis=0, keepdims=True) / DD
        scale = 1.0 / jnp.sqrt(power + EPSILON)
        return [v * scale for v in values]

    def upright(ups, downs, kind):
        return placed(
            [(i, ups[i][kind]) for i in range(cols)]
            + [(cols + i, downs[i][kind]) for i in range(cols)]
        )

    def copy(src, dst, turn, k, device):
        return pltpu.make_async_remote_copy(
            src_ref=src, dst_ref=dst, send_sem=send_sem.at[turn, k],
            recv_sem=recv_sem.at[turn, k], device_id=device, device_id_type=MESH,
        )

    def above_arrives(sent, arriving, dst, edges):
        @pl.when(has_up)
        def _():
            sent.wait_send()
            arriving.wait_recv()

        @pl.when(jnp.logical_not(has_up))
        def _():
            dst[...] = edges.astype(BF16)

    def below_arrives(sent, arriving, dst, edges):
        @pl.when(has_down)
        def _():
            sent.wait_send()
            arriving.wait_recv()

        @pl.when(jnp.logical_not(has_down))
        def _():
            dst[...] = edges.astype(BF16)

    def joined_rows(above, below):
        return [
            jnp.where(slot < cols, above[k * D : (k + 1) * D], below[k * D : (k + 1) * D])
            for k in range(above.shape[0] // D)
        ]

    from_left = (slot == 0) | (slot == 2 * cols)
    from_right = (slot == 2 * cols - 1) | (slot == 2 * cols + 1)

    def joined_sides(dst, local, edges):
        got = dst[...].astype(F32)
        out = []
        for k, (value, edge) in enumerate(zip(local, edges)):
            other = got[k * D : (k + 1) * D]
            value = jnp.where(from_left, jnp.where(group == 0, edge, other), value)
            out.append(
                jnp.where(from_right, jnp.where(group == groups - 1, edge, other), value)
            )
        return out

    loads[0].wait()
    spot = (row & (per - 1)) * D + within
    flat = msg_ref[...].reshape(legs, DD)

    def unfolded(m):
        source = jnp.concatenate(
            [
                jnp.broadcast_to(flat[m : m + 1, h * LANES : (h + 1) * LANES], (per, LANES))
                for h in range(halves)
            ],
            axis=0,
        )
        return pick(source, spot)

    singles = [unfolded(m) for m in range(legs)]
    edge_rows = placed(
        [(i, singles[4 * i]) for i in range(cols)]
        + [(cols + i, singles[4 * i + 2]) for i in range(cols)]
    )
    edge_sides = placed(
        [(i, singles[4 * i + 1]) for i in range(cols)]
        + [(cols + i, singles[4 * i + 3]) for i in range(cols)]
    )

    def unmix(i):
        for b in range(0, mixed, 2):
            pair = jnp.concatenate(
                [
                    jnp.concatenate(
                        [
                            a_ref[i, u * D * mixed + (b + c) * D : u * D * mixed + (b + c + 1) * D]
                            for u in range(D)
                        ],
                        axis=0,
                    )
                    for c in range(2)
                ],
                axis=1,
            )
            block = dot(gather, pair).astype(BF16)
            span = sub * D
            for c in range(2):
                for g in range(mixed):
                    x_ref[
                        i,
                        g % 2,
                        (b + c) * span : (b + c + 1) * span,
                        (g // 2) * LANES : (g // 2 + 1) * LANES,
                    ] = block[g * span : (g + 1) * span, c * LANES : (c + 1) * LANES]

    def exchanged(groups_of, masks, unit_lanes):
        step = 1
        for high in masks:
            following = []
            for values in groups_of:
                out = list(values)
                for a in range(len(values)):
                    if a & step:
                        continue
                    b = a | step
                    low_up = pltpu.roll(values[b], unit_lanes * step, 1)
                    high_down = pltpu.roll(values[a], LANES - unit_lanes * step, 1)
                    out[a] = jnp.where(high[0], low_up, values[a])
                    out[b] = jnp.where(high[1], values[b], high_down)
                following.append(out)
            groups_of = following
            step *= 2
        return groups_of

    def relayout(j, s):
        bits = per.bit_length() - 1
        masks = [((slot & (1 << n)) != 0,) * 2 for n in range(bits)]
        blocks = [(h, lh) for h in range(halves) for lh in range(halves)]
        groups_of = [
            [
                x_ref[
                    order[j], s, (lh * per + k) * D : (lh * per + k + 1) * D,
                    h * LANES : (h + 1) * LANES,
                ]
                for k in range(per)
            ]
            for h, lh in blocks
        ]
        for (h, lh), values in zip(blocks, exchanged(groups_of, masks, D)):
            for d in range(per):
                x2_ref[
                    j, s, (h * per + d) * D : (h * per + d + 1) * D,
                    lh * LANES : (lh + 1) * LANES,
                ] = values[d]
        x2t_ref[j, s] = x2_ref[j, s].T

    def cross_layout(s):
        shut = jnp.where(swap_sides, 0, 1)
        masks = []
        for n in range(shift):
            bit = (lane >> n) & 1
            masks.append(((bit & (1 - shut)) != 0, (bit | shut) != 0))
        groups_of = [
            [
                x_ref[crossing, s, k * D : (k + 1) * D, h * LANES : (h + 1) * LANES]
                for k in range(D)
            ]
            for h in range(halves)
        ]
        for h, values in enumerate(exchanged(groups_of, masks, 1)):
            for k in range(D):
                xq_ref[0, s, k * D : (k + 1) * D, h * LANES : (h + 1) * LANES] = values[k]
        xq_ref[1, s] = xq_ref[0, s].T

    v_rows, v_sides = rounded(edge_rows), rounded(edge_sides)
    weights = []
    for i in range(cols):
        w_up, w_down = by_minor(v_rows, i), by_major(v_rows, cols + i)
        w_left, w_right = by_major(v_sides, i), by_minor(v_sides, cols + i)
        weights.append((w_up, w_down, w_left, w_right))
        build_kron(kron_ref, 2 * i, w_down, w_right)
        build_kron(kron_ref, 2 * i + 1, w_left, w_up)
    for load in loads[1:]:
        load.wait()
    for i in range(cols):
        unmix(i)
    for i in range(cols):
        for s in range(2):
            xt_ref[i, s] = x_ref[i, s].T
    sides_of = ((x_ref, xt_ref), (xt_ref, x_ref))

    def first_gram(path, i):
        left, right = sides_of[path]
        y = [dot(left[i, s], kron_ref[2 * i + path]).astype(BF16) for s in range(2)]
        gram_ref[2 * i + path, 0] = dot(
            jnp.concatenate(y, axis=1), right[i].reshape(2 * DD, DD)
        )

    def outer(i, leg):
        w_up, w_down, w_left, w_right = weights[i]
        if leg == 0:
            return [reduce_major(gram_ref[2 * i, 0], w_left)]
        if leg == 1:
            return [reduce_minor(gram_ref[2 * i, 0], w_up)]
        if leg == 2:
            return [reduce_minor(gram_ref[2 * i + 1, 0], w_right)]
        return [reduce_major(gram_ref[2 * i + 1, 0], w_down)]

    first_gram(0, 0)
    first_gram(1, cols - 1)
    for i in range(1, cols):
        first_gram(0, i)
    for i in range(cols - 1):
        first_gram(1, i)
    (left_first,), (right_last,) = majors([outer(0, 1)]), minors([outer(cols - 1, 3)])
    (side_out,) = normalised([jnp.where(from_left, right_last[0], left_first[0])])
    send_s0[...] = side_out.astype(BF16)
    ups = [outer(i, 0) for i in range(cols)]

    mix = jnp.full((D, DD), math.tanh(FIELD), BF16)
    for i in range(cols):
        for d in range(0, DD, D):
            a0, a1 = (x_ref[i, s, d : d + D] for s in range(2))
            ax_ref[i, 0, d : d + D] = a0 + mix * a1
            ax_ref[i, 1, d : d + D] = a1 + mix * a0

    inside = jnp.logical_and(has_up, has_down)

    @pl.when(inside)
    def _():
        pl.semaphore_wait(barrier, 3)

    @pl.when(jnp.logical_not(inside))
    def _():
        pl.semaphore_wait(barrier, 2)

    sides_0 = copy(send_s0, side_0, 0, 2, {"group": 1 - group})
    sides_0.start()
    downs = majors([outer(i, 2) for i in range(cols)])
    ups = minors(ups)
    send_v0[...] = normalised([upright(downs, ups, 0)])[0].astype(BF16)
    to_up = copy(send_v0, down_0, 0, 0, {"tile": tile - 1})
    to_down = copy(send_v0, up_0, 0, 1, {"tile": tile + 1})

    @pl.when(has_up)
    def _():
        to_up.start()

    @pl.when(has_down)
    def _():
        to_down.start()

    for s in range(2):
        cross_layout(s)
    for j in range(cols - 1):
        for s in range(2):
            relayout(j, s)

    lefts = [left_first] + majors([outer(i, 1) for i in range(1, cols)])
    rights = minors([outer(i, 3) for i in range(cols - 1)]) + [right_last]

    def inner_view(lefts, rights, kind):
        return placed(
            [(i, rights[i - 1][kind]) for i in range(1, cols)]
            + [(cols + i, lefts[i + 1][kind]) for i in range(cols - 1)]
        )

    n_sides = normalised([inner_view(lefts, rights, 0)])

    def above_0():
        above_arrives(to_up, to_down, up_0, edge_rows)

    def below_0():
        below_arrives(to_down, to_up, down_0, edge_rows)

    side_weights = []

    def paired(j, kron, left, right, at):
        for s in range(2):
            y = dot(left[j, s], kron_ref[kron]).astype(BF16)
            gram_ref[at, s] = dot_nt(y, x2_ref[j, s]) if right is x2t_ref else dot(y, right[j, s])

    v_sides = rounded(jnp.where(from_left | from_right, edge_sides, n_sides[0]))
    for j in range(cols - 1):
        i = order[j]
        w_left, w_right = by_major(v_sides, i), by_minor(v_sides, cols + i)
        side_weights.append((w_left, w_right))
        build_kron(kron_ref, 2 * j, w_left, w_right)
        paired(j, 2 * j, x2_ref, x2t_ref, 2 * j)
    other_major, other_minor = by_major(v_sides, other_slot), by_minor(v_sides, other_slot)

    final = 2 * (cols - 1)

    def crossing_gram(first, second, path):
        build_kron(kron_ref, final, first, second)
        for s in range(2):
            y = dot(xq_ref[path, s], kron_ref[final]).astype(BF16)
            gram_ref[final, s] = dot_nt(y, xq_ref[path, s])

    def all_sides():
        return rounded(joined_sides(side_0, n_sides, [edge_sides])[0])

    def up_legs(weight, j):
        return kinds_of([reduce_major(gram_ref[2 * j, s], weight) for s in range(2)])

    def down_legs(weight, j):
        return kinds_of([reduce_minor(gram_ref[2 * j, s], weight) for s in range(2)])

    def ship(buffer, values):
        for k in range(2):
            buffer[k * D : (k + 1) * D] = values[k].astype(BF16)

    def ordered(above, below, kind):
        return placed(
            [(order[j], above[j][kind]) for j in range(cols)]
            + [(cols + order[j], below[j][kind]) for j in range(cols)]
        )

    nothing = [[jnp.zeros((D, LANES), F32)] * 2] * cols
    up_far = copy(send_f1, down_1, 1, 0, {"tile": tile - 1})
    up_near = copy(send_v1, down_1, 1, 0, {"tile": tile - 1})
    down_far = copy(send_f1, up_1, 1, 1, {"tile": tile + 1})
    down_near = copy(send_v1, up_1, 1, 1, {"tile": tile + 1})

    sides_1 = copy(send_s1, side_1, 1, 2, {"group": 1 - group})

    def cross_major(at, weight):
        return kinds_of([reduce_major(gram_ref[at, s], weight) for s in range(2)])

    def cross_minor(at, weight):
        return kinds_of([reduce_minor(gram_ref[at, s], weight) for s in range(2)])

    @pl.when(far_up)
    def _():
        below_0()
        near = down_0[...].astype(F32)
        crossing_gram(by_major(near, cols + crossing), other_minor, 0)
        early = [up_legs(by_major(near, cols + order[j]), j) for j in range(cols - 1)]
        early = minors(early)
        sides_0.wait()
        weight = by_major(all_sides(), cross_slot)
        legs_up = early + minors([cross_major(final, weight)])
        ship(send_f1, normalised([ordered(nothing, legs_up, k) for k in range(2)]))

        @pl.when(has_up)
        def _():
            up_far.start()

        above_0()
        weight = by_minor(up_0[...].astype(F32), crossing)
        (cross,) = majors([cross_minor(final, weight)])
        ship(send_s1, normalised(cross))
        sides_1.start()

    @pl.when(far_down)
    def _():
        above_0()
        near = up_0[...].astype(F32)
        crossing_gram(other_major, by_minor(near, crossing), 1)
        early = [down_legs(by_minor(near, order[j]), j) for j in range(cols - 1)]
        early = majors(early)
        sides_0.wait()
        weight = by_minor(all_sides(), cross_slot)
        legs_down = early + majors([cross_minor(final, weight)])
        ship(send_f1, normalised([ordered(legs_down, nothing, k) for k in range(2)]))

        @pl.when(has_down)
        def _():
            down_far.start()

        below_0()
        weight = by_major(down_0[...].astype(F32), cols + crossing)
        (cross,) = minors([cross_major(final, weight)])
        ship(send_s1, normalised(cross))
        sides_1.start()

    v_rows = rounded(joined_rows(up_0[...].astype(F32), down_0[...].astype(F32))[0])
    weights = []
    for j in range(cols):
        i = order[j]
        weights.append((by_minor(v_rows, i), by_major(v_rows, cols + i)))
    v_sides = all_sides()
    cross_first, cross_second = by_major(v_sides, cross_slot), by_minor(v_sides, cross_slot)

    def horizontal_gram(j):
        build_kron(kron_ref, 2 * j + 1, weights[j][1], weights[j][0])
        paired(j, 2 * j + 1, x2t_ref, x2_ref, 2 * j + 1)

    def horizontal(j):
        w_left, w_right = side_weights[j]
        left = kinds_of([reduce_minor(gram_ref[2 * j + 1, s], w_right) for s in range(2)])
        right = kinds_of([reduce_major(gram_ref[2 * j + 1, s], w_left) for s in range(2)])
        return left, right

    def last_gram(first, second, path):
        build_kron(kron_ref, final + 1, first, second)
        for s in range(2):
            y = dot(xq_ref[path, s], kron_ref[final + 1]).astype(BF16)
            gram_ref[final + 1, s] = dot(y, xq_ref[1 - path, s])

    @pl.when(far_up)
    def _():
        last_gram(cross_first, weights[-1][0], 1)
        for j in range(cols - 1):
            horizontal_gram(j)
        near = [down_legs(weights[j][0], j) for j in range(cols - 1)]
        near = majors(near + [cross_minor(final + 1, other_minor)])
        ship(send_v1, normalised([ordered(near, nothing, k) for k in range(2)]))
        (other,) = minors([cross_major(final + 1, weights[-1][1])])
        for k in range(2):
            other_ref[k] = other[k]

        @pl.when(has_down)
        def _():
            down_near.start()

    @pl.when(far_down)
    def _():
        last_gram(weights[-1][1], cross_second, 0)
        for j in range(cols - 1):
            horizontal_gram(j)
        near = [up_legs(weights[j][1], j) for j in range(cols - 1)]
        near = minors(near + [cross_major(final + 1, other_major)])
        ship(send_v1, normalised([ordered(nothing, near, k) for k in range(2)]))
        (other,) = majors([cross_minor(final + 1, weights[-1][0])])
        for k in range(2):
            other_ref[k] = other[k]

        @pl.when(has_up)
        def _():
            up_near.start()

    half = cols * D
    swapped = jnp.where(
        slot < cols, lane + half, jnp.where(slot < 2 * cols, lane - half, lane)
    )
    o_rows = [
        pick(
            send_f1[k * D : (k + 1) * D].astype(F32) + send_v1[k * D : (k + 1) * D].astype(F32),
            swapped,
        )
        for k in range(2)
    ]
    others = [horizontal(j) for j in range(cols - 1)]
    lefts = majors([o[0] for o in others])
    rights = minors([o[1] for o in others])

    def own_sides(kind):
        return placed(
            [(order[j], lefts[j][kind]) for j in range(cols - 1)]
            + [(cols + order[j], rights[j][kind]) for j in range(cols - 1)]
            + [(other_slot, other_ref[kind])]
        )

    def other_sides(kind):
        entries = []
        for j in range(cols - 1):
            i = order[j]
            entries.append((jnp.where(i == 0, -1, cols + i - 1), lefts[j][kind]))
            entries.append((jnp.where(i == cols - 1, -1, i + 1), rights[j][kind]))
        entries.append((jnp.where(group == 0, cols + crossing - 1, 1), other_ref[kind]))
        return placed(entries)

    is_cross = (slot == cross_slot) | (slot == jnp.where(group == 0, 2 * cols + 1, 2 * cols))
    o_sides = [
        jnp.where(is_cross, send_s1[k * D : (k + 1) * D].astype(F32), value)
        for k, value in enumerate(normalised([own_sides(k) for k in range(2)]))
    ]
    n_sides = normalised([other_sides(k) for k in range(2)])
    state, rotated, trace = bond_open(*[o + n for o, n in zip(o_sides, n_sides)])
    for step in range(EARLY_STEPS):
        state, rotated = bond_step(state, rotated)
    for n, value in enumerate([state] + rotated + [trace]):
        inner_ref[n] = value
    zero = jnp.zeros((D, LANES), F32)
    sides_1.wait()
    n_sides = joined_sides(side_1, n_sides, [edge_sides, zero])
    rows_edges = jnp.concatenate([edge_rows, zero], axis=0)
    above_arrives(up_near, down_near, up_1, rows_edges)
    below_arrives(down_near, up_near, down_1, rows_edges)
    n_rows = joined_rows(up_1[...].astype(F32), down_1[...].astype(F32))
    on_edge = ((slot < cols) & jnp.logical_not(has_up)) | (
        (slot >= cols) & (slot < 2 * cols) & jnp.logical_not(has_down)
    )
    n_rows[0] = jnp.where(on_edge, edge_rows, n_rows[0])
    for k in range(2):
        env_ref[k] = jnp.where(
            slot < 2 * cols, o_rows[k] + n_rows[k], o_sides[k] + n_sides[k]
        )
    mout_ref[0] = n_rows[0]
    mout_ref[1] = n_sides[0]


def gates_kernel(tiles, groups, cols, D, ax_ref, env_ref, inner_ref, in_ref, out_hbm, mout_hbm,
                 kron_ref, out_ref, mout_ref, early_ref, fence_ref, store_sem):
    tile = lax.axis_index("tile")
    group = lax.axis_index("group")
    DD = D * D
    shift = D.bit_length() - 1
    halves = DD // LANES
    mixed = 2 * halves
    rows = DD // mixed
    lane = iota((D, LANES), 1)
    row = iota((D, LANES), 0)
    inner = lane & (D - 1)
    start = lane - inner
    slot = lane >> shift

    unit = jnp.where(inner == row, 1.0, 0.0).astype(F32)
    at_edge = (
        ((slot < cols) & (tile == 0))
        | ((slot >= cols) & (slot < 2 * cols) & (tile == tiles - 1))
        | ((slot == 2 * cols) & (group == 0))
        | ((slot == 2 * cols + 1) & (group == groups - 1))
    )
    fence = pltpu.make_async_copy(env_ref.at[0], fence_ref, store_sem.at[cols + 1])
    fence.start()
    state, rotated, trace = bond_open(env_ref[0], env_ref[1])
    begun, turning = inner_ref[0], [inner_ref[1], inner_ref[2]]
    early_left = NS_STEPS - 2 - EARLY_STEPS
    for step in range(NS_STEPS - 2):
        if step < early_left:
            begun, turning = bond_step(begun, turning)
        elif step == early_left:
            for s, weight in enumerate(bond_close(begun, turning, inner_ref[3])):
                early_ref[s] = weight.astype(BF16).astype(F32)
        state, rotated = bond_step(state, rotated)
        if step == FENCE_STEP:
            fence.wait()
    early = [early_ref[s] for s in range(2)]
    late = [
        jnp.where(at_edge, unit, w).astype(BF16).astype(F32)
        for w in bond_close(state, rotated, trace)
    ]

    unfold_mask = slot == (row & (LANES // D - 1))
    flat_rows = []
    for m in range(4 * cols):
        at = m // 4 + (cols if m % 4 >= 2 else 0)
        tiled = jnp.where(unfold_mask, pick(in_ref[m % 2], inner + at * D), 0.0)
        step = D // halves
        flat_rows.append(
            jnp.concatenate(
                [
                    jnp.sum(tiled[h * step : (h + 1) * step], axis=0, keepdims=True)
                    for h in range(halves)
                ],
                axis=1,
            )
        )
    mout_ref[...] = jnp.concatenate(flat_rows, axis=0).reshape(cols, 4, DD)
    store_msg = pltpu.make_async_copy(mout_ref, mout_hbm, store_sem.at[cols])
    store_msg.start()

    def by_major(value, m):
        return jnp.concatenate(
            [pick(value, m * D + slot + h * (LANES // D)) for h in range(halves)], axis=1
        )

    def by_minor(value, m):
        part = pick(value, m * D + inner)
        return jnp.concatenate([part] * halves, axis=1)

    scatter = unmixing(D, mixed, 1)
    stores = [
        pltpu.make_async_copy(out_ref.at[i], out_hbm.at[i], store_sem.at[i]) for i in range(cols)
    ]

    for i in range(cols):
        for s in range(2):
            left = by_major(late[s], 2 * cols) if i == 0 else by_major(early[s], i)
            right = (
                by_minor(late[s], 2 * cols + 1) if i == cols - 1 else by_minor(early[s], i + 1)
            )
            at = (i * 2 + s) * 2
            down = math.cosh(FIELD) * by_major(late[s], cols + i)
            build_kron(kron_ref, at, down, right)
            build_kron(kron_ref, at + 1, left, by_minor(late[s], i))
    gated = [
        [dot_nt(ax_ref[i, s], kron_ref[(i * 2 + s) * 2]).astype(BF16) for s in range(2)]
        for i in range(cols)
    ]
    gated = [
        [dot(kron_ref[(i * 2 + s) * 2 + 1], gated[i][s]).astype(BF16) for s in range(2)]
        for i in range(cols)
    ]

    def emit(i, gated):
        for b in range(0, mixed, 2):
            block = jnp.concatenate(
                [
                    jnp.concatenate(
                        [
                            gated[g % 2][
                                (b + c) * rows : (b + c + 1) * rows,
                                (g // 2) * LANES : (g // 2 + 1) * LANES,
                            ]
                            for c in range(2)
                        ],
                        axis=1,
                    )
                    for g in range(mixed)
                ],
                axis=0,
            )
            done = dot(scatter, block).astype(BF16)
            for c in range(2):
                for u in range(D):
                    at = u * D * mixed + (b + c) * D
                    out_ref[i, at : at + D, :] = done[
                        u * D : (u + 1) * D, c * LANES : (c + 1) * LANES
                    ]
        stores[i].start()

    for i in range(cols):
        emit(i, gated[i])
    for store in stores + [store_msg]:
        store.wait()


def per_device(tiles, groups, site_tensors, msg_in):
    _, cols, _, size = site_tensors.shape
    DD = msg_in.shape[-1]
    D = math.isqrt(DD)
    chunks = size // LANES
    a = site_tensors.reshape(cols, 2, chunks, LANES).transpose(0, 2, 1, 3)
    a = a.reshape(cols, 2 * chunks, LANES)
    vmem = pl.BlockSpec(memory_space=pltpu.VMEM)
    hbm = pl.BlockSpec(memory_space=pltpu.HBM)
    gated, env, inner, stacked = pl.pallas_call(
        functools.partial(messages_kernel, tiles, groups, cols, D),
        out_shape=(
            jax.ShapeDtypeStruct((cols, 2, DD, DD), BF16),
            jax.ShapeDtypeStruct((2, D, LANES), F32),
            jax.ShapeDtypeStruct((4, D, LANES), F32),
            jax.ShapeDtypeStruct((2, D, LANES), F32),
        ),
        in_specs=[hbm, hbm],
        out_specs=(vmem, vmem, vmem, vmem),
        scratch_shapes=[
            pltpu.VMEM(a.shape, BF16),
            pltpu.VMEM((cols, 4, DD), F32),
            pltpu.VMEM((2, D, LANES), F32),
            pltpu.VMEM((cols, 2, DD, DD), BF16),
            pltpu.VMEM((cols, 2, DD, DD), BF16),
            pltpu.VMEM((2, 2, DD, DD), BF16),
            pltpu.VMEM((cols - 1, 2, DD, DD), BF16),
            pltpu.VMEM((cols - 1, 2, DD, DD), BF16),
            pltpu.VMEM((2 * cols, DD, DD), BF16),
            pltpu.VMEM((2 * cols, 2, DD, DD), F32),
        ]
        + [
            pltpu.VMEM(((1 + turn) * D, LANES), BF16) for _ in range(6) for turn in range(ITERS)
        ]
        + [
            pltpu.SemaphoreType.DMA((ITERS, 3)),
            pltpu.SemaphoreType.DMA((ITERS, 3)),
            pltpu.SemaphoreType.DMA((cols + 1,)),
        ],
        compiler_params=pltpu.CompilerParams(
            collective_id=0, has_side_effects=True, vmem_limit_bytes=24 * 2**20
        ),
    )(
        pltpu.with_memory_space_constraint(a, pltpu.HBM),
        pltpu.with_memory_space_constraint(msg_in[0], pltpu.HBM),
    )
    out, messages = pl.pallas_call(
        functools.partial(gates_kernel, tiles, groups, cols, D),
        out_shape=(
            jax.ShapeDtypeStruct(a.shape, BF16),
            jax.ShapeDtypeStruct((cols, 4, DD), F32),
        ),
        in_specs=[vmem, vmem, vmem, vmem],
        out_specs=(hbm, hbm),
        scratch_shapes=[
            pltpu.VMEM((4 * cols, DD, DD), BF16),
            pltpu.VMEM(a.shape, BF16),
            pltpu.VMEM((cols, 4, DD), F32),
            pltpu.VMEM((2, D, LANES), F32),
            pltpu.VMEM((D, LANES), F32),
            pltpu.SemaphoreType.DMA((cols + 2,)),
        ],
        compiler_params=pltpu.CompilerParams(vmem_limit_bytes=24 * 2**20),
    )(gated, env, inner, stacked)
    out = out.reshape(cols, chunks, 2, LANES).transpose(0, 2, 1, 3)
    return out.reshape(1, cols, 2, size), messages[None]


def solution(mesh):
    spec = P("tile", "group", None, None)
    return jax.shard_map(
        functools.partial(per_device, mesh.shape["tile"], mesh.shape["group"]),
        mesh=mesh, in_specs=(spec, spec), out_specs=(spec, spec), check_vma=False,
    )
```
